256 devices in a mesh: kv: 8 (over y, core), blk: 32 (over x, z).
Axes of the slice: x: 4, y: 4, z: 8, core: 2. Of those that a mesh axis runs over, the one named last changes fastest.
Arguments:
- hidden_in: bfloat16 [4096, 5120], P('blk', 'kv'), may hold values from -6 to 6
- norm_gain: bfloat16 [5120], replicated, may hold values from 0.099609375 to 1.8984375
- w_query: bfloat16 [5120, 5120], P(None, 'kv'), may hold values from -0.078125 to 0.078125
- key_weight: bfloat16 [5120, 1024], P(None, 'kv'), may hold values from -0.078125 to 0.078125
- value_weight: bfloat16 [5120, 1024], P(None, 'kv'), may hold values from -0.3125 to 0.3125
- b_query: bfloat16 [5120], P('kv'), may hold values from -3 to 3
- key_bias: bfloat16 [1024], P('kv'), may hold values from -3 to 3
- value_bias: bfloat16 [1024], P('kv'), may hold values from -4 to 4
- key_cache: bfloat16 [384, 128, 1024], P('blk', None, 'kv'), as said below
- value_cache: bfloat16 [384, 128, 1024], P('blk', None, 'kv'), may hold values from -24 to 24
- cached_len: int32 [4], replicated, may hold values from 1 to 8192, as said below
- block_table: int32 [4, 72], replicated, may hold values from -1 to 383, as said below
Outputs:
- attn_out: bfloat16 [4096, 5120], P('blk', 'kv')
- cache_k_out: bfloat16 [384, 128, 1024], P('blk', None, 'kv')
- cache_v_out: bfloat16 [384, 128, 1024], P('blk', None, 'kv')
The draws below stay inside these ranges and needn't reach their ends.
Inputs may be any that keep to these rules, and one draw needn't show every extreme that they name: `cached_len`: the lengths sum to 24576; the largest is exactly 8192. `block_table`: row r names, in its first ceil((cached_len[r] + 1024) / 128) entries, the blocks holding positions j * 128 to (j + 1) * 128 - 1 of request r in order; its other entries are -1. No block is named twice. `key_cache`: keys as the layer wrote them, already rotated.
All inputs are finite; a program needn't handle non-finite values.
Results may differ from the reference program's by a relative error of at most 0.02.
The reference program's roundings to bfloat16 on the way count: a program that leaves them out, or rounds other values in their place, can miss the bound.
Values may be sent and summed in bfloat16 or wider, within the bound.
A program may use at most 128 MiB of HBM per device.

```python
import math
import jax
import jax.numpy as jnp
from jax import lax

MODEL_WIDTH = 5120
QUERY_HEADS = 40
KEY_VALUE_HEADS = 8
HEAD_SIZE = 128
BLOCK_SLOTS = 128
REQUEST_COUNT = 4
TOKEN_COUNT = 4096
REQUEST_TOKENS = 1024
TOTAL_BLOCKS = 384
CACHED = 24576
MAXLEN = 8192
MAXB = 72


def draw_lengths(key):
    start_offset = jax.random.fold_in(key, 11)
    first, second_half = jax.random.split(start_offset)
    rest = CACHED - MAXLEN
    share = rest // (REQUEST_COUNT - 1)
    spread = min(share // 2, MAXLEN - share - REQUEST_COUNT)
    bumps = jax.random.randint(first, (REQUEST_COUNT - 1,), 0, spread + 1)
    parts = share + bumps - jnp.roll(bumps, -1)
    parts = parts.at[0].add(rest - share * (REQUEST_COUNT - 1))
    lengths = jnp.concatenate([jnp.full((1,), MAXLEN, jnp.int32), parts.astype(jnp.int32)])
    order = jax.random.permutation(second_half, REQUEST_COUNT)
    return lengths[order].astype(jnp.int32)


def draw_cached_len(key, part):
    return draw_lengths(key)


def draw_block_table(key, part):
    lengths = draw_lengths(key)
    need = (lengths + REQUEST_TOKENS + BLOCK_SLOTS - 1) // BLOCK_SLOTS
    offsets = jnp.cumsum(need) - need
    order = jax.random.permutation(jax.random.fold_in(key, 23), TOTAL_BLOCKS).astype(jnp.int32)
    columns = jnp.arange(MAXB, dtype=jnp.int32)
    slot_index = jnp.minimum(offsets[:, None] + columns[None, :], TOTAL_BLOCKS - 1)
    return jnp.where(columns[None, :] < need[:, None], order[slot_index], -1).astype(jnp.int32)


def draw_key_cache(key, part):
    first = jax.random.fold_in(jax.random.fold_in(key, 37), 0)
    target_shape = (TOTAL_BLOCKS, BLOCK_SLOTS, KEY_VALUE_HEADS * HEAD_SIZE)
    values = 1.5 * jax.random.normal(first, target_shape, jnp.float32)
    return values.astype(jnp.bfloat16)


def block_levels(own_key, shape, shards, smallest, top_value):
    loudness, own = 1.0, jax.random.fold_in(own_key, 6)
    for dim, blocks in shards:
        draws = jnp.exp(jax.random.uniform(jax.random.fold_in(own, dim), (blocks,), jnp.float32, smallest / len(shards), top_value / len(shards)))
        loudness = loudness * jnp.repeat(draws, shape[dim] // blocks).reshape([-1 if axis == dim else 1 for axis in range(len(shape))])
    return loudness


def normal_values(rng, dims, width, most, pieces=(), kind=jnp.bfloat16):
    drawn = jax.random.normal(rng, dims, jnp.float32) * width
    if len(pieces) > 0:
        drawn = block_levels(rng, dims, pieces, -0.22, 0.18) * drawn
    return jnp.clip(drawn, min=-most, max=most).astype(kind)


def setup_inputs(seed: int = 0) -> dict:
    streams_of = jax.random.split(jax.random.key(seed), 13)
    hidden_in = normal_values(streams_of[0], (TOKEN_COUNT, MODEL_WIDTH), 1.0, 6.0, ((0, 32), (1, 8)))
    norm_gain = jnp.clip(1.0 + 0.18 * jax.random.normal(streams_of[1], (MODEL_WIDTH,), jnp.float32), 0.099609375, 1.8984375).astype(jnp.bfloat16)
    w_query = normal_values(streams_of[2], (MODEL_WIDTH, QUERY_HEADS * HEAD_SIZE), MODEL_WIDTH ** -0.5, 0.078125, ((1, 8),))
    key_weight = normal_values(streams_of[3], (MODEL_WIDTH, KEY_VALUE_HEADS * HEAD_SIZE), MODEL_WIDTH ** -0.5, 0.078125, ((1, 8),))
    value_weight = normal_values(streams_of[4], (MODEL_WIDTH, KEY_VALUE_HEADS * HEAD_SIZE), (MODEL_WIDTH // 16) ** -0.5, 0.3125, ((1, 8),))
    b_query = normal_values(streams_of[5], (QUERY_HEADS * HEAD_SIZE,), 0.5, 3.0, ((0, 8),))
    key_bias = normal_values(streams_of[6], (KEY_VALUE_HEADS * HEAD_SIZE,), 0.5, 3.0, ((0, 8),))
    value_bias = normal_values(streams_of[7], (KEY_VALUE_HEADS * HEAD_SIZE,), 1.0, 4.0, ((0, 8),))
    key_cache = draw_key_cache(jax.random.fold_in(streams_of[12], 71), 0)
    value_cache = normal_values(streams_of[9], (TOTAL_BLOCKS, BLOCK_SLOTS, KEY_VALUE_HEADS * HEAD_SIZE), 4.0, 24.0, ((0, 32), (2, 8)))
    cached_len = draw_cached_len(jax.random.fold_in(streams_of[12], 71), 0)
    block_table = draw_block_table(jax.random.fold_in(streams_of[12], 71), 0)
    return {"hidden_in": hidden_in, "norm_gain": norm_gain, "w_query": w_query, "key_weight": key_weight, "value_weight": value_weight, "b_query": b_query, "key_bias": key_bias, "value_bias": value_bias, "key_cache": key_cache, "value_cache": value_cache, "cached_len": cached_len, "block_table": block_table}


EPS = 1e-06
THETA = 1000000.0

def apply_rotary(values, token_positions, head_dim):
    half = head_dim // 2
    rates = THETA ** (-(jnp.arange(half, dtype=jnp.float32) * 2.0) / head_dim)
    angle = token_positions.astype(jnp.float32)[:, None] * rates[None, :]
    cosine = jnp.cos(angle)[:, None, :]
    sine = jnp.sin(angle)[:, None, :]
    first = values[..., :half]
    second_half = values[..., half:]
    return jnp.concatenate([first * cosine - second_half * sine, second_half * cosine + first * sine], axis=-1)

def reference(hidden_in, norm_gain, w_query, key_weight, value_weight, b_query, key_bias, value_bias, key_cache, value_cache, cached_len, block_table):
    tok_ids = jnp.arange(TOKEN_COUNT, dtype=jnp.int32)
    request = (tok_ids // REQUEST_TOKENS).astype(jnp.int32)
    token_positions = (cached_len[request] + tok_ids % REQUEST_TOKENS).astype(jnp.int32)
    wide_in = hidden_in.astype(jnp.float32)
    scale = lax.rsqrt(lax.optimization_barrier(jnp.mean(wide_in * wide_in, axis=1, keepdims=True)) + EPS)
    normed = (wide_in * scale * norm_gain.astype(jnp.float32)[None, :]).astype(jnp.bfloat16)
    q_lin = jnp.dot(normed, w_query, preferred_element_type=jnp.float32) + b_query.astype(jnp.float32)[None, :]
    key_linear = jnp.dot(normed, key_weight, preferred_element_type=jnp.float32) + key_bias.astype(jnp.float32)[None, :]
    value_linear = jnp.dot(normed, value_weight, preferred_element_type=jnp.float32) + value_bias.astype(jnp.float32)[None, :]
    fresh_queries = apply_rotary(q_lin.reshape(TOKEN_COUNT, QUERY_HEADS, HEAD_SIZE), token_positions, HEAD_SIZE).astype(jnp.bfloat16)
    fresh_keys = apply_rotary(key_linear.reshape(TOKEN_COUNT, KEY_VALUE_HEADS, HEAD_SIZE), token_positions, HEAD_SIZE).astype(jnp.bfloat16)
    fresh_values = value_linear.astype(jnp.bfloat16).reshape(TOKEN_COUNT, KEY_VALUE_HEADS, HEAD_SIZE)
    blocks = block_table[request, token_positions // BLOCK_SLOTS].astype(jnp.int32)
    slot_ids = (blocks * BLOCK_SLOTS + token_positions % BLOCK_SLOTS).astype(jnp.int32)
    flat_keys = key_cache.reshape(TOTAL_BLOCKS * BLOCK_SLOTS, KEY_VALUE_HEADS, HEAD_SIZE).at[slot_ids].set(fresh_keys)
    flat_values = value_cache.reshape(TOTAL_BLOCKS * BLOCK_SLOTS, KEY_VALUE_HEADS, HEAD_SIZE).at[slot_ids].set(fresh_values)
    group_size = QUERY_HEADS // KEY_VALUE_HEADS
    grouped_queries = fresh_queries.reshape(TOKEN_COUNT, KEY_VALUE_HEADS, group_size, HEAD_SIZE)
    key_pos = jnp.arange(MAXB * BLOCK_SLOTS, dtype=jnp.int32)
    table_rows = jnp.maximum(block_table, 0).astype(jnp.int32)
    offsets = jnp.arange(BLOCK_SLOTS, dtype=jnp.int32)

    def single_head(slot_index):
        request_index = slot_index // KEY_VALUE_HEADS
        head_index = slot_index % KEY_VALUE_HEADS
        rows = table_rows[request_index]
        key_slots = (rows[:, None] * BLOCK_SLOTS + offsets[None, :]).reshape(-1).astype(jnp.int32)
        keys = flat_keys[key_slots, head_index].astype(jnp.float32)
        vals = flat_values[key_slots, head_index].astype(jnp.float32)
        start = (request_index * REQUEST_TOKENS).astype(jnp.int32)
        queries = lax.dynamic_slice_in_dim(grouped_queries, start, REQUEST_TOKENS, 0)[:, head_index].astype(jnp.float32)
        query_pos = lax.dynamic_slice_in_dim(token_positions, start, REQUEST_TOKENS, 0)
        score = jnp.einsum('cfd,kd->cfk', queries, keys) / math.sqrt(HEAD_SIZE)
        allowed = key_pos[None, None, :] <= query_pos[:, None, None]
        score = jnp.where(allowed, score, -jnp.inf)
        top = lax.optimization_barrier(jnp.max(score, axis=2, keepdims=True))
        weights = jnp.where(allowed, jnp.exp(score - top), 0.0)
        total = lax.optimization_barrier(jnp.sum(weights, axis=2, keepdims=True))
        rounded = lax.optimization_barrier(weights.astype(jnp.bfloat16)).astype(jnp.float32)
        mixed = jnp.einsum('cfk,kd->cfd', rounded, vals) / total
        return mixed.astype(jnp.bfloat16)
    output_rows = lax.map(single_head, jnp.arange(REQUEST_COUNT * KEY_VALUE_HEADS, dtype=jnp.int32))
    attention_fn = output_rows.reshape(REQUEST_COUNT, KEY_VALUE_HEADS, REQUEST_TOKENS, group_size, HEAD_SIZE).transpose(0, 2, 1, 3, 4).reshape(TOKEN_COUNT, QUERY_HEADS * HEAD_SIZE)
    return (attention_fn, flat_keys.reshape(key_cache.shape), flat_values.reshape(value_cache.shape))
```

```python
import functools
import math

import jax
import jax.numpy as jnp
from jax import lax
from jax.experimental import pallas as pl
from jax.experimental.pallas import tpu as pltpu
from jax.sharding import PartitionSpec as P

HEAD_SIZE = 128


EPS = 1e-06
THETA = 1000000.0
NEG_FILL = -1e30


def apply_rotary(values, token_positions, head_dim):
    half = head_dim // 2
    rates = THETA ** (-(jnp.arange(half, dtype=jnp.float32) * 2.0) / head_dim)
    angle = token_positions.astype(jnp.float32)[:, None] * rates[None, :]
    cosine = jnp.cos(angle)[:, None, :]
    sine = jnp.sin(angle)[:, None, :]
    first = values[..., :half]
    second_half = values[..., half:]
    return jnp.concatenate(
        [first * cosine - second_half * sine, second_half * cosine + first * sine], axis=-1
    )


def lookup(table_values, slot_index):
    matches = slot_index[:, None] == jnp.arange(table_values.shape[0], dtype=jnp.int32)[None, :]
    return jnp.sum(jnp.where(matches, table_values[None, :], 0), axis=1)


def block_owner(block_table, block_id):
    matched = block_table == block_id
    row_ids = jnp.arange(block_table.shape[0], dtype=jnp.int32)[:, None]
    col_ids = jnp.arange(block_table.shape[1], dtype=jnp.int32)[None, :]
    used = jnp.any(matched)
    owner = jnp.sum(jnp.where(matched, row_ids, 0))
    column = jnp.sum(jnp.where(matched, col_ids, 0))
    return (used, owner, column)


def merge_new_rows(key_cache, value_cache, kv_all, used, owner, column, cached_len, span):
    nb_dev, block_size, kv_width = key_cache.shape
    padded = jnp.pad(kv_all, ((block_size, block_size), (0, 0)))
    start = block_size + owner * span + column * block_size - cached_len[owner]
    rows = jax.vmap(lambda s: lax.dynamic_slice_in_dim(padded, s, block_size, 0))(start)
    key_pos = column[:, None] * block_size + jnp.arange(block_size, dtype=jnp.int32)[None, :]
    first_new = cached_len[owner][:, None]
    fresh = (used[:, None] == 1) & (key_pos >= first_new) & (key_pos < first_new + span)
    new_k = jnp.where(fresh[..., None], rows[..., :kv_width], key_cache)
    new_v = jnp.where(fresh[..., None], rows[..., kv_width:], value_cache)
    return new_k, new_v


def attention_kernel(
    used_ref, owner_ref, column_ref, clen_ref, q_ref, k_ref, v_ref, o_ref, m_sc, l_sc, acc_sc,
    *, q_heads, head_dim
):
    r = pl.program_id(0)
    i = pl.program_id(1)
    rows = q_ref.shape[0]
    block_size = k_ref.shape[1]

    @pl.when(i == 0)
    def _init():
        m_sc[...] = jnp.full(m_sc.shape, NEG_FILL, jnp.float32)
        l_sc[...] = jnp.zeros(l_sc.shape, jnp.float32)
        acc_sc[...] = jnp.zeros(acc_sc.shape, jnp.float32)

    @pl.when((used_ref[i] == 1) & (owner_ref[i] == r))
    def _work():
        keys = k_ref[0]
        values = v_ref[0]
        query_pos = clen_ref[r] + lax.broadcasted_iota(jnp.int32, (rows, block_size), 0)
        key_pos = column_ref[i] * block_size + lax.broadcasted_iota(
            jnp.int32, (rows, block_size), 1
        )
        allowed = key_pos <= query_pos
        for g in range(q_heads):
            queries = q_ref[:, g * head_dim : (g + 1) * head_dim]
            score = lax.dot_general(
                queries, keys, (((1,), (1,)), ((), ())), preferred_element_type=jnp.float32
            ) / math.sqrt(head_dim)
            score = jnp.where(allowed, score, NEG_FILL)
            top = m_sc[g]
            new_top = jnp.maximum(top, jnp.max(score, axis=1, keepdims=True))
            weights = jnp.where(allowed, jnp.exp(score - new_top), 0.0)
            factor = jnp.exp(top - new_top)
            l_sc[g] = l_sc[g] * factor + jnp.sum(weights, axis=1, keepdims=True)
            acc_sc[g] = acc_sc[g] * factor + jnp.dot(
                weights.astype(jnp.bfloat16), values, preferred_element_type=jnp.float32
            )
            m_sc[g] = new_top

    @pl.when(i == pl.num_programs(1) - 1)
    def _finish():
        lane = lax.broadcasted_iota(jnp.int32, (rows, head_dim), 1)
        stats = jnp.zeros((rows, head_dim), jnp.float32)
        for g in range(q_heads):
            top = m_sc[g]
            valid = top > NEG_FILL / 2
            ref = jnp.where(valid, top.astype(jnp.bfloat16).astype(jnp.float32), NEG_FILL)
            factor = jnp.where(valid, jnp.exp(top - ref), 0.0)
            o_ref[:, g * head_dim : (g + 1) * head_dim] = (acc_sc[g] * factor).astype(o_ref.dtype)
            stats = jnp.where(lane == g, l_sc[g] * factor, stats)
            stats = jnp.where(lane == q_heads + g, ref, stats)
        o_ref[:, q_heads * head_dim :] = stats.astype(o_ref.dtype)


def local_attention(packed_all, new_k, new_v, used, owner, column, cached_len, span, q_heads, head_dim):
    tokens = packed_all.shape[0]
    nb_dev, block_size, kv_width = new_k.shape
    requests = tokens // span
    out_width = (q_heads + 1) * head_dim
    grid_spec = pltpu.PrefetchScalarGridSpec(
        num_scalar_prefetch=4,
        grid=(requests, nb_dev),
        in_specs=[
            pl.BlockSpec((span, q_heads * head_dim), lambda r, i, *_: (r, 0)),
            pl.BlockSpec((1, block_size, kv_width), lambda r, i, *_: (i, 0, 0)),
            pl.BlockSpec((1, block_size, kv_width), lambda r, i, *_: (i, 0, 0)),
        ],
        out_specs=pl.BlockSpec((span, out_width), lambda r, i, *_: (r, 0)),
        scratch_shapes=[
            pltpu.VMEM((q_heads, span, head_dim), jnp.float32),
            pltpu.VMEM((q_heads, span, head_dim), jnp.float32),
            pltpu.VMEM((q_heads, span, head_dim), jnp.float32),
        ],
    )
    flops = 4 * nb_dev * span * q_heads * block_size * head_dim
    return pl.pallas_call(
        functools.partial(attention_kernel, q_heads=q_heads, head_dim=head_dim),
        grid_spec=grid_spec,
        out_shape=jax.ShapeDtypeStruct((tokens, out_width), jnp.bfloat16),
        compiler_params=pltpu.CompilerParams(
            dimension_semantics=("arbitrary", "arbitrary"), vmem_limit_bytes=48 * 1024 * 1024
        ),
        cost_estimate=pl.CostEstimate(
            flops=flops,
            transcendentals=nb_dev * span * q_heads * block_size,
            bytes_accessed=tokens * (q_heads * head_dim + out_width) * 2,
        ),
    )(used, owner, column, cached_len, packed_all, new_k, new_v)


def on_device(
    hidden_in,
    norm_gain,
    w_query,
    key_weight,
    value_weight,
    b_query,
    key_bias,
    value_bias,
    key_cache,
    value_cache,
    cached_len,
    block_table,
):
    tok_dev = hidden_in.shape[0]
    n_blk = lax.axis_size("blk")
    device = lax.axis_index("blk")
    requests = cached_len.shape[0]
    tokens = tok_dev * n_blk
    span = tokens // requests
    nb_dev, block_size, kv_width = key_cache.shape
    head_dim = HEAD_SIZE
    kv_heads = kv_width // head_dim
    q_heads = w_query.shape[1] // head_dim
    group_size = q_heads // kv_heads
    gain = norm_gain.astype(jnp.float32)
    whole = lax.all_gather(hidden_in, "kv", axis=1, tiled=True)
    wide_in = whole.astype(jnp.float32)
    scale = lax.rsqrt(jnp.mean(wide_in * wide_in, axis=1, keepdims=True) + EPS)
    normed = (wide_in * scale * gain[None, :]).astype(jnp.bfloat16)
    q_lin = jnp.dot(normed, w_query, preferred_element_type=jnp.float32)
    key_linear = jnp.dot(normed, key_weight, preferred_element_type=jnp.float32)
    value_linear = jnp.dot(normed, value_weight, preferred_element_type=jnp.float32)
    my_tokens = device * tok_dev + jnp.arange(tok_dev, dtype=jnp.int32)
    my_pos = lookup(cached_len, my_tokens // span) + my_tokens % span
    fresh_queries = apply_rotary(
        (q_lin + b_query.astype(jnp.float32)[None, :]).reshape(tok_dev, q_heads, head_dim),
        my_pos,
        head_dim,
    )
    fresh_queries = fresh_queries.astype(jnp.bfloat16).reshape(tok_dev, q_heads * head_dim)
    fresh_keys = apply_rotary(
        (key_linear + key_bias.astype(jnp.float32)[None, :]).reshape(tok_dev, kv_heads, head_dim),
        my_pos,
        head_dim,
    )
    fresh_keys = fresh_keys.astype(jnp.bfloat16).reshape(tok_dev, kv_width)
    fresh_values = (value_linear + value_bias.astype(jnp.float32)[None, :]).astype(jnp.bfloat16)
    q_width = q_heads * head_dim
    packed = jnp.concatenate([fresh_queries, fresh_keys, fresh_values], axis=1)
    packed_all = lax.all_gather(packed, "blk", axis=0, tiled=True)
    first_block = device * nb_dev
    owner_info = [block_owner(block_table, first_block + b) for b in range(nb_dev)]
    used = jnp.stack([o[0] for o in owner_info]).astype(jnp.int32)
    owner = jnp.stack([o[1] for o in owner_info]).astype(jnp.int32)
    column = jnp.stack([o[2] for o in owner_info]).astype(jnp.int32)
    new_k, new_v = merge_new_rows(
        key_cache, value_cache, packed_all[:, q_width:], used, owner, column, cached_len, span
    )
    parts = local_attention(
        packed_all, new_k, new_v, used, owner, column, cached_len, span, q_heads, head_dim
    )
    got = lax.all_to_all(parts, "blk", 0, 0, tiled=True).reshape(n_blk, tok_dev, q_width + 128)
    got = got.astype(jnp.float32)
    got_w = got[..., :q_width].reshape(n_blk, tok_dev, q_heads, head_dim)
    got_l = got[..., q_width : q_width + group_size]
    got_m = got[..., q_width + group_size : q_width + 2 * group_size]
    best = jnp.max(got_m, axis=0)
    scale_d = jnp.exp(got_m - best[None])
    mine_total = jnp.sum(got_l * scale_d, axis=0)
    mine_weighted = jnp.sum(got_w * scale_d[..., None], axis=0)
    attn_out = (
        (mine_weighted / mine_total[..., None])
        .astype(jnp.bfloat16)
        .reshape(tok_dev, q_heads * head_dim)
    )
    return (attn_out, new_k, new_v)


def solution(mesh):
    in_specs = (
        P("blk", "kv"),
        P(),
        P(None, "kv"),
        P(None, "kv"),
        P(None, "kv"),
        P("kv"),
        P("kv"),
        P("kv"),
        P("blk", None, "kv"),
        P("blk", None, "kv"),
        P(),
        P(),
    )
    out_specs = (P("blk", "kv"), P("blk", None, "kv"), P("blk", None, "kv"))
    return jax.shard_map(
        on_device, mesh=mesh, in_specs=in_specs, out_specs=out_specs, check_vma=False
    )
```

```python
import functools
import math

import jax
import jax.numpy as jnp
from jax import lax
from jax.experimental import pallas as pl
from jax.experimental.pallas import tpu as pltpu
from jax.sharding import PartitionSpec as P

HEAD_SIZE = 128


EPS = 1e-06
THETA = 1000000.0
NEG_FILL = -1e30


def apply_rotary(values, token_positions, head_dim):
    half = head_dim // 2
    rates = THETA ** (-(jnp.arange(half, dtype=jnp.float32) * 2.0) / head_dim)
    angle = token_positions.astype(jnp.float32)[:, None] * rates[None, :]
    cosine = jnp.cos(angle)[:, None, :]
    sine = jnp.sin(angle)[:, None, :]
    first = values[..., :half]
    second_half = values[..., half:]
    return jnp.concatenate(
        [first * cosine - second_half * sine, second_half * cosine + first * sine], axis=-1
    )


def lookup(table_values, slot_index):
    matches = slot_index[:, None] == jnp.arange(table_values.shape[0], dtype=jnp.int32)[None, :]
    return jnp.sum(jnp.where(matches, table_values[None, :], 0), axis=1)


def block_owners(block_table, block_ids):
    matched = block_table[None, :, :] == block_ids[:, None, None]
    row_ids = jnp.arange(block_table.shape[0], dtype=jnp.int32)[None, :, None]
    col_ids = jnp.arange(block_table.shape[1], dtype=jnp.int32)[None, None, :]
    used = jnp.any(matched, axis=(1, 2)).astype(jnp.int32)
    owner = jnp.sum(jnp.where(matched, row_ids, 0), axis=(1, 2)).astype(jnp.int32)
    column = jnp.sum(jnp.where(matched, col_ids, 0), axis=(1, 2)).astype(jnp.int32)
    return used, owner, column


def attention_kernel(
    used_ref, owner_ref, column_ref, clen_ref, start_ref, q_ref, fresh_ref, kc_ref, vc_ref,
    o_ref, nk_ref, nv_ref, m_sc, l_sc, acc_sc, *, q_heads, head_dim
):
    r = pl.program_id(0)
    i = pl.program_id(1)
    rows = q_ref.shape[0]
    block_size, kv_width = kc_ref.shape[1], kc_ref.shape[2]

    start = start_ref[i]
    base = pl.multiple_of((start // 8) * 8, 8)
    window = fresh_ref[pl.ds(base, block_size + 8), :].astype(jnp.bfloat16)
    pick = lax.broadcasted_iota(jnp.int32, (block_size, block_size + 8), 1) == (
        lax.broadcasted_iota(jnp.int32, (block_size, block_size + 8), 0) + (start - base)
    )
    window = jnp.dot(pick.astype(jnp.bfloat16), window, preferred_element_type=jnp.float32)
    slot_pos = column_ref[i] * block_size + lax.broadcasted_iota(
        jnp.int32, (block_size, kv_width), 0
    )
    first_new = clen_ref[owner_ref[i]]
    fresh = (used_ref[i] == 1) & (slot_pos >= first_new) & (slot_pos < first_new + rows)
    keys = jnp.where(fresh, window[:, :kv_width], kc_ref[0].astype(jnp.float32))
    values = jnp.where(fresh, window[:, kv_width:], vc_ref[0].astype(jnp.float32))
    keys = keys.astype(nk_ref.dtype)
    values = values.astype(nv_ref.dtype)
    nk_ref[0] = keys
    nv_ref[0] = values

    @pl.when(i == 0)
    def _init():
        m_sc[...] = jnp.full(m_sc.shape, NEG_FILL, jnp.float32)
        l_sc[...] = jnp.zeros(l_sc.shape, jnp.float32)
        acc_sc[...] = jnp.zeros(acc_sc.shape, jnp.float32)

    @pl.when((used_ref[i] == 1) & (owner_ref[i] == r))
    def _work():
        query_pos = clen_ref[r] + lax.broadcasted_iota(jnp.int32, (rows, block_size), 0)
        key_pos = column_ref[i] * block_size + lax.broadcasted_iota(
            jnp.int32, (rows, block_size), 1
        )
        allowed = key_pos <= query_pos
        for g in range(q_heads):
            queries = q_ref[:, g * head_dim : (g + 1) * head_dim]
            score = lax.dot_general(
                queries, keys, (((1,), (1,)), ((), ())), preferred_element_type=jnp.float32
            ) / math.sqrt(head_dim)
            score = jnp.where(allowed, score, NEG_FILL)
            top = m_sc[g]
            new_top = jnp.maximum(top, jnp.max(score, axis=1, keepdims=True))
            weights = jnp.where(allowed, jnp.exp(score - new_top), 0.0)
            factor = jnp.exp(top - new_top)
            l_sc[g] = l_sc[g] * factor + jnp.sum(weights, axis=1, keepdims=True)
            acc_sc[g] = acc_sc[g] * factor + jnp.dot(
                weights.astype(jnp.bfloat16), values, preferred_element_type=jnp.float32
            )
            m_sc[g] = new_top

    @pl.when(i == pl.num_programs(1) - 1)
    def _finish():
        lane = lax.broadcasted_iota(jnp.int32, (rows, head_dim), 1)
        stats = jnp.zeros((rows, head_dim), jnp.float32)
        for g in range(q_heads):
            top = m_sc[g]
            valid = top > NEG_FILL / 2
            ref = jnp.where(valid, top.astype(jnp.bfloat16).astype(jnp.float32), NEG_FILL)
            factor = jnp.where(valid, jnp.exp(top - ref), 0.0)
            o_ref[:, g * head_dim : (g + 1) * head_dim] = (acc_sc[g] * factor).astype(o_ref.dtype)
            stats = jnp.where(lane == g, l_sc[g] * factor, stats)
            stats = jnp.where(lane == q_heads + g, ref, stats)
        o_ref[:, q_heads * head_dim :] = stats.astype(o_ref.dtype)


def local_attention(packed_all, key_cache, value_cache, block_table, cached_len, device, q_heads, head_dim):
    tokens = packed_all.shape[0]
    nb_dev, block_size, kv_width = key_cache.shape
    requests = cached_len.shape[0]
    span = tokens // requests
    q_width = q_heads * head_dim
    out_width = q_width + head_dim
    used, owner, column = block_owners(
        block_table, device * nb_dev + jnp.arange(nb_dev, dtype=jnp.int32)
    )
    fresh_rows = jnp.pad(
        packed_all[:, q_width:].astype(jnp.float32), ((block_size, block_size + 8), (0, 0))
    )
    start = block_size + owner * span + column * block_size - cached_len[owner]
    start = jnp.clip(start, 0, fresh_rows.shape[0] - block_size - 8).astype(jnp.int32)
    grid_spec = pltpu.PrefetchScalarGridSpec(
        num_scalar_prefetch=5,
        grid=(requests, nb_dev),
        in_specs=[
            pl.BlockSpec((span, q_width), lambda r, i, *_: (r, 0)),
            pl.BlockSpec(fresh_rows.shape, lambda r, i, *_: (0, 0)),
            pl.BlockSpec((1, block_size, kv_width), lambda r, i, *_: (i, 0, 0)),
            pl.BlockSpec((1, block_size, kv_width), lambda r, i, *_: (i, 0, 0)),
        ],
        out_specs=[
            pl.BlockSpec((span, out_width), lambda r, i, *_: (r, 0)),
            pl.BlockSpec((1, block_size, kv_width), lambda r, i, *_: (i, 0, 0)),
            pl.BlockSpec((1, block_size, kv_width), lambda r, i, *_: (i, 0, 0)),
        ],
        scratch_shapes=[
            pltpu.VMEM((q_heads, span, head_dim), jnp.float32),
            pltpu.VMEM((q_heads, span, head_dim), jnp.float32),
            pltpu.VMEM((q_heads, span, head_dim), jnp.float32),
        ],
    )
    flops = 4 * nb_dev * span * q_heads * block_size * head_dim
    return pl.pallas_call(
        functools.partial(attention_kernel, q_heads=q_heads, head_dim=head_dim),
        grid_spec=grid_spec,
        out_shape=(
            jax.ShapeDtypeStruct((tokens, out_width), jnp.bfloat16),
            jax.ShapeDtypeStruct(key_cache.shape, key_cache.dtype),
            jax.ShapeDtypeStruct(value_cache.shape, value_cache.dtype),
        ),
        compiler_params=pltpu.CompilerParams(
            dimension_semantics=("arbitrary", "arbitrary"), vmem_limit_bytes=48 * 1024 * 1024
        ),
        cost_estimate=pl.CostEstimate(
            flops=flops,
            transcendentals=nb_dev * span * q_heads * block_size,
            bytes_accessed=tokens * (q_width + out_width) * 2,
        ),
    )(used, owner, column, cached_len, start, packed_all, fresh_rows, key_cache, value_cache)


def on_device(
    hidden_in,
    norm_gain,
    w_query,
    key_weight,
    value_weight,
    b_query,
    key_bias,
    value_bias,
    key_cache,
    value_cache,
    cached_len,
    block_table,
):
    tok_dev = hidden_in.shape[0]
    n_blk = lax.axis_size("blk")
    device = lax.axis_index("blk")
    requests = cached_len.shape[0]
    tokens = tok_dev * n_blk
    span = tokens // requests
    nb_dev, block_size, kv_width = key_cache.shape
    head_dim = HEAD_SIZE
    kv_heads = kv_width // head_dim
    q_heads = w_query.shape[1] // head_dim
    group_size = q_heads // kv_heads
    gain = norm_gain.astype(jnp.float32)
    whole = lax.all_gather(hidden_in, "kv", axis=1, tiled=True)
    wide_in = whole.astype(jnp.float32)
    scale = lax.rsqrt(jnp.mean(wide_in * wide_in, axis=1, keepdims=True) + EPS)
    normed = (wide_in * scale * gain[None, :]).astype(jnp.bfloat16)
    q_lin = jnp.dot(normed, w_query, preferred_element_type=jnp.float32)
    key_linear = jnp.dot(normed, key_weight, preferred_element_type=jnp.float32)
    value_linear = jnp.dot(normed, value_weight, preferred_element_type=jnp.float32)
    my_tokens = device * tok_dev + jnp.arange(tok_dev, dtype=jnp.int32)
    my_pos = lookup(cached_len, my_tokens // span) + my_tokens % span
    fresh_queries = apply_rotary(
        (q_lin + b_query.astype(jnp.float32)[None, :]).reshape(tok_dev, q_heads, head_dim),
        my_pos,
        head_dim,
    )
    fresh_queries = fresh_queries.astype(jnp.bfloat16).reshape(tok_dev, q_heads * head_dim)
    fresh_keys = apply_rotary(
        (key_linear + key_bias.astype(jnp.float32)[None, :]).reshape(tok_dev, kv_heads, head_dim),
        my_pos,
        head_dim,
    )
    fresh_keys = fresh_keys.astype(jnp.bfloat16).reshape(tok_dev, kv_width)
    fresh_values = (value_linear + value_bias.astype(jnp.float32)[None, :]).astype(jnp.bfloat16)
    q_width = q_heads * head_dim
    packed = jnp.concatenate([fresh_queries, fresh_keys, fresh_values], axis=1)
    packed_all = lax.all_gather(packed, "blk", axis=0, tiled=True)
    parts, new_k, new_v = local_attention(
        packed_all, key_cache, value_cache, block_table, cached_len, device, q_heads, head_dim
    )
    got = lax.all_to_all(parts, "blk", 0, 0, tiled=True).reshape(n_blk, tok_dev, q_width + 128)
    got = got.astype(jnp.float32)
    got_w = got[..., :q_width].reshape(n_blk, tok_dev, q_heads, head_dim)
    got_l = got[..., q_width : q_width + group_size]
    got_m = got[..., q_width + group_size : q_width + 2 * group_size]
    best = jnp.max(got_m, axis=0)
    scale_d = jnp.exp(got_m - best[None])
    mine_total = jnp.sum(got_l * scale_d, axis=0)
    mine_weighted = jnp.sum(got_w * scale_d[..., None], axis=0)
    attn_out = (
        (mine_weighted / mine_total[..., None])
        .astype(jnp.bfloat16)
        .reshape(tok_dev, q_heads * head_dim)
    )
    return (attn_out, new_k, new_v)


def solution(mesh):
    in_specs = (
        P("blk", "kv"),
        P(),
        P(None, "kv"),
        P(None, "kv"),
        P(None, "kv"),
        P("kv"),
        P("kv"),
        P("kv"),
        P("blk", None, "kv"),
        P("blk", None, "kv"),
        P(),
        P(),
    )
    out_specs = (P("blk", "kv"), P("blk", None, "kv"), P("blk", None, "kv"))
    return jax.shard_map(
        on_device, mesh=mesh, in_specs=in_specs, out_specs=out_specs, check_vma=False
    )
```

```python
import functools
import math

import jax
import jax.numpy as jnp
from jax import lax
from jax.experimental import pallas as pl
from jax.experimental.pallas import tpu as pltpu
from jax.sharding import PartitionSpec as P

HEAD_SIZE = 128


EPS = 1e-06
THETA = 1000000.0
NEG_FILL = -1e30


def apply_rotary(values, token_positions, head_dim):
    half = head_dim // 2
    rates = THETA ** (-(jnp.arange(half, dtype=jnp.float32) * 2.0) / head_dim)
    angle = token_positions.astype(jnp.float32)[:, None] * rates[None, :]
    cosine = jnp.cos(angle)[:, None, :]
    sine = jnp.sin(angle)[:, None, :]
    first = values[..., :half]
    second_half = values[..., half:]
    return jnp.concatenate(
        [first * cosine - second_half * sine, second_half * cosine + first * sine], axis=-1
    )


def lookup(table_values, slot_index):
    matches = slot_index[:, None] == jnp.arange(table_values.shape[0], dtype=jnp.int32)[None, :]
    return jnp.sum(jnp.where(matches, table_values[None, :], 0), axis=1)


def block_owners(block_table, block_ids):
    matched = block_table[None, :, :] == block_ids[:, None, None]
    row_ids = jnp.arange(block_table.shape[0], dtype=jnp.int32)[None, :, None]
    col_ids = jnp.arange(block_table.shape[1], dtype=jnp.int32)[None, None, :]
    used = jnp.any(matched, axis=(1, 2)).astype(jnp.int32)
    owner = jnp.sum(jnp.where(matched, row_ids, 0), axis=(1, 2)).astype(jnp.int32)
    column = jnp.sum(jnp.where(matched, col_ids, 0), axis=(1, 2)).astype(jnp.int32)
    return used, owner, column


def attention_kernel(
    used_ref, owner_ref, column_ref, clen_ref, start_ref, q_ref, fresh_ref, kc_ref, vc_ref,
    o_ref, nk_ref, nv_ref, m_sc, l_sc, acc_sc, *, q_heads, head_dim
):
    r = pl.program_id(0)
    i = pl.program_id(1)
    rows = q_ref.shape[0]
    block_size, kv_width = kc_ref.shape[1], kc_ref.shape[2]

    start = start_ref[i]
    base = pl.multiple_of((start // 8) * 8, 8)
    window = fresh_ref[pl.ds(base, block_size + 8), :].astype(jnp.bfloat16)
    pick = lax.broadcasted_iota(jnp.int32, (block_size, block_size + 8), 1) == (
        lax.broadcasted_iota(jnp.int32, (block_size, block_size + 8), 0) + (start - base)
    )
    window = jnp.dot(pick.astype(jnp.bfloat16), window, preferred_element_type=jnp.float32)
    slot_pos = column_ref[i] * block_size + lax.broadcasted_iota(
        jnp.int32, (block_size, kv_width), 0
    )
    first_new = clen_ref[owner_ref[i]]
    fresh = (used_ref[i] == 1) & (slot_pos >= first_new) & (slot_pos < first_new + rows)
    keys = jnp.where(fresh, window[:, :kv_width], kc_ref[0].astype(jnp.float32))
    values = jnp.where(fresh, window[:, kv_width:], vc_ref[0].astype(jnp.float32))
    keys = keys.astype(nk_ref.dtype)
    values = values.astype(nv_ref.dtype)
    nk_ref[0] = keys
    nv_ref[0] = values

    @pl.when(i == 0)
    def _init():
        m_sc[...] = jnp.full(m_sc.shape, NEG_FILL, jnp.float32)
        l_sc[...] = jnp.zeros(l_sc.shape, jnp.float32)
        acc_sc[...] = jnp.zeros(acc_sc.shape, jnp.float32)

    @pl.when((used_ref[i] == 1) & (owner_ref[i] == r))
    def _work():
        query_pos = clen_ref[r] + lax.broadcasted_iota(jnp.int32, (rows, block_size), 0)
        key_pos = column_ref[i] * block_size + lax.broadcasted_iota(
            jnp.int32, (rows, block_size), 1
        )
        allowed = key_pos <= query_pos
        for g in range(q_heads):
            queries = q_ref[:, g * head_dim : (g + 1) * head_dim]
            score = lax.dot_general(
                queries, keys, (((1,), (1,)), ((), ())), preferred_element_type=jnp.float32
            ) / math.sqrt(head_dim)
            score = jnp.where(allowed, score, NEG_FILL)
            top = m_sc[g]
            new_top = jnp.maximum(top, jnp.max(score, axis=1, keepdims=True))
            weights = jnp.where(allowed, jnp.exp(score - new_top), 0.0)
            factor = jnp.exp(top - new_top)
            l_sc[g] = l_sc[g] * factor + jnp.sum(weights, axis=1, keepdims=True)
            acc_sc[g] = acc_sc[g] * factor + jnp.dot(
                weights.astype(jnp.bfloat16), values, preferred_element_type=jnp.float32
            )
            m_sc[g] = new_top

    @pl.when(i == pl.num_programs(1) - 1)
    def _finish():
        lane = lax.broadcasted_iota(jnp.int32, (rows, head_dim), 1)
        stats = jnp.zeros((rows, head_dim), jnp.float32)
        for g in range(q_heads):
            top = m_sc[g]
            valid = top > NEG_FILL / 2
            ref = jnp.where(valid, top.astype(jnp.bfloat16).astype(jnp.float32), NEG_FILL)
            factor = jnp.where(valid, jnp.exp(top - ref), 0.0)
            o_ref[:, g * head_dim : (g + 1) * head_dim] = (acc_sc[g] * factor).astype(o_ref.dtype)
            stats = jnp.where(lane == g, l_sc[g] * factor, stats)
            stats = jnp.where(lane == q_heads + g, ref, stats)
        o_ref[:, q_heads * head_dim :] = stats.astype(o_ref.dtype)


def local_attention(packed_all, key_cache, value_cache, block_table, cached_len, device, q_heads, head_dim):
    tokens = packed_all.shape[0]
    nb_dev, block_size, kv_width = key_cache.shape
    requests = cached_len.shape[0]
    span = tokens // requests
    q_width = q_heads * head_dim
    out_width = q_width + head_dim
    used, owner, column = block_owners(
        block_table, device * nb_dev + jnp.arange(nb_dev, dtype=jnp.int32)
    )
    fresh_rows = jnp.pad(
        packed_all[:, q_width:].astype(jnp.float32), ((block_size, block_size + 8), (0, 0))
    )
    start = block_size + owner * span + column * block_size - cached_len[owner]
    start = jnp.clip(start, 0, fresh_rows.shape[0] - block_size - 8).astype(jnp.int32)
    grid_spec = pltpu.PrefetchScalarGridSpec(
        num_scalar_prefetch=5,
        grid=(requests, nb_dev),
        in_specs=[
            pl.BlockSpec((span, q_width), lambda r, i, *_: (r, 0)),
            pl.BlockSpec(fresh_rows.shape, lambda r, i, *_: (0, 0)),
            pl.BlockSpec((1, block_size, kv_width), lambda r, i, *_: (i, 0, 0)),
            pl.BlockSpec((1, block_size, kv_width), lambda r, i, *_: (i, 0, 0)),
        ],
        out_specs=[
            pl.BlockSpec((span, out_width), lambda r, i, *_: (r, 0)),
            pl.BlockSpec((1, block_size, kv_width), lambda r, i, *_: (i, 0, 0)),
            pl.BlockSpec((1, block_size, kv_width), lambda r, i, *_: (i, 0, 0)),
        ],
        scratch_shapes=[
            pltpu.VMEM((q_heads, span, head_dim), jnp.float32),
            pltpu.VMEM((q_heads, span, head_dim), jnp.float32),
            pltpu.VMEM((q_heads, span, head_dim), jnp.float32),
        ],
    )
    flops = 4 * nb_dev * span * q_heads * block_size * head_dim
    return pl.pallas_call(
        functools.partial(attention_kernel, q_heads=q_heads, head_dim=head_dim),
        grid_spec=grid_spec,
        out_shape=(
            jax.ShapeDtypeStruct((tokens, out_width), jnp.bfloat16),
            jax.ShapeDtypeStruct(key_cache.shape, key_cache.dtype),
            jax.ShapeDtypeStruct(value_cache.shape, value_cache.dtype),
        ),
        compiler_params=pltpu.CompilerParams(
            dimension_semantics=("arbitrary", "arbitrary"), vmem_limit_bytes=48 * 1024 * 1024
        ),
        cost_estimate=pl.CostEstimate(
            flops=flops,
            transcendentals=nb_dev * span * q_heads * block_size,
            bytes_accessed=tokens * (q_width + out_width) * 2,
        ),
    )(used, owner, column, cached_len, start, packed_all, fresh_rows, key_cache, value_cache)


MESH = pl.DeviceIdType.MESH


def exchange_kernel(src_ref, dst_ref, send_sem, recv_sem, own_sem, *, n, rows, gather):
    me = lax.axis_index("blk")
    kv = lax.axis_index("kv")
    barrier = pltpu.get_barrier_semaphore()
    for k in range(1, n):
        peer = lax.rem(me + k, n)
        pl.semaphore_signal(barrier, inc=1, device_id=(kv, peer), device_id_type=MESH)
    pl.semaphore_wait(barrier, n - 1)

    def chunk(j):
        if gather:
            return src_ref
        return src_ref.at[pl.ds(pl.multiple_of(j * rows, rows), rows)]

    own = pltpu.make_async_copy(chunk(me), dst_ref.at[me], own_sem)
    own.start()
    copies = []
    for k in range(1, n):
        peer = lax.rem(me + k, n)
        copy = pltpu.make_async_remote_copy(
            src_ref=chunk(peer),
            dst_ref=dst_ref.at[me],
            send_sem=send_sem.at[k],
            recv_sem=recv_sem.at[k],
            device_id=(kv, peer),
            device_id_type=MESH,
        )
        copy.start()
        copies.append(copy)
    own.wait()
    for k in range(1, n):
        sender = lax.rem(me + n - k, n)
        incoming = pltpu.make_async_remote_copy(
            src_ref=chunk(me),
            dst_ref=dst_ref.at[sender],
            send_sem=send_sem.at[k],
            recv_sem=recv_sem.at[k],
            device_id=(kv, sender),
            device_id_type=MESH,
        )
        copies[k - 1].wait_send()
        incoming.wait_recv()


def exchange(x, n, gather, collective_id):
    rows = x.shape[0] if gather else x.shape[0] // n
    return pl.pallas_call(
        functools.partial(exchange_kernel, n=n, rows=rows, gather=gather),
        out_shape=jax.ShapeDtypeStruct((n, rows, x.shape[1]), x.dtype),
        in_specs=[pl.BlockSpec(memory_space=pl.ANY)],
        out_specs=pl.BlockSpec(memory_space=pl.ANY),
        scratch_shapes=[
            pltpu.SemaphoreType.DMA((n,)),
            pltpu.SemaphoreType.DMA((n,)),
            pltpu.SemaphoreType.DMA,
        ],
        compiler_params=pltpu.CompilerParams(collective_id=collective_id, has_side_effects=True),
    )(x)


def on_device(
    hidden_in,
    norm_gain,
    w_query,
    key_weight,
    value_weight,
    b_query,
    key_bias,
    value_bias,
    key_cache,
    value_cache,
    cached_len,
    block_table,
):
    tok_dev = hidden_in.shape[0]
    n_blk = lax.axis_size("blk")
    device = lax.axis_index("blk")
    requests = cached_len.shape[0]
    tokens = tok_dev * n_blk
    span = tokens // requests
    nb_dev, block_size, kv_width = key_cache.shape
    head_dim = HEAD_SIZE
    kv_heads = kv_width // head_dim
    q_heads = w_query.shape[1] // head_dim
    group_size = q_heads // kv_heads
    gain = norm_gain.astype(jnp.float32)
    whole = lax.all_gather(hidden_in, "kv", axis=1, tiled=True)
    wide_in = whole.astype(jnp.float32)
    scale = lax.rsqrt(jnp.mean(wide_in * wide_in, axis=1, keepdims=True) + EPS)
    normed = (wide_in * scale * gain[None, :]).astype(jnp.bfloat16)
    q_lin = jnp.dot(normed, w_query, preferred_element_type=jnp.float32)
    key_linear = jnp.dot(normed, key_weight, preferred_element_type=jnp.float32)
    value_linear = jnp.dot(normed, value_weight, preferred_element_type=jnp.float32)
    my_tokens = device * tok_dev + jnp.arange(tok_dev, dtype=jnp.int32)
    my_pos = lookup(cached_len, my_tokens // span) + my_tokens % span
    fresh_queries = apply_rotary(
        (q_lin + b_query.astype(jnp.float32)[None, :]).reshape(tok_dev, q_heads, head_dim),
        my_pos,
        head_dim,
    )
    fresh_queries = fresh_queries.astype(jnp.bfloat16).reshape(tok_dev, q_heads * head_dim)
    fresh_keys = apply_rotary(
        (key_linear + key_bias.astype(jnp.float32)[None, :]).reshape(tok_dev, kv_heads, head_dim),
        my_pos,
        head_dim,
    )
    fresh_keys = fresh_keys.astype(jnp.bfloat16).reshape(tok_dev, kv_width)
    fresh_values = (value_linear + value_bias.astype(jnp.float32)[None, :]).astype(jnp.bfloat16)
    q_width = q_heads * head_dim
    packed = jnp.concatenate([fresh_queries, fresh_keys, fresh_values], axis=1)
    packed_all = lax.all_gather(packed, "blk", axis=0, tiled=True)
    parts, new_k, new_v = local_attention(
        packed_all, key_cache, value_cache, block_table, cached_len, device, q_heads, head_dim
    )
    got = exchange(parts, n_blk, False, 0)
    got = got.astype(jnp.float32)
    got_w = got[..., :q_width].reshape(n_blk, tok_dev, q_heads, head_dim)
    got_l = got[..., q_width : q_width + group_size]
    got_m = got[..., q_width + group_size : q_width + 2 * group_size]
    best = jnp.max(got_m, axis=0)
    scale_d = jnp.exp(got_m - best[None])
    mine_total = jnp.sum(got_l * scale_d, axis=0)
    mine_weighted = jnp.sum(got_w * scale_d[..., None], axis=0)
    attn_out = (
        (mine_weighted / mine_total[..., None])
        .astype(jnp.bfloat16)
        .reshape(tok_dev, q_heads * head_dim)
    )
    return (attn_out, new_k, new_v)


def solution(mesh):
    in_specs = (
        P("blk", "kv"),
        P(),
        P(None, "kv"),
        P(None, "kv"),
        P(None, "kv"),
        P("kv"),
        P("kv"),
        P("kv"),
        P("blk", None, "kv"),
        P("blk", None, "kv"),
        P(),
        P(),
    )
    out_specs = (P("blk", "kv"), P("blk", None, "kv"), P("blk", None, "kv"))
    return jax.shard_map(
        on_device, mesh=mesh, in_specs=in_specs, out_specs=out_specs, check_vma=False
    )
```

```python
import functools
import math

import jax
import jax.numpy as jnp
from jax import lax
from jax.experimental import pallas as pl
from jax.experimental.pallas import tpu as pltpu
from jax.sharding import PartitionSpec as P

HEAD_SIZE = 128


EPS = 1e-06
THETA = 1000000.0
NEG_FILL = -1e30


def apply_rotary(values, token_positions, head_dim):
    half = head_dim // 2
    rates = THETA ** (-(jnp.arange(half, dtype=jnp.float32) * 2.0) / head_dim)
    angle = token_positions.astype(jnp.float32)[:, None] * rates[None, :]
    cosine = jnp.cos(angle)[:, None, :]
    sine = jnp.sin(angle)[:, None, :]
    first = values[..., :half]
    second_half = values[..., half:]
    return jnp.concatenate(
        [first * cosine - second_half * sine, second_half * cosine + first * sine], axis=-1
    )


def lookup(table_values, slot_index):
    matches = slot_index[:, None] == jnp.arange(table_values.shape[0], dtype=jnp.int32)[None, :]
    return jnp.sum(jnp.where(matches, table_values[None, :], 0), axis=1)


def block_owners(block_table, block_ids):
    matched = block_table[None, :, :] == block_ids[:, None, None]
    row_ids = jnp.arange(block_table.shape[0], dtype=jnp.int32)[None, :, None]
    col_ids = jnp.arange(block_table.shape[1], dtype=jnp.int32)[None, None, :]
    used = jnp.any(matched, axis=(1, 2)).astype(jnp.int32)
    owner = jnp.sum(jnp.where(matched, row_ids, 0), axis=(1, 2)).astype(jnp.int32)
    column = jnp.sum(jnp.where(matched, col_ids, 0), axis=(1, 2)).astype(jnp.int32)
    return used, owner, column


def merged_block(i, used_ref, owner_ref, column_ref, clen_ref, start_ref, fresh_ref, kc_ref, vc_ref, span):
    block_size, kv_width = kc_ref.shape[1], kc_ref.shape[2]
    start = start_ref[i]
    base = pl.multiple_of((start // 8) * 8, 8)
    window = fresh_ref[pl.ds(base, block_size + 8), :].astype(jnp.bfloat16)
    pick = lax.broadcasted_iota(jnp.int32, (block_size, block_size + 8), 1) == (
        lax.broadcasted_iota(jnp.int32, (block_size, block_size + 8), 0) + (start - base)
    )
    window = jnp.dot(pick.astype(jnp.bfloat16), window, preferred_element_type=jnp.float32)
    slot_pos = column_ref[i] * block_size + lax.broadcasted_iota(
        jnp.int32, (block_size, kv_width), 0
    )
    first_new = clen_ref[owner_ref[i]]
    fresh = (used_ref[i] == 1) & (slot_pos >= first_new) & (slot_pos < first_new + span)
    keys = jnp.where(fresh, window[:, :kv_width], kc_ref[0].astype(jnp.float32))
    values = jnp.where(fresh, window[:, kv_width:], vc_ref[0].astype(jnp.float32))
    return keys.astype(kc_ref.dtype), values.astype(vc_ref.dtype)


def merge_kernel(used_ref, owner_ref, column_ref, clen_ref, start_ref, fresh_ref, kc_ref, vc_ref, nk_ref, nv_ref, *, span):
    keys, values = merged_block(
        pl.program_id(0), used_ref, owner_ref, column_ref, clen_ref, start_ref, fresh_ref,
        kc_ref, vc_ref, span,
    )
    nk_ref[0] = keys
    nv_ref[0] = values


def attention_kernel(
    used_ref, owner_ref, column_ref, clen_ref, start_ref, req_ref, q_ref, fresh_ref, kc_ref, vc_ref,
    o_ref, m_sc, l_sc, acc_sc, *, q_heads, head_dim
):
    i = pl.program_id(0)
    r = req_ref[0]
    rows = q_ref.shape[0]
    block_size = kc_ref.shape[1]

    @pl.when(i == 0)
    def _init():
        m_sc[...] = jnp.full(m_sc.shape, NEG_FILL, jnp.float32)
        l_sc[...] = jnp.zeros(l_sc.shape, jnp.float32)
        acc_sc[...] = jnp.zeros(acc_sc.shape, jnp.float32)

    @pl.when((used_ref[i] == 1) & (owner_ref[i] == r))
    def _work():
        keys, values = merged_block(
            i, used_ref, owner_ref, column_ref, clen_ref, start_ref, fresh_ref, kc_ref, vc_ref, rows
        )
        query_pos = clen_ref[r] + lax.broadcasted_iota(jnp.int32, (rows, block_size), 0)
        key_pos = column_ref[i] * block_size + lax.broadcasted_iota(
            jnp.int32, (rows, block_size), 1
        )
        allowed = key_pos <= query_pos
        for g in range(q_heads):
            queries = q_ref[:, g * head_dim : (g + 1) * head_dim]
            score = lax.dot_general(
                queries, keys, (((1,), (1,)), ((), ())), preferred_element_type=jnp.float32
            ) / math.sqrt(head_dim)
            score = jnp.where(allowed, score, NEG_FILL)
            top = m_sc[g]
            new_top = jnp.maximum(top, jnp.max(score, axis=1, keepdims=True))
            weights = jnp.where(allowed, jnp.exp(score - new_top), 0.0)
            factor = jnp.exp(top - new_top)
            l_sc[g] = l_sc[g] * factor + jnp.sum(weights, axis=1, keepdims=True)
            acc_sc[g] = acc_sc[g] * factor + jnp.dot(
                weights.astype(jnp.bfloat16), values, preferred_element_type=jnp.float32
            )
            m_sc[g] = new_top

    @pl.when(i == pl.num_programs(0) - 1)
    def _finish():
        lane = lax.broadcasted_iota(jnp.int32, (rows, head_dim), 1)
        stats = jnp.zeros((rows, head_dim), jnp.float32)
        for g in range(q_heads):
            top = m_sc[g]
            valid = top > NEG_FILL / 2
            ref = jnp.where(valid, top.astype(jnp.bfloat16).astype(jnp.float32), NEG_FILL)
            factor = jnp.where(valid, jnp.exp(top - ref), 0.0)
            o_ref[:, g * head_dim : (g + 1) * head_dim] = (acc_sc[g] * factor).astype(o_ref.dtype)
            stats = jnp.where(lane == g, l_sc[g] * factor, stats)
            stats = jnp.where(lane == q_heads + g, ref, stats)
        o_ref[:, q_heads * head_dim :] = stats.astype(o_ref.dtype)


def block_meta(block_table, block_ids, cached_len, span, block_size, fresh_len):
    used, owner, column = block_owners(block_table, block_ids)
    start = block_size + owner * span + column * block_size - cached_len[owner]
    start = jnp.clip(start, 0, fresh_len - block_size - 8).astype(jnp.int32)
    return used, owner, column, cached_len, start


def merge_local(meta, fresh_rows, key_cache, value_cache, span):
    nb_dev, block_size, kv_width = key_cache.shape
    block = pl.BlockSpec((1, block_size, kv_width), lambda i, *_: (i, 0, 0))
    grid_spec = pltpu.PrefetchScalarGridSpec(
        num_scalar_prefetch=5,
        grid=(nb_dev,),
        in_specs=[pl.BlockSpec(fresh_rows.shape, lambda i, *_: (0, 0)), block, block],
        out_specs=[block, block],
    )
    return pl.pallas_call(
        functools.partial(merge_kernel, span=span),
        grid_spec=grid_spec,
        out_shape=(
            jax.ShapeDtypeStruct(key_cache.shape, key_cache.dtype),
            jax.ShapeDtypeStruct(value_cache.shape, value_cache.dtype),
        ),
        compiler_params=pltpu.CompilerParams(vmem_limit_bytes=32 * 1024 * 1024),
    )(*meta, fresh_rows, key_cache, value_cache)


def attend(packed_all, fresh_rows, keys, values, meta, request, span, q_heads, head_dim):
    n_blocks, block_size, kv_width = keys.shape
    q_width = q_heads * head_dim
    out_width = q_width + head_dim
    block = pl.BlockSpec((1, block_size, kv_width), lambda i, *_: (i, 0, 0))
    grid_spec = pltpu.PrefetchScalarGridSpec(
        num_scalar_prefetch=6,
        grid=(n_blocks,),
        in_specs=[
            pl.BlockSpec((span, q_width), lambda i, *s: (s[5][0], 0)),
            pl.BlockSpec(fresh_rows.shape, lambda i, *_: (0, 0)),
            block,
            block,
        ],
        out_specs=pl.BlockSpec((span, out_width), lambda i, *_: (0, 0)),
        scratch_shapes=[
            pltpu.VMEM((q_heads, span, head_dim), jnp.float32),
            pltpu.VMEM((q_heads, span, head_dim), jnp.float32),
            pltpu.VMEM((q_heads, span, head_dim), jnp.float32),
        ],
    )
    flops = n_blocks * span * q_heads * block_size * head_dim
    return pl.pallas_call(
        functools.partial(attention_kernel, q_heads=q_heads, head_dim=head_dim),
        grid_spec=grid_spec,
        out_shape=jax.ShapeDtypeStruct((span, out_width), jnp.bfloat16),
        compiler_params=pltpu.CompilerParams(vmem_limit_bytes=48 * 1024 * 1024),
        cost_estimate=pl.CostEstimate(
            flops=flops,
            transcendentals=n_blocks * span * q_heads * block_size // 4,
            bytes_accessed=span * (q_width + out_width) * 2 + n_blocks * block_size * kv_width * 4,
        ),
    )(*meta, request, packed_all, fresh_rows, keys, values)


MESH = pl.DeviceIdType.MESH


def group_exchange_kernel(*refs, m, stride, gather, n_arr):
    srcs, dsts = refs[:n_arr], refs[n_arr : 2 * n_arr]
    send_sem, recv_sem, own_sem = refs[2 * n_arr :]
    me = lax.axis_index("blk")
    kv = lax.axis_index("kv")
    pos = lax.rem(me // stride, m)
    base = me - pos * stride

    def member(j):
        return base + j * stride

    barrier = pltpu.get_barrier_semaphore()
    for k in range(1, m):
        peer = member(lax.rem(pos + k, m))
        pl.semaphore_signal(barrier, inc=1, device_id=(kv, peer), device_id_type=MESH)
    pl.semaphore_wait(barrier, m - 1)

    def chunk(src, j):
        if gather:
            return src
        rows = src.shape[0] // m
        return src.at[pl.ds(pl.multiple_of(j * rows, rows), rows)]

    owns = []
    for a in range(n_arr):
        own = pltpu.make_async_copy(chunk(srcs[a], pos), dsts[a].at[pos], own_sem.at[a])
        own.start()
        owns.append(own)
    copies = []
    for k in range(1, m):
        peer_pos = lax.rem(pos + k, m)
        for a in range(n_arr):
            copy = pltpu.make_async_remote_copy(
                src_ref=chunk(srcs[a], peer_pos),
                dst_ref=dsts[a].at[pos],
                send_sem=send_sem.at[k * n_arr + a],
                recv_sem=recv_sem.at[k * n_arr + a],
                device_id=(kv, member(peer_pos)),
                device_id_type=MESH,
            )
            copy.start()
            copies.append(copy)
    for own in owns:
        own.wait()
    for k in range(1, m):
        sender_pos = lax.rem(pos + m - k, m)
        for a in range(n_arr):
            incoming = pltpu.make_async_remote_copy(
                src_ref=chunk(srcs[a], pos),
                dst_ref=dsts[a].at[sender_pos],
                send_sem=send_sem.at[k * n_arr + a],
                recv_sem=recv_sem.at[k * n_arr + a],
                device_id=(kv, member(sender_pos)),
                device_id_type=MESH,
            )
            copies[(k - 1) * n_arr + a].wait_send()
            incoming.wait_recv()


def group_exchange(arrays, m, stride, gather, collective_id):
    n_arr = len(arrays)
    shapes = []
    for x in arrays:
        rows = x.shape[0] if gather else x.shape[0] // m
        shapes.append(jax.ShapeDtypeStruct((m, rows) + x.shape[1:], x.dtype))
    return pl.pallas_call(
        functools.partial(group_exchange_kernel, m=m, stride=stride, gather=gather, n_arr=n_arr),
        out_shape=tuple(shapes),
        in_specs=[pl.BlockSpec(memory_space=pl.ANY)] * n_arr,
        out_specs=tuple([pl.BlockSpec(memory_space=pl.ANY)] * n_arr),
        scratch_shapes=[
            pltpu.SemaphoreType.DMA((m * n_arr,)),
            pltpu.SemaphoreType.DMA((m * n_arr,)),
            pltpu.SemaphoreType.DMA((n_arr,)),
        ],
        compiler_params=pltpu.CompilerParams(collective_id=collective_id, has_side_effects=True),
    )(*arrays)


def on_device(
    hidden_in,
    norm_gain,
    w_query,
    key_weight,
    value_weight,
    b_query,
    key_bias,
    value_bias,
    key_cache,
    value_cache,
    cached_len,
    block_table,
):
    tok_dev = hidden_in.shape[0]
    n_blk = lax.axis_size("blk")
    device = lax.axis_index("blk")
    requests = cached_len.shape[0]
    tokens = tok_dev * n_blk
    span = tokens // requests
    nb_dev, block_size, kv_width = key_cache.shape
    head_dim = HEAD_SIZE
    kv_heads = kv_width // head_dim
    q_heads = w_query.shape[1] // head_dim
    group_size = q_heads // kv_heads
    gain = norm_gain.astype(jnp.float32)
    whole = lax.all_gather(hidden_in, "kv", axis=1, tiled=True)
    wide_in = whole.astype(jnp.float32)
    scale = lax.rsqrt(jnp.mean(wide_in * wide_in, axis=1, keepdims=True) + EPS)
    normed = (wide_in * scale * gain[None, :]).astype(jnp.bfloat16)
    q_lin = jnp.dot(normed, w_query, preferred_element_type=jnp.float32)
    key_linear = jnp.dot(normed, key_weight, preferred_element_type=jnp.float32)
    value_linear = jnp.dot(normed, value_weight, preferred_element_type=jnp.float32)
    my_tokens = device * tok_dev + jnp.arange(tok_dev, dtype=jnp.int32)
    my_pos = lookup(cached_len, my_tokens // span) + my_tokens % span
    fresh_queries = apply_rotary(
        (q_lin + b_query.astype(jnp.float32)[None, :]).reshape(tok_dev, q_heads, head_dim),
        my_pos,
        head_dim,
    )
    fresh_queries = fresh_queries.astype(jnp.bfloat16).reshape(tok_dev, q_heads * head_dim)
    fresh_keys = apply_rotary(
        (key_linear + key_bias.astype(jnp.float32)[None, :]).reshape(tok_dev, kv_heads, head_dim),
        my_pos,
        head_dim,
    )
    fresh_keys = fresh_keys.astype(jnp.bfloat16).reshape(tok_dev, kv_width)
    fresh_values = (value_linear + value_bias.astype(jnp.float32)[None, :]).astype(jnp.bfloat16)
    q_width = q_heads * head_dim
    packed = jnp.concatenate([fresh_queries, fresh_keys, fresh_values], axis=1)
    packed_all = lax.all_gather(packed, "blk", axis=0, tiled=True)
    ring = span // tok_dev
    cols = n_blk // ring
    position = device % ring
    col_keys, col_values = group_exchange([key_cache, value_cache], cols, ring, True, 0)
    fresh_rows = jnp.pad(
        packed_all[:, q_width:].astype(jnp.float32), ((block_size, block_size + 8), (0, 0))
    )
    local_ids = device * nb_dev + jnp.arange(nb_dev, dtype=jnp.int32)
    meta = block_meta(block_table, local_ids, cached_len, span, block_size, fresh_rows.shape[0])
    new_k, new_v = merge_local(meta, fresh_rows, key_cache, value_cache, span)
    holders = jnp.arange(cols, dtype=jnp.int32) * ring + position
    col_ids = (holders[:, None] * nb_dev + jnp.arange(nb_dev, dtype=jnp.int32)[None, :]).reshape(-1)
    meta = block_meta(block_table, col_ids, cached_len, span, block_size, fresh_rows.shape[0])
    request = (device // ring).reshape(1).astype(jnp.int32)
    parts = attend(
        packed_all,
        fresh_rows,
        col_keys.reshape(cols * nb_dev, block_size, kv_width),
        col_values.reshape(cols * nb_dev, block_size, kv_width),
        meta,
        request,
        span,
        q_heads,
        head_dim,
    )
    (got,) = group_exchange([parts], ring, 1, False, 1)
    got = got.astype(jnp.float32)
    got_w = got[..., :q_width].reshape(ring, tok_dev, q_heads, head_dim)
    got_l = got[..., q_width : q_width + group_size]
    got_m = got[..., q_width + group_size : q_width + 2 * group_size]
    best = jnp.max(got_m, axis=0)
    scale_d = jnp.exp(got_m - best[None])
    mine_total = jnp.sum(got_l * scale_d, axis=0)
    mine_weighted = jnp.sum(got_w * scale_d[..., None], axis=0)
    attn_out = (
        (mine_weighted / mine_total[..., None])
        .astype(jnp.bfloat16)
        .reshape(tok_dev, q_heads * head_dim)
    )
    return (attn_out, new_k, new_v)


def solution(mesh):
    in_specs = (
        P("blk", "kv"),
        P(),
        P(None, "kv"),
        P(None, "kv"),
        P(None, "kv"),
        P("kv"),
        P("kv"),
        P("kv"),
        P("blk", None, "kv"),
        P("blk", None, "kv"),
        P(),
        P(),
    )
    out_specs = (P("blk", "kv"), P("blk", None, "kv"), P("blk", None, "kv"))
    return jax.shard_map(
        on_device, mesh=mesh, in_specs=in_specs, out_specs=out_specs, check_vma=False
    )
```

```python
import functools
import math

import jax
import jax.numpy as jnp
from jax import lax
from jax.experimental import pallas as pl
from jax.experimental.pallas import tpu as pltpu
from jax.sharding import PartitionSpec as P

HEAD_SIZE = 128


EPS = 1e-06
THETA = 1000000.0
NEG_FILL = -1e30


def apply_rotary(values, token_positions, head_dim):
    half = head_dim // 2
    rates = THETA ** (-(jnp.arange(half, dtype=jnp.float32) * 2.0) / head_dim)
    angle = token_positions.astype(jnp.float32)[:, None] * rates[None, :]
    cosine = jnp.cos(angle)[:, None, :]
    sine = jnp.sin(angle)[:, None, :]
    first = values[..., :half]
    second_half = values[..., half:]
    return jnp.concatenate(
        [first * cosine - second_half * sine, second_half * cosine + first * sine], axis=-1
    )


def lookup(table_values, slot_index):
    matches = slot_index[:, None] == jnp.arange(table_values.shape[0], dtype=jnp.int32)[None, :]
    return jnp.sum(jnp.where(matches, table_values[None, :], 0), axis=1)


def block_owners(block_table, block_ids):
    matched = block_table[None, :, :] == block_ids[:, None, None]
    row_ids = jnp.arange(block_table.shape[0], dtype=jnp.int32)[None, :, None]
    col_ids = jnp.arange(block_table.shape[1], dtype=jnp.int32)[None, None, :]
    used = jnp.any(matched, axis=(1, 2)).astype(jnp.int32)
    owner = jnp.sum(jnp.where(matched, row_ids, 0), axis=(1, 2)).astype(jnp.int32)
    column = jnp.sum(jnp.where(matched, col_ids, 0), axis=(1, 2)).astype(jnp.int32)
    return used, owner, column


def merged_block(i, used_ref, owner_ref, column_ref, clen_ref, start_ref, fresh_ref, kc_ref, vc_ref, span):
    block_size, kv_width = kc_ref.shape[1], kc_ref.shape[2]
    start = start_ref[i]
    base = pl.multiple_of((start // 8) * 8, 8)
    window = fresh_ref[pl.ds(base, block_size + 8), :].astype(jnp.bfloat16)
    pick = lax.broadcasted_iota(jnp.int32, (block_size, block_size + 8), 1) == (
        lax.broadcasted_iota(jnp.int32, (block_size, block_size + 8), 0) + (start - base)
    )
    window = jnp.dot(pick.astype(jnp.bfloat16), window, preferred_element_type=jnp.float32)
    slot_pos = column_ref[i] * block_size + lax.broadcasted_iota(
        jnp.int32, (block_size, kv_width), 0
    )
    first_new = clen_ref[owner_ref[i]]
    fresh = (used_ref[i] == 1) & (slot_pos >= first_new) & (slot_pos < first_new + span)
    keys = jnp.where(fresh, window[:, :kv_width], kc_ref[0].astype(jnp.float32))
    values = jnp.where(fresh, window[:, kv_width:], vc_ref[0].astype(jnp.float32))
    return keys.astype(kc_ref.dtype), values.astype(vc_ref.dtype)


def merge_kernel(used_ref, owner_ref, column_ref, clen_ref, start_ref, fresh_ref, kc_ref, vc_ref, nk_ref, nv_ref, *, span):
    keys, values = merged_block(
        pl.program_id(0), used_ref, owner_ref, column_ref, clen_ref, start_ref, fresh_ref,
        kc_ref, vc_ref, span,
    )
    nk_ref[0] = keys
    nv_ref[0] = values


def attention_kernel(
    used_ref, owner_ref, column_ref, clen_ref, start_ref, req_ref, q_ref, fresh_ref, kc_ref, vc_ref,
    o_ref, m_sc, l_sc, acc_sc, *, q_heads, head_dim
):
    i = pl.program_id(0)
    r = req_ref[0]
    rows = q_ref.shape[0]
    block_size = kc_ref.shape[1]

    @pl.when(i == 0)
    def _init():
        m_sc[...] = jnp.full(m_sc.shape, NEG_FILL, jnp.float32)
        l_sc[...] = jnp.zeros(l_sc.shape, jnp.float32)
        acc_sc[...] = jnp.zeros(acc_sc.shape, jnp.float32)

    @pl.when((used_ref[i] == 1) & (owner_ref[i] == r))
    def _work():
        keys, values = merged_block(
            i, used_ref, owner_ref, column_ref, clen_ref, start_ref, fresh_ref, kc_ref, vc_ref, rows
        )
        query_pos = clen_ref[r] + lax.broadcasted_iota(jnp.int32, (rows, block_size), 0)
        key_pos = column_ref[i] * block_size + lax.broadcasted_iota(
            jnp.int32, (rows, block_size), 1
        )
        allowed = key_pos <= query_pos
        for g in range(q_heads):
            queries = q_ref[:, g * head_dim : (g + 1) * head_dim]
            score = lax.dot_general(
                queries, keys, (((1,), (1,)), ((), ())), preferred_element_type=jnp.float32
            ) / math.sqrt(head_dim)
            score = jnp.where(allowed, score, NEG_FILL)
            top = m_sc[g]
            new_top = jnp.maximum(top, jnp.max(score, axis=1, keepdims=True))
            weights = jnp.where(allowed, jnp.exp(score - new_top), 0.0)
            factor = jnp.exp(top - new_top)
            l_sc[g] = l_sc[g] * factor + jnp.sum(weights, axis=1, keepdims=True)
            acc_sc[g] = acc_sc[g] * factor + jnp.dot(
                weights.astype(jnp.bfloat16), values, preferred_element_type=jnp.float32
            )
            m_sc[g] = new_top

    @pl.when(i == pl.num_programs(0) - 1)
    def _finish():
        lane = lax.broadcasted_iota(jnp.int32, (rows, head_dim), 1)
        stats = jnp.zeros((rows, head_dim), jnp.float32)
        for g in range(q_heads):
            top = m_sc[g]
            valid = top > NEG_FILL / 2
            ref = jnp.where(valid, top.astype(jnp.bfloat16).astype(jnp.float32), NEG_FILL)
            factor = jnp.where(valid, jnp.exp(top - ref), 0.0)
            o_ref[:, g * head_dim : (g + 1) * head_dim] = (acc_sc[g] * factor).astype(o_ref.dtype)
            stats = jnp.where(lane == g, l_sc[g] * factor, stats)
            stats = jnp.where(lane == q_heads + g, ref, stats)
        o_ref[:, q_heads * head_dim :] = stats.astype(o_ref.dtype)


def block_meta(block_table, block_ids, cached_len, span, block_size, fresh_len):
    used, owner, column = block_owners(block_table, block_ids)
    start = block_size + owner * span + column * block_size - cached_len[owner]
    start = jnp.clip(start, 0, fresh_len - block_size - 8).astype(jnp.int32)
    return used, owner, column, cached_len, start


def merge_local(meta, fresh_rows, key_cache, value_cache, span):
    nb_dev, block_size, kv_width = key_cache.shape
    block = pl.BlockSpec((1, block_size, kv_width), lambda i, *_: (i, 0, 0))
    grid_spec = pltpu.PrefetchScalarGridSpec(
        num_scalar_prefetch=5,
        grid=(nb_dev,),
        in_specs=[pl.BlockSpec(fresh_rows.shape, lambda i, *_: (0, 0)), block, block],
        out_specs=[block, block],
    )
    return pl.pallas_call(
        functools.partial(merge_kernel, span=span),
        grid_spec=grid_spec,
        out_shape=(
            jax.ShapeDtypeStruct(key_cache.shape, key_cache.dtype),
            jax.ShapeDtypeStruct(value_cache.shape, value_cache.dtype),
        ),
        compiler_params=pltpu.CompilerParams(vmem_limit_bytes=32 * 1024 * 1024),
    )(*meta, fresh_rows, key_cache, value_cache)


def attend(queries, fresh_rows, keys, values, meta, request, span, q_heads, head_dim):
    n_blocks, block_size, kv_width = keys.shape
    q_width = q_heads * head_dim
    out_width = q_width + head_dim
    block = pl.BlockSpec((1, block_size, kv_width), lambda i, *_: (i, 0, 0))
    grid_spec = pltpu.PrefetchScalarGridSpec(
        num_scalar_prefetch=6,
        grid=(n_blocks,),
        in_specs=[
            pl.BlockSpec((span, q_width), lambda i, *_: (0, 0)),
            pl.BlockSpec(fresh_rows.shape, lambda i, *_: (0, 0)),
            block,
            block,
        ],
        out_specs=pl.BlockSpec((span, out_width), lambda i, *_: (0, 0)),
        scratch_shapes=[
            pltpu.VMEM((q_heads, span, head_dim), jnp.float32),
            pltpu.VMEM((q_heads, span, head_dim), jnp.float32),
            pltpu.VMEM((q_heads, span, head_dim), jnp.float32),
        ],
    )
    flops = n_blocks * span * q_heads * block_size * head_dim
    return pl.pallas_call(
        functools.partial(attention_kernel, q_heads=q_heads, head_dim=head_dim),
        grid_spec=grid_spec,
        out_shape=jax.ShapeDtypeStruct((span, out_width), jnp.bfloat16),
        compiler_params=pltpu.CompilerParams(vmem_limit_bytes=48 * 1024 * 1024),
        cost_estimate=pl.CostEstimate(
            flops=flops,
            transcendentals=n_blocks * span * q_heads * block_size // 4,
            bytes_accessed=span * (q_width + out_width) * 2 + n_blocks * block_size * kv_width * 4,
        ),
    )(*meta, request, queries, fresh_rows, keys, values)


MESH = pl.DeviceIdType.MESH


def group_exchange_kernel(*refs, m, stride, gather, n_arr):
    srcs, dsts = refs[:n_arr], refs[n_arr : 2 * n_arr]
    send_sem, recv_sem, own_sem = refs[2 * n_arr :]
    me = lax.axis_index("blk")
    kv = lax.axis_index("kv")
    pos = lax.rem(me // stride, m)
    base = me - pos * stride

    def member(j):
        return base + j * stride

    barrier = pltpu.get_barrier_semaphore()
    for k in range(1, m):
        peer = member(lax.rem(pos + k, m))
        pl.semaphore_signal(barrier, inc=1, device_id=(kv, peer), device_id_type=MESH)
    pl.semaphore_wait(barrier, m - 1)

    def chunk(src, j):
        if gather:
            return src
        rows = src.shape[0] // m
        return src.at[pl.ds(pl.multiple_of(j * rows, rows), rows)]

    owns = []
    for a in range(n_arr):
        own = pltpu.make_async_copy(chunk(srcs[a], pos), dsts[a].at[pos], own_sem.at[a])
        own.start()
        owns.append(own)
    copies = []
    for k in range(1, m):
        peer_pos = lax.rem(pos + k, m)
        for a in range(n_arr):
            copy = pltpu.make_async_remote_copy(
                src_ref=chunk(srcs[a], peer_pos),
                dst_ref=dsts[a].at[pos],
                send_sem=send_sem.at[k * n_arr + a],
                recv_sem=recv_sem.at[k * n_arr + a],
                device_id=(kv, member(peer_pos)),
                device_id_type=MESH,
            )
            copy.start()
            copies.append(copy)
    for own in owns:
        own.wait()
    for k in range(1, m):
        sender_pos = lax.rem(pos + m - k, m)
        for a in range(n_arr):
            incoming = pltpu.make_async_remote_copy(
                src_ref=chunk(srcs[a], pos),
                dst_ref=dsts[a].at[sender_pos],
                send_sem=send_sem.at[k * n_arr + a],
                recv_sem=recv_sem.at[k * n_arr + a],
                device_id=(kv, member(sender_pos)),
                device_id_type=MESH,
            )
            copies[(k - 1) * n_arr + a].wait_send()
            incoming.wait_recv()


def group_exchange(arrays, m, stride, gather, collective_id):
    n_arr = len(arrays)
    shapes = []
    for x in arrays:
        rows = x.shape[0] if gather else x.shape[0] // m
        shapes.append(jax.ShapeDtypeStruct((m, rows) + x.shape[1:], x.dtype))
    return pl.pallas_call(
        functools.partial(group_exchange_kernel, m=m, stride=stride, gather=gather, n_arr=n_arr),
        out_shape=tuple(shapes),
        in_specs=[pl.BlockSpec(memory_space=pl.ANY)] * n_arr,
        out_specs=tuple([pl.BlockSpec(memory_space=pl.ANY)] * n_arr),
        scratch_shapes=[
            pltpu.SemaphoreType.DMA((m * n_arr,)),
            pltpu.SemaphoreType.DMA((m * n_arr,)),
            pltpu.SemaphoreType.DMA((n_arr,)),
        ],
        compiler_params=pltpu.CompilerParams(collective_id=collective_id, has_side_effects=True),
    )(*arrays)


def on_device(
    hidden_in,
    norm_gain,
    w_query,
    key_weight,
    value_weight,
    b_query,
    key_bias,
    value_bias,
    key_cache,
    value_cache,
    cached_len,
    block_table,
):
    tok_dev = hidden_in.shape[0]
    n_blk = lax.axis_size("blk")
    device = lax.axis_index("blk")
    requests = cached_len.shape[0]
    tokens = tok_dev * n_blk
    span = tokens // requests
    nb_dev, block_size, kv_width = key_cache.shape
    head_dim = HEAD_SIZE
    kv_heads = kv_width // head_dim
    q_heads = w_query.shape[1] // head_dim
    group_size = q_heads // kv_heads
    gain = norm_gain.astype(jnp.float32)
    whole = lax.all_gather(hidden_in, "kv", axis=1, tiled=True)
    wide_in = whole.astype(jnp.float32)
    scale = lax.rsqrt(jnp.mean(wide_in * wide_in, axis=1, keepdims=True) + EPS)
    normed = (wide_in * scale * gain[None, :]).astype(jnp.bfloat16)
    q_lin = jnp.dot(normed, w_query, preferred_element_type=jnp.float32)
    key_linear = jnp.dot(normed, key_weight, preferred_element_type=jnp.float32)
    value_linear = jnp.dot(normed, value_weight, preferred_element_type=jnp.float32)
    my_tokens = device * tok_dev + jnp.arange(tok_dev, dtype=jnp.int32)
    my_pos = lookup(cached_len, my_tokens // span) + my_tokens % span
    fresh_queries = apply_rotary(
        (q_lin + b_query.astype(jnp.float32)[None, :]).reshape(tok_dev, q_heads, head_dim),
        my_pos,
        head_dim,
    )
    fresh_queries = fresh_queries.astype(jnp.bfloat16).reshape(tok_dev, q_heads * head_dim)
    fresh_keys = apply_rotary(
        (key_linear + key_bias.astype(jnp.float32)[None, :]).reshape(tok_dev, kv_heads, head_dim),
        my_pos,
        head_dim,
    )
    fresh_keys = fresh_keys.astype(jnp.bfloat16).reshape(tok_dev, kv_width)
    fresh_values = (value_linear + value_bias.astype(jnp.float32)[None, :]).astype(jnp.bfloat16)
    q_width = q_heads * head_dim
    packed = jnp.concatenate([fresh_keys, fresh_values], axis=1)
    kv_all = lax.all_gather(packed, "blk", axis=0, tiled=True)
    ring = span // tok_dev
    cols = n_blk // ring
    position = device % ring
    col_keys, col_values = group_exchange([key_cache, value_cache], cols, ring, True, 0)
    (ring_queries,) = group_exchange([fresh_queries], ring, 1, True, 2)
    fresh_rows = jnp.pad(kv_all.astype(jnp.float32), ((block_size, block_size + 8), (0, 0)))
    local_ids = device * nb_dev + jnp.arange(nb_dev, dtype=jnp.int32)
    meta = block_meta(block_table, local_ids, cached_len, span, block_size, fresh_rows.shape[0])
    new_k, new_v = merge_local(meta, fresh_rows, key_cache, value_cache, span)
    holders = jnp.arange(cols, dtype=jnp.int32) * ring + position
    col_ids = (holders[:, None] * nb_dev + jnp.arange(nb_dev, dtype=jnp.int32)[None, :]).reshape(-1)
    meta = block_meta(block_table, col_ids, cached_len, span, block_size, fresh_rows.shape[0])
    request = (device // ring).reshape(1).astype(jnp.int32)
    parts = attend(
        ring_queries.reshape(span, q_width),
        fresh_rows,
        col_keys.reshape(cols * nb_dev, block_size, kv_width),
        col_values.reshape(cols * nb_dev, block_size, kv_width),
        meta,
        request,
        span,
        q_heads,
        head_dim,
    )
    (got,) = group_exchange([parts], ring, 1, False, 1)
    got = got.astype(jnp.float32)
    got_w = got[..., :q_width].reshape(ring, tok_dev, q_heads, head_dim)
    got_l = got[..., q_width : q_width + group_size]
    got_m = got[..., q_width + group_size : q_width + 2 * group_size]
    best = jnp.max(got_m, axis=0)
    scale_d = jnp.exp(got_m - best[None])
    mine_total = jnp.sum(got_l * scale_d, axis=0)
    mine_weighted = jnp.sum(got_w * scale_d[..., None], axis=0)
    attn_out = (
        (mine_weighted / mine_total[..., None])
        .astype(jnp.bfloat16)
        .reshape(tok_dev, q_heads * head_dim)
    )
    return (attn_out, new_k, new_v)


def solution(mesh):
    in_specs = (
        P("blk", "kv"),
        P(),
        P(None, "kv"),
        P(None, "kv"),
        P(None, "kv"),
        P("kv"),
        P("kv"),
        P("kv"),
        P("blk", None, "kv"),
        P("blk", None, "kv"),
        P(),
        P(),
    )
    out_specs = (P("blk", "kv"), P("blk", None, "kv"), P("blk", None, "kv"))
    return jax.shard_map(
        on_device, mesh=mesh, in_specs=in_specs, out_specs=out_specs, check_vma=False
    )
```

```python
import functools
import math

import jax
import jax.numpy as jnp
from jax import lax
from jax.experimental import pallas as pl
from jax.experimental.pallas import tpu as pltpu
from jax.sharding import PartitionSpec as P

HEAD_SIZE = 128


EPS = 1e-06
THETA = 1000000.0
NEG_FILL = -1e30


def apply_rotary(values, token_positions, head_dim):
    half = head_dim // 2
    rates = THETA ** (-(jnp.arange(half, dtype=jnp.float32) * 2.0) / head_dim)
    angle = token_positions.astype(jnp.float32)[:, None] * rates[None, :]
    cosine = jnp.cos(angle)[:, None, :]
    sine = jnp.sin(angle)[:, None, :]
    first = values[..., :half]
    second_half = values[..., half:]
    return jnp.concatenate(
        [first * cosine - second_half * sine, second_half * cosine + first * sine], axis=-1
    )


def lookup(table_values, slot_index):
    matches = slot_index[:, None] == jnp.arange(table_values.shape[0], dtype=jnp.int32)[None, :]
    return jnp.sum(jnp.where(matches, table_values[None, :], 0), axis=1)


def block_owners(block_table, block_ids):
    matched = block_table[None, :, :] == block_ids[:, None, None]
    row_ids = jnp.arange(block_table.shape[0], dtype=jnp.int32)[None, :, None]
    col_ids = jnp.arange(block_table.shape[1], dtype=jnp.int32)[None, None, :]
    used = jnp.any(matched, axis=(1, 2)).astype(jnp.int32)
    owner = jnp.sum(jnp.where(matched, row_ids, 0), axis=(1, 2)).astype(jnp.int32)
    column = jnp.sum(jnp.where(matched, col_ids, 0), axis=(1, 2)).astype(jnp.int32)
    return used, owner, column


def merged_block(i, used_ref, owner_ref, column_ref, clen_ref, start_ref, fresh_ref, kc_ref, vc_ref, span):
    block_size, kv_width = kc_ref.shape[1], kc_ref.shape[2]
    start = start_ref[i]
    base = pl.multiple_of((start // 8) * 8, 8)
    window = fresh_ref[pl.ds(base, block_size + 8), :].astype(jnp.bfloat16)
    pick = lax.broadcasted_iota(jnp.int32, (block_size, block_size + 8), 1) == (
        lax.broadcasted_iota(jnp.int32, (block_size, block_size + 8), 0) + (start - base)
    )
    window = jnp.dot(pick.astype(jnp.bfloat16), window, preferred_element_type=jnp.float32)
    slot_pos = column_ref[i] * block_size + lax.broadcasted_iota(
        jnp.int32, (block_size, kv_width), 0
    )
    first_new = clen_ref[owner_ref[i]]
    fresh = (used_ref[i] == 1) & (slot_pos >= first_new) & (slot_pos < first_new + span)
    keys = jnp.where(fresh, window[:, :kv_width], kc_ref[0].astype(jnp.float32))
    values = jnp.where(fresh, window[:, kv_width:], vc_ref[0].astype(jnp.float32))
    return keys.astype(kc_ref.dtype), values.astype(vc_ref.dtype)


def attention_kernel(
    used_ref, owner_ref, column_ref, clen_ref, start_ref, req_ref, q_ref, fresh_ref, kc_ref, vc_ref,
    o_ref, nk_ref, nv_ref, m_sc, l_sc, acc_sc, *, q_heads, head_dim
):
    i = pl.program_id(0)
    r = req_ref[0]
    rows = q_ref.shape[0]
    block_size = kc_ref.shape[1]

    @pl.when(i == 0)
    def _init():
        m_sc[...] = jnp.full(m_sc.shape, NEG_FILL, jnp.float32)
        l_sc[...] = jnp.zeros(l_sc.shape, jnp.float32)
        acc_sc[...] = jnp.zeros(acc_sc.shape, jnp.float32)

    active = (used_ref[i] == 1) & (owner_ref[i] == r)

    @pl.when(jnp.logical_not(active))
    def _keep():
        nk_ref[...] = kc_ref[...]
        nv_ref[...] = vc_ref[...]

    @pl.when(active)
    def _work():
        keys, values = merged_block(
            i, used_ref, owner_ref, column_ref, clen_ref, start_ref, fresh_ref, kc_ref, vc_ref, rows
        )
        nk_ref[0] = keys
        nv_ref[0] = values
        query_pos = clen_ref[r] + lax.broadcasted_iota(jnp.int32, (rows, block_size), 0)
        key_pos = column_ref[i] * block_size + lax.broadcasted_iota(
            jnp.int32, (rows, block_size), 1
        )
        allowed = key_pos <= query_pos
        for g in range(q_heads):
            queries = q_ref[:, g * head_dim : (g + 1) * head_dim]
            score = lax.dot_general(
                queries, keys, (((1,), (1,)), ((), ())), preferred_element_type=jnp.float32
            ) / math.sqrt(head_dim)
            score = jnp.where(allowed, score, NEG_FILL)
            top = m_sc[g]
            new_top = jnp.maximum(top, jnp.max(score, axis=1, keepdims=True))
            weights = jnp.where(allowed, jnp.exp(score - new_top), 0.0)
            factor = jnp.exp(top - new_top)
            l_sc[g] = l_sc[g] * factor + jnp.sum(weights, axis=1, keepdims=True)
            acc_sc[g] = acc_sc[g] * factor + jnp.dot(
                weights.astype(jnp.bfloat16), values, preferred_element_type=jnp.float32
            )
            m_sc[g] = new_top

    @pl.when(i == pl.num_programs(0) - 1)
    def _finish():
        lane = lax.broadcasted_iota(jnp.int32, (rows, head_dim), 1)
        stats = jnp.zeros((rows, head_dim), jnp.float32)
        for g in range(q_heads):
            top = m_sc[g]
            valid = top > NEG_FILL / 2
            ref = jnp.where(valid, top.astype(jnp.bfloat16).astype(jnp.float32), NEG_FILL)
            factor = jnp.where(valid, jnp.exp(top - ref), 0.0)
            o_ref[:, g * head_dim : (g + 1) * head_dim] = (acc_sc[g] * factor).astype(o_ref.dtype)
            stats = jnp.where(lane == g, l_sc[g] * factor, stats)
            stats = jnp.where(lane == q_heads + g, ref, stats)
        o_ref[:, q_heads * head_dim :] = stats.astype(o_ref.dtype)


def block_meta(block_table, block_ids, cached_len, block_size, fresh_len):
    used, owner, column = block_owners(block_table, block_ids)
    start = block_size + column * block_size - cached_len[owner]
    start = jnp.clip(start, 0, fresh_len - block_size - 8).astype(jnp.int32)
    return used, owner, column, cached_len, start


def attend(queries, fresh_rows, keys, values, meta, request, span, q_heads, head_dim):
    n_blocks, block_size, kv_width = keys.shape
    q_width = q_heads * head_dim
    out_width = q_width + head_dim
    block = pl.BlockSpec((1, block_size, kv_width), lambda i, *_: (i, 0, 0))
    grid_spec = pltpu.PrefetchScalarGridSpec(
        num_scalar_prefetch=6,
        grid=(n_blocks,),
        in_specs=[
            pl.BlockSpec((span, q_width), lambda i, *_: (0, 0)),
            pl.BlockSpec(fresh_rows.shape, lambda i, *_: (0, 0)),
            block,
            block,
        ],
        out_specs=[pl.BlockSpec((span, out_width), lambda i, *_: (0, 0)), block, block],
        scratch_shapes=[
            pltpu.VMEM((q_heads, span, head_dim), jnp.float32),
            pltpu.VMEM((q_heads, span, head_dim), jnp.float32),
            pltpu.VMEM((q_heads, span, head_dim), jnp.float32),
        ],
    )
    flops = n_blocks * span * q_heads * block_size * head_dim
    return pl.pallas_call(
        functools.partial(attention_kernel, q_heads=q_heads, head_dim=head_dim),
        grid_spec=grid_spec,
        out_shape=(
            jax.ShapeDtypeStruct((span, out_width), jnp.bfloat16),
            jax.ShapeDtypeStruct(keys.shape, keys.dtype),
            jax.ShapeDtypeStruct(values.shape, values.dtype),
        ),
        compiler_params=pltpu.CompilerParams(vmem_limit_bytes=48 * 1024 * 1024),
        cost_estimate=pl.CostEstimate(
            flops=flops,
            transcendentals=n_blocks * span * q_heads * block_size // 4,
            bytes_accessed=span * (q_width + out_width) * 2 + n_blocks * block_size * kv_width * 4,
        ),
    )(*meta, request, queries, fresh_rows, keys, values)


MESH = pl.DeviceIdType.MESH


def multi_exchange_kernel(*refs, specs):
    n_total = sum(s[4] for s in specs)
    srcs, dsts = refs[:n_total], refs[n_total : 2 * n_total]
    send_sem, recv_sem, own_sem = refs[2 * n_total :]
    here = {"kv": lax.axis_index("kv"), "blk": lax.axis_index("blk")}

    def device(axis, index):
        return (index, here["blk"]) if axis == "kv" else (here["kv"], index)

    groups = []
    arr0, sem0 = 0, 0
    for axis, m, stride, gather, n_arr in specs:
        pos = lax.rem(here[axis] // stride, m)
        base = here[axis] - pos * stride
        groups.append((axis, m, stride, gather, n_arr, pos, base, arr0, sem0))
        arr0 += n_arr
        sem0 += m * n_arr

    barrier = pltpu.get_barrier_semaphore()
    for axis, m, stride, gather, n_arr, pos, base, _, _ in groups:
        for k in range(1, m):
            peer = base + lax.rem(pos + k, m) * stride
            pl.semaphore_signal(barrier, inc=1, device_id=device(axis, peer), device_id_type=MESH)
    pl.semaphore_wait(barrier, sum(s[1] - 1 for s in specs))

    def chunk(src, j, m, gather):
        if gather:
            return src
        rows = src.shape[0] // m
        return src.at[pl.ds(pl.multiple_of(j * rows, rows), rows)]

    owns, copies = [], []
    for axis, m, stride, gather, n_arr, pos, base, a0, s0 in groups:
        for a in range(a0, a0 + n_arr):
            own = pltpu.make_async_copy(chunk(srcs[a], pos, m, gather), dsts[a].at[pos], own_sem.at[a])
            own.start()
            owns.append(own)
    for axis, m, stride, gather, n_arr, pos, base, a0, s0 in groups:
        for k in range(1, m):
            peer_pos = lax.rem(pos + k, m)
            for a in range(n_arr):
                copy = pltpu.make_async_remote_copy(
                    src_ref=chunk(srcs[a0 + a], peer_pos, m, gather),
                    dst_ref=dsts[a0 + a].at[pos],
                    send_sem=send_sem.at[s0 + k * n_arr + a],
                    recv_sem=recv_sem.at[s0 + k * n_arr + a],
                    device_id=device(axis, base + peer_pos * stride),
                    device_id_type=MESH,
                )
                copy.start()
                copies.append(copy)
    for own in owns:
        own.wait()
    c = 0
    for axis, m, stride, gather, n_arr, pos, base, a0, s0 in groups:
        for k in range(1, m):
            sender_pos = lax.rem(pos + m - k, m)
            for a in range(n_arr):
                incoming = pltpu.make_async_remote_copy(
                    src_ref=chunk(srcs[a0 + a], pos, m, gather),
                    dst_ref=dsts[a0 + a].at[sender_pos],
                    send_sem=send_sem.at[s0 + k * n_arr + a],
                    recv_sem=recv_sem.at[s0 + k * n_arr + a],
                    device_id=device(axis, base + sender_pos * stride),
                    device_id_type=MESH,
                )
                copies[c].wait_send()
                incoming.wait_recv()
                c += 1


def multi_exchange(groups, collective_id):
    specs, arrays, shapes = [], [], []
    for axis, m, stride, gather, arrs in groups:
        specs.append((axis, m, stride, gather, len(arrs)))
        for x in arrs:
            rows = x.shape[0] if gather else x.shape[0] // m
            arrays.append(x)
            shapes.append(jax.ShapeDtypeStruct((m, rows) + x.shape[1:], x.dtype))
    n_sem = sum(s[1] * s[4] for s in specs)
    return pl.pallas_call(
        functools.partial(multi_exchange_kernel, specs=tuple(specs)),
        out_shape=tuple(shapes),
        in_specs=[pl.BlockSpec(memory_space=pl.ANY)] * len(arrays),
        out_specs=tuple([pl.BlockSpec(memory_space=pl.ANY)] * len(arrays)),
        scratch_shapes=[
            pltpu.SemaphoreType.DMA((n_sem,)),
            pltpu.SemaphoreType.DMA((n_sem,)),
            pltpu.SemaphoreType.DMA((len(arrays),)),
        ],
        compiler_params=pltpu.CompilerParams(collective_id=collective_id, has_side_effects=True),
    )(*arrays)


def on_device(
    hidden_in,
    norm_gain,
    w_query,
    key_weight,
    value_weight,
    b_query,
    key_bias,
    value_bias,
    key_cache,
    value_cache,
    cached_len,
    block_table,
):
    tok_dev = hidden_in.shape[0]
    n_blk = lax.axis_size("blk")
    device = lax.axis_index("blk")
    requests = cached_len.shape[0]
    tokens = tok_dev * n_blk
    span = tokens // requests
    nb_dev, block_size, kv_width = key_cache.shape
    head_dim = HEAD_SIZE
    kv_heads = kv_width // head_dim
    q_heads = w_query.shape[1] // head_dim
    group_size = q_heads // kv_heads
    gain = norm_gain.astype(jnp.float32)
    ring = span // tok_dev
    cols = n_blk // ring
    position = device % ring
    kv_n = lax.axis_size("kv")
    got_hidden, col_keys, col_values = multi_exchange(
        [("kv", kv_n, 1, True, [hidden_in]), ("blk", cols, ring, True, [key_cache, value_cache])], 0
    )
    whole = got_hidden.transpose(1, 0, 2).reshape(tok_dev, kv_n * hidden_in.shape[1])
    wide_in = whole.astype(jnp.float32)
    scale = lax.rsqrt(jnp.mean(wide_in * wide_in, axis=1, keepdims=True) + EPS)
    normed = (wide_in * scale * gain[None, :]).astype(jnp.bfloat16)
    q_lin = jnp.dot(normed, w_query, preferred_element_type=jnp.float32)
    key_linear = jnp.dot(normed, key_weight, preferred_element_type=jnp.float32)
    value_linear = jnp.dot(normed, value_weight, preferred_element_type=jnp.float32)
    my_tokens = device * tok_dev + jnp.arange(tok_dev, dtype=jnp.int32)
    my_pos = lookup(cached_len, my_tokens // span) + my_tokens % span
    fresh_queries = apply_rotary(
        (q_lin + b_query.astype(jnp.float32)[None, :]).reshape(tok_dev, q_heads, head_dim),
        my_pos,
        head_dim,
    )
    fresh_queries = fresh_queries.astype(jnp.bfloat16).reshape(tok_dev, q_heads * head_dim)
    fresh_keys = apply_rotary(
        (key_linear + key_bias.astype(jnp.float32)[None, :]).reshape(tok_dev, kv_heads, head_dim),
        my_pos,
        head_dim,
    )
    fresh_keys = fresh_keys.astype(jnp.bfloat16).reshape(tok_dev, kv_width)
    fresh_values = (value_linear + value_bias.astype(jnp.float32)[None, :]).astype(jnp.bfloat16)
    q_width = q_heads * head_dim
    packed = jnp.concatenate([fresh_queries, fresh_keys, fresh_values], axis=1)
    (ring_packed,) = multi_exchange([("blk", ring, 1, True, [packed])], 1)
    ring_packed = ring_packed.reshape(span, packed.shape[1])
    fresh_rows = jnp.pad(
        ring_packed[:, q_width:].astype(jnp.float32), ((block_size, block_size + 8), (0, 0))
    )
    holders = jnp.arange(cols, dtype=jnp.int32) * ring + position
    col_ids = (holders[:, None] * nb_dev + jnp.arange(nb_dev, dtype=jnp.int32)[None, :]).reshape(-1)
    meta = block_meta(block_table, col_ids, cached_len, block_size, fresh_rows.shape[0])
    request = (device // ring).reshape(1).astype(jnp.int32)
    parts, merged_k, merged_v = attend(
        ring_packed,
        fresh_rows,
        col_keys.reshape(cols * nb_dev, block_size, kv_width),
        col_values.reshape(cols * nb_dev, block_size, kv_width),
        meta,
        request,
        span,
        q_heads,
        head_dim,
    )
    got, back_k, back_v = multi_exchange(
        [("blk", ring, 1, False, [parts]), ("blk", cols, ring, False, [merged_k, merged_v])], 2
    )
    local_ids = device * nb_dev + jnp.arange(nb_dev, dtype=jnp.int32)
    _, owner, _ = block_owners(block_table, local_ids)
    new_k = back_k.reshape(cols, nb_dev, block_size, kv_width)[owner, jnp.arange(nb_dev)]
    new_v = back_v.reshape(cols, nb_dev, block_size, kv_width)[owner, jnp.arange(nb_dev)]
    got = got.astype(jnp.float32)
    got_w = got[..., :q_width].reshape(ring, tok_dev, q_heads, head_dim)
    got_l = got[..., q_width : q_width + group_size]
    got_m = got[..., q_width + group_size : q_width + 2 * group_size]
    best = jnp.max(got_m, axis=0)
    scale_d = jnp.exp(got_m - best[None])
    mine_total = jnp.sum(got_l * scale_d, axis=0)
    mine_weighted = jnp.sum(got_w * scale_d[..., None], axis=0)
    attn_out = (
        (mine_weighted / mine_total[..., None])
        .astype(jnp.bfloat16)
        .reshape(tok_dev, q_heads * head_dim)
    )
    return (attn_out, new_k, new_v)


def solution(mesh):
    in_specs = (
        P("blk", "kv"),
        P(),
        P(None, "kv"),
        P(None, "kv"),
        P(None, "kv"),
        P("kv"),
        P("kv"),
        P("kv"),
        P("blk", None, "kv"),
        P("blk", None, "kv"),
        P(),
        P(),
    )
    out_specs = (P("blk", "kv"), P("blk", None, "kv"), P("blk", None, "kv"))
    return jax.shard_map(
        on_device, mesh=mesh, in_specs=in_specs, out_specs=out_specs, check_vma=False
    )
```

```python
import functools
import math

import jax
import jax.numpy as jnp
from jax import lax
from jax.experimental import pallas as pl
from jax.experimental.pallas import tpu as pltpu
from jax.sharding import PartitionSpec as P

HEAD_SIZE = 128


EPS = 1e-06
THETA = 1000000.0
NEG_FILL = -1e30


def apply_rotary(values, token_positions, head_dim):
    half = head_dim // 2
    rates = THETA ** (-(jnp.arange(half, dtype=jnp.float32) * 2.0) / head_dim)
    angle = token_positions.astype(jnp.float32)[:, None] * rates[None, :]
    cosine = jnp.cos(angle)[:, None, :]
    sine = jnp.sin(angle)[:, None, :]
    first = values[..., :half]
    second_half = values[..., half:]
    return jnp.concatenate(
        [first * cosine - second_half * sine, second_half * cosine + first * sine], axis=-1
    )


def lookup(table_values, slot_index):
    matches = slot_index[:, None] == jnp.arange(table_values.shape[0], dtype=jnp.int32)[None, :]
    return jnp.sum(jnp.where(matches, table_values[None, :], 0), axis=1)


def block_owners(block_table, block_ids):
    matched = block_table[None, :, :] == block_ids[:, None, None]
    row_ids = jnp.arange(block_table.shape[0], dtype=jnp.int32)[None, :, None]
    col_ids = jnp.arange(block_table.shape[1], dtype=jnp.int32)[None, None, :]
    used = jnp.any(matched, axis=(1, 2)).astype(jnp.int32)
    owner = jnp.sum(jnp.where(matched, row_ids, 0), axis=(1, 2)).astype(jnp.int32)
    column = jnp.sum(jnp.where(matched, col_ids, 0), axis=(1, 2)).astype(jnp.int32)
    return used, owner, column


def merged_block(i, used_ref, owner_ref, column_ref, clen_ref, start_ref, fresh_ref, kc_ref, vc_ref, span):
    block_size, kv_width = kc_ref.shape[1], kc_ref.shape[2]
    start = start_ref[i]
    base = pl.multiple_of((start // 8) * 8, 8)
    window = fresh_ref[pl.ds(base, block_size + 8), :].astype(jnp.bfloat16)
    pick = lax.broadcasted_iota(jnp.int32, (block_size, block_size + 8), 1) == (
        lax.broadcasted_iota(jnp.int32, (block_size, block_size + 8), 0) + (start - base)
    )
    window = jnp.dot(pick.astype(jnp.bfloat16), window, preferred_element_type=jnp.float32)
    slot_pos = column_ref[i] * block_size + lax.broadcasted_iota(
        jnp.int32, (block_size, kv_width), 0
    )
    first_new = clen_ref[owner_ref[i]]
    fresh = (used_ref[i] == 1) & (slot_pos >= first_new) & (slot_pos < first_new + span)
    keys = jnp.where(fresh, window[:, :kv_width], kc_ref[i].astype(jnp.float32))
    values = jnp.where(fresh, window[:, kv_width:], vc_ref[i].astype(jnp.float32))
    return keys.astype(kc_ref.dtype), values.astype(vc_ref.dtype)


def attention_kernel(
    used_ref, owner_ref, column_ref, clen_ref, start_ref, req_ref, q_ref, fresh_ref, kc_ref, vc_ref,
    o_ref, nk_ref, nv_ref, m_sc, l_sc, acc_sc, *, q_heads, head_dim
):
    i = pl.program_id(0)
    r = req_ref[0]
    rows = q_ref.shape[0]
    block_size = kc_ref.shape[1]

    @pl.when(i == 0)
    def _init():
        m_sc[...] = jnp.full(m_sc.shape, NEG_FILL, jnp.float32)
        l_sc[...] = jnp.zeros(l_sc.shape, jnp.float32)
        acc_sc[...] = jnp.zeros(acc_sc.shape, jnp.float32)

    active = (used_ref[i] == 1) & (owner_ref[i] == r)

    @pl.when(jnp.logical_not(active))
    def _keep():
        nk_ref[i] = kc_ref[i]
        nv_ref[i] = vc_ref[i]

    @pl.when(active)
    def _work():
        keys, values = merged_block(
            i, used_ref, owner_ref, column_ref, clen_ref, start_ref, fresh_ref, kc_ref, vc_ref, rows
        )
        nk_ref[i] = keys
        nv_ref[i] = values
        query_pos = clen_ref[r] + lax.broadcasted_iota(jnp.int32, (rows, block_size), 0)
        key_pos = column_ref[i] * block_size + lax.broadcasted_iota(
            jnp.int32, (rows, block_size), 1
        )
        allowed = key_pos <= query_pos
        for g in range(q_heads):
            queries = q_ref[:, g * head_dim : (g + 1) * head_dim]
            score = lax.dot_general(
                queries, keys, (((1,), (1,)), ((), ())), preferred_element_type=jnp.float32
            ) / math.sqrt(head_dim)
            score = jnp.where(allowed, score, NEG_FILL)
            top = m_sc[g]
            new_top = jnp.maximum(top, jnp.max(score, axis=1, keepdims=True))
            weights = jnp.where(allowed, jnp.exp(score - new_top), 0.0)
            factor = jnp.exp(top - new_top)
            l_sc[g] = l_sc[g] * factor + jnp.sum(weights, axis=1, keepdims=True)
            acc_sc[g] = acc_sc[g] * factor + jnp.dot(
                weights.astype(jnp.bfloat16), values, preferred_element_type=jnp.float32
            )
            m_sc[g] = new_top

    @pl.when(i == pl.num_programs(0) - 1)
    def _finish():
        lane = lax.broadcasted_iota(jnp.int32, (rows, head_dim), 1)
        stats = jnp.zeros((rows, head_dim), jnp.float32)
        for g in range(q_heads):
            top = m_sc[g]
            valid = top > NEG_FILL / 2
            ref = jnp.where(valid, top.astype(jnp.bfloat16).astype(jnp.float32), NEG_FILL)
            factor = jnp.where(valid, jnp.exp(top - ref), 0.0)
            o_ref[:, g * head_dim : (g + 1) * head_dim] = (acc_sc[g] * factor).astype(o_ref.dtype)
            stats = jnp.where(lane == g, l_sc[g] * factor, stats)
            stats = jnp.where(lane == q_heads + g, ref, stats)
        o_ref[:, q_heads * head_dim :] = stats.astype(o_ref.dtype)


def block_meta(block_table, block_ids, cached_len, block_size, fresh_len):
    used, owner, column = block_owners(block_table, block_ids)
    start = block_size + column * block_size - cached_len[owner]
    start = jnp.clip(start, 0, fresh_len - block_size - 8).astype(jnp.int32)
    return used, owner, column, cached_len, start


def attend(queries, fresh_rows, keys, values, meta, request, span, q_heads, head_dim):
    n_blocks, block_size, kv_width = keys.shape
    q_width = q_heads * head_dim
    out_width = q_width + head_dim
    block = pl.BlockSpec(keys.shape, lambda i, *_: (0, 0, 0))
    grid_spec = pltpu.PrefetchScalarGridSpec(
        num_scalar_prefetch=6,
        grid=(n_blocks,),
        in_specs=[
            pl.BlockSpec((span, q_width), lambda i, *_: (0, 0)),
            pl.BlockSpec(fresh_rows.shape, lambda i, *_: (0, 0)),
            block,
            block,
        ],
        out_specs=[pl.BlockSpec((span, out_width), lambda i, *_: (0, 0)), block, block],
        scratch_shapes=[
            pltpu.VMEM((q_heads, span, head_dim), jnp.float32),
            pltpu.VMEM((q_heads, span, head_dim), jnp.float32),
            pltpu.VMEM((q_heads, span, head_dim), jnp.float32),
        ],
    )
    flops = n_blocks * span * q_heads * block_size * head_dim
    return pl.pallas_call(
        functools.partial(attention_kernel, q_heads=q_heads, head_dim=head_dim),
        grid_spec=grid_spec,
        out_shape=(
            jax.ShapeDtypeStruct((span, out_width), jnp.bfloat16),
            jax.ShapeDtypeStruct(keys.shape, keys.dtype),
            jax.ShapeDtypeStruct(values.shape, values.dtype),
        ),
        compiler_params=pltpu.CompilerParams(vmem_limit_bytes=48 * 1024 * 1024),
        cost_estimate=pl.CostEstimate(
            flops=flops,
            transcendentals=n_blocks * span * q_heads * block_size // 4,
            bytes_accessed=span * (q_width + out_width) * 2 + n_blocks * block_size * kv_width * 4,
        ),
    )(*meta, request, queries, fresh_rows, keys, values)


MESH = pl.DeviceIdType.MESH


def multi_exchange_kernel(*refs, specs):
    n_total = sum(s[4] for s in specs)
    srcs, dsts = refs[:n_total], refs[n_total : 2 * n_total]
    send_sem, recv_sem, own_sem = refs[2 * n_total :]
    here = {"kv": lax.axis_index("kv"), "blk": lax.axis_index("blk")}

    def device(axis, index):
        return (index, here["blk"]) if axis == "kv" else (here["kv"], index)

    groups = []
    arr0, sem0 = 0, 0
    for axis, m, stride, gather, n_arr in specs:
        pos = lax.rem(here[axis] // stride, m)
        base = here[axis] - pos * stride
        groups.append((axis, m, stride, gather, n_arr, pos, base, arr0, sem0))
        arr0 += n_arr
        sem0 += m * n_arr

    barrier = pltpu.get_barrier_semaphore()
    for axis, m, stride, gather, n_arr, pos, base, _, _ in groups:
        for k in range(1, m):
            peer = base + lax.rem(pos + k, m) * stride
            pl.semaphore_signal(barrier, inc=1, device_id=device(axis, peer), device_id_type=MESH)
    pl.semaphore_wait(barrier, sum(s[1] - 1 for s in specs))

    def chunk(src, j, m, gather):
        if gather:
            return src
        rows = src.shape[0] // m
        return src.at[pl.ds(pl.multiple_of(j * rows, rows), rows)]

    owns, copies = [], []
    for axis, m, stride, gather, n_arr, pos, base, a0, s0 in groups:
        for a in range(a0, a0 + n_arr):
            own = pltpu.make_async_copy(chunk(srcs[a], pos, m, gather), dsts[a].at[pos], own_sem.at[a])
            own.start()
            owns.append(own)
    for axis, m, stride, gather, n_arr, pos, base, a0, s0 in groups:
        for k in range(1, m):
            peer_pos = lax.rem(pos + k, m)
            for a in range(n_arr):
                copy = pltpu.make_async_remote_copy(
                    src_ref=chunk(srcs[a0 + a], peer_pos, m, gather),
                    dst_ref=dsts[a0 + a].at[pos],
                    send_sem=send_sem.at[s0 + k * n_arr + a],
                    recv_sem=recv_sem.at[s0 + k * n_arr + a],
                    device_id=device(axis, base + peer_pos * stride),
                    device_id_type=MESH,
                )
                copy.start()
                copies.append(copy)
    for own in owns:
        own.wait()
    c = 0
    for axis, m, stride, gather, n_arr, pos, base, a0, s0 in groups:
        for k in range(1, m):
            sender_pos = lax.rem(pos + m - k, m)
            for a in range(n_arr):
                incoming = pltpu.make_async_remote_copy(
                    src_ref=chunk(srcs[a0 + a], pos, m, gather),
                    dst_ref=dsts[a0 + a].at[sender_pos],
                    send_sem=send_sem.at[s0 + k * n_arr + a],
                    recv_sem=recv_sem.at[s0 + k * n_arr + a],
                    device_id=device(axis, base + sender_pos * stride),
                    device_id_type=MESH,
                )
                copies[c].wait_send()
                incoming.wait_recv()
                c += 1


def multi_exchange(groups, collective_id):
    specs, arrays, shapes = [], [], []
    for axis, m, stride, gather, arrs in groups:
        specs.append((axis, m, stride, gather, len(arrs)))
        for x in arrs:
            rows = x.shape[0] if gather else x.shape[0] // m
            arrays.append(x)
            shapes.append(jax.ShapeDtypeStruct((m, rows) + x.shape[1:], x.dtype))
    n_sem = sum(s[1] * s[4] for s in specs)
    return pl.pallas_call(
        functools.partial(multi_exchange_kernel, specs=tuple(specs)),
        out_shape=tuple(shapes),
        in_specs=[pl.BlockSpec(memory_space=pl.ANY)] * len(arrays),
        out_specs=tuple([pl.BlockSpec(memory_space=pl.ANY)] * len(arrays)),
        scratch_shapes=[
            pltpu.SemaphoreType.DMA((n_sem,)),
            pltpu.SemaphoreType.DMA((n_sem,)),
            pltpu.SemaphoreType.DMA((len(arrays),)),
        ],
        compiler_params=pltpu.CompilerParams(collective_id=collective_id, has_side_effects=True),
    )(*arrays)


def on_device(
    hidden_in,
    norm_gain,
    w_query,
    key_weight,
    value_weight,
    b_query,
    key_bias,
    value_bias,
    key_cache,
    value_cache,
    cached_len,
    block_table,
):
    tok_dev = hidden_in.shape[0]
    n_blk = lax.axis_size("blk")
    device = lax.axis_index("blk")
    requests = cached_len.shape[0]
    tokens = tok_dev * n_blk
    span = tokens // requests
    nb_dev, block_size, kv_width = key_cache.shape
    head_dim = HEAD_SIZE
    kv_heads = kv_width // head_dim
    q_heads = w_query.shape[1] // head_dim
    group_size = q_heads // kv_heads
    gain = norm_gain.astype(jnp.float32)
    ring = span // tok_dev
    cols = n_blk // ring
    position = device % ring
    kv_n = lax.axis_size("kv")
    got_hidden, col_keys, col_values = multi_exchange(
        [("kv", kv_n, 1, True, [hidden_in]), ("blk", cols, ring, True, [key_cache, value_cache])], 0
    )
    whole = got_hidden.transpose(1, 0, 2).reshape(tok_dev, kv_n * hidden_in.shape[1])
    wide_in = whole.astype(jnp.float32)
    scale = lax.rsqrt(jnp.mean(wide_in * wide_in, axis=1, keepdims=True) + EPS)
    normed = (wide_in * scale * gain[None, :]).astype(jnp.bfloat16)
    q_lin = jnp.dot(normed, w_query, preferred_element_type=jnp.float32)
    key_linear = jnp.dot(normed, key_weight, preferred_element_type=jnp.float32)
    value_linear = jnp.dot(normed, value_weight, preferred_element_type=jnp.float32)
    my_tokens = device * tok_dev + jnp.arange(tok_dev, dtype=jnp.int32)
    my_pos = lookup(cached_len, my_tokens // span) + my_tokens % span
    fresh_queries = apply_rotary(
        (q_lin + b_query.astype(jnp.float32)[None, :]).reshape(tok_dev, q_heads, head_dim),
        my_pos,
        head_dim,
    )
    fresh_queries = fresh_queries.astype(jnp.bfloat16).reshape(tok_dev, q_heads * head_dim)
    fresh_keys = apply_rotary(
        (key_linear + key_bias.astype(jnp.float32)[None, :]).reshape(tok_dev, kv_heads, head_dim),
        my_pos,
        head_dim,
    )
    fresh_keys = fresh_keys.astype(jnp.bfloat16).reshape(tok_dev, kv_width)
    fresh_values = (value_linear + value_bias.astype(jnp.float32)[None, :]).astype(jnp.bfloat16)
    q_width = q_heads * head_dim
    packed = jnp.concatenate([fresh_queries, fresh_keys, fresh_values], axis=1)
    (ring_packed,) = multi_exchange([("blk", ring, 1, True, [packed])], 1)
    ring_packed = ring_packed.reshape(span, packed.shape[1])
    fresh_rows = jnp.pad(
        ring_packed[:, q_width:].astype(jnp.float32), ((block_size, block_size + 8), (0, 0))
    )
    holders = jnp.arange(cols, dtype=jnp.int32) * ring + position
    col_ids = (holders[:, None] * nb_dev + jnp.arange(nb_dev, dtype=jnp.int32)[None, :]).reshape(-1)
    meta = block_meta(block_table, col_ids, cached_len, block_size, fresh_rows.shape[0])
    request = (device // ring).reshape(1).astype(jnp.int32)
    parts, merged_k, merged_v = attend(
        ring_packed,
        fresh_rows,
        col_keys.reshape(cols * nb_dev, block_size, kv_width),
        col_values.reshape(cols * nb_dev, block_size, kv_width),
        meta,
        request,
        span,
        q_heads,
        head_dim,
    )
    got, back_k, back_v = multi_exchange(
        [("blk", ring, 1, False, [parts]), ("blk", cols, ring, False, [merged_k, merged_v])], 2
    )
    local_ids = device * nb_dev + jnp.arange(nb_dev, dtype=jnp.int32)
    _, owner, _ = block_owners(block_table, local_ids)
    new_k = back_k.reshape(cols, nb_dev, block_size, kv_width)[owner, jnp.arange(nb_dev)]
    new_v = back_v.reshape(cols, nb_dev, block_size, kv_width)[owner, jnp.arange(nb_dev)]
    got = got.astype(jnp.float32)
    got_w = got[..., :q_width].reshape(ring, tok_dev, q_heads, head_dim)
    got_l = got[..., q_width : q_width + group_size]
    got_m = got[..., q_width + group_size : q_width + 2 * group_size]
    best = jnp.max(got_m, axis=0)
    scale_d = jnp.exp(got_m - best[None])
    mine_total = jnp.sum(got_l * scale_d, axis=0)
    mine_weighted = jnp.sum(got_w * scale_d[..., None], axis=0)
    attn_out = (
        (mine_weighted / mine_total[..., None])
        .astype(jnp.bfloat16)
        .reshape(tok_dev, q_heads * head_dim)
    )
    return (attn_out, new_k, new_v)


def solution(mesh):
    in_specs = (
        P("blk", "kv"),
        P(),
        P(None, "kv"),
        P(None, "kv"),
        P(None, "kv"),
        P("kv"),
        P("kv"),
        P("kv"),
        P("blk", None, "kv"),
        P("blk", None, "kv"),
        P(),
        P(),
    )
    out_specs = (P("blk", "kv"), P("blk", None, "kv"), P("blk", None, "kv"))
    return jax.shard_map(
        on_device, mesh=mesh, in_specs=in_specs, out_specs=out_specs, check_vma=False
    )
```

```python
import functools
import math

import jax
import jax.numpy as jnp
from jax import lax
from jax.experimental import pallas as pl
from jax.experimental.pallas import tpu as pltpu
from jax.sharding import PartitionSpec as P

HEAD_SIZE = 128


EPS = 1e-06
THETA = 1000000.0
NEG_FILL = -1e30


def apply_rotary(values, token_positions, head_dim):
    half = head_dim // 2
    rates = THETA ** (-(jnp.arange(half, dtype=jnp.float32) * 2.0) / head_dim)
    angle = token_positions.astype(jnp.float32)[:, None] * rates[None, :]
    cosine = jnp.cos(angle)[:, None, :]
    sine = jnp.sin(angle)[:, None, :]
    first = values[..., :half]
    second_half = values[..., half:]
    return jnp.concatenate(
        [first * cosine - second_half * sine, second_half * cosine + first * sine], axis=-1
    )


def lookup(table_values, slot_index):
    matches = slot_index[:, None] == jnp.arange(table_values.shape[0], dtype=jnp.int32)[None, :]
    return jnp.sum(jnp.where(matches, table_values[None, :], 0), axis=1)


def block_owners(block_table, block_ids):
    matched = block_table[None, :, :] == block_ids[:, None, None]
    row_ids = jnp.arange(block_table.shape[0], dtype=jnp.int32)[None, :, None]
    col_ids = jnp.arange(block_table.shape[1], dtype=jnp.int32)[None, None, :]
    used = jnp.any(matched, axis=(1, 2)).astype(jnp.int32)
    owner = jnp.sum(jnp.where(matched, row_ids, 0), axis=(1, 2)).astype(jnp.int32)
    column = jnp.sum(jnp.where(matched, col_ids, 0), axis=(1, 2)).astype(jnp.int32)
    return used, owner, column


def merged_block(i, used_ref, owner_ref, column_ref, clen_ref, start_ref, fresh_ref, kc_ref, vc_ref, span):
    block_size, kv_width = kc_ref.shape[1], kc_ref.shape[2]
    start = start_ref[i]
    base = pl.multiple_of((start // 8) * 8, 8)
    window = fresh_ref[pl.ds(base, block_size + 8), :].astype(jnp.bfloat16)
    pick = lax.broadcasted_iota(jnp.int32, (block_size, block_size + 8), 1) == (
        lax.broadcasted_iota(jnp.int32, (block_size, block_size + 8), 0) + (start - base)
    )
    window = jnp.dot(pick.astype(jnp.bfloat16), window, preferred_element_type=jnp.float32)
    slot_pos = column_ref[i] * block_size + lax.broadcasted_iota(
        jnp.int32, (block_size, kv_width), 0
    )
    first_new = clen_ref[owner_ref[i]]
    fresh = (used_ref[i] == 1) & (slot_pos >= first_new) & (slot_pos < first_new + span)
    keys = jnp.where(fresh, window[:, :kv_width], kc_ref[i].astype(jnp.float32))
    values = jnp.where(fresh, window[:, kv_width:], vc_ref[i].astype(jnp.float32))
    return keys.astype(kc_ref.dtype), values.astype(vc_ref.dtype)


def attention_kernel(
    used_ref, owner_ref, column_ref, clen_ref, start_ref, req_ref, q_ref, fresh_ref, kc_ref, vc_ref,
    o_ref, nk_ref, nv_ref, m_sc, l_sc, acc_sc, *, q_heads, head_dim
):
    i = pl.program_id(0)
    r = req_ref[0]
    rows = q_ref.shape[0]
    block_size = kc_ref.shape[1]

    @pl.when(i == 0)
    def _init():
        m_sc[...] = jnp.full(m_sc.shape, NEG_FILL, jnp.float32)
        l_sc[...] = jnp.zeros(l_sc.shape, jnp.float32)
        acc_sc[...] = jnp.zeros(acc_sc.shape, jnp.float32)

    active = (used_ref[i] == 1) & (owner_ref[i] == r)

    @pl.when(jnp.logical_not(active))
    def _keep():
        nk_ref[i] = kc_ref[i]
        nv_ref[i] = vc_ref[i]

    @pl.when(active)
    def _work():
        keys, values = merged_block(
            i, used_ref, owner_ref, column_ref, clen_ref, start_ref, fresh_ref, kc_ref, vc_ref, rows
        )
        nk_ref[i] = keys
        nv_ref[i] = values
        query_pos = clen_ref[r] + lax.broadcasted_iota(jnp.int32, (rows, block_size), 0)
        key_pos = column_ref[i] * block_size + lax.broadcasted_iota(
            jnp.int32, (rows, block_size), 1
        )
        allowed = key_pos <= query_pos
        for g in range(q_heads):
            queries = q_ref[:, g * head_dim : (g + 1) * head_dim]
            score = lax.dot_general(
                queries, keys, (((1,), (1,)), ((), ())), preferred_element_type=jnp.float32
            ) / math.sqrt(head_dim)
            score = jnp.where(allowed, score, NEG_FILL)
            top = m_sc[g]
            new_top = jnp.maximum(top, jnp.max(score, axis=1, keepdims=True))
            weights = jnp.where(allowed, jnp.exp(score - new_top), 0.0)
            factor = jnp.exp(top - new_top)
            l_sc[g] = l_sc[g] * factor + jnp.sum(weights, axis=1, keepdims=True)
            acc_sc[g] = acc_sc[g] * factor + jnp.dot(
                weights.astype(jnp.bfloat16), values, preferred_element_type=jnp.float32
            )
            m_sc[g] = new_top

    @pl.when(i == pl.num_programs(0) - 1)
    def _finish():
        lane = lax.broadcasted_iota(jnp.int32, (rows, head_dim), 1)
        stats = jnp.zeros((rows, head_dim), jnp.float32)
        for g in range(q_heads):
            top = m_sc[g]
            valid = top > NEG_FILL / 2
            ref = jnp.where(valid, top.astype(jnp.bfloat16).astype(jnp.float32), NEG_FILL)
            factor = jnp.where(valid, jnp.exp(top - ref), 0.0)
            o_ref[:, g * head_dim : (g + 1) * head_dim] = (acc_sc[g] * factor).astype(o_ref.dtype)
            stats = jnp.where(lane == g, l_sc[g] * factor, stats)
            stats = jnp.where(lane == q_heads + g, ref, stats)
        o_ref[:, q_heads * head_dim :] = stats.astype(o_ref.dtype)


def block_meta(block_table, block_ids, cached_len, block_size, fresh_len):
    used, owner, column = block_owners(block_table, block_ids)
    start = block_size + column * block_size - cached_len[owner]
    start = jnp.clip(start, 0, fresh_len - block_size - 8).astype(jnp.int32)
    return used, owner, column, cached_len, start


def attend(queries, fresh_rows, keys, values, meta, request, span, q_heads, head_dim):
    n_blocks, block_size, kv_width = keys.shape
    q_width = q_heads * head_dim
    out_width = q_width + head_dim
    block = pl.BlockSpec(keys.shape, lambda i, *_: (0, 0, 0))
    grid_spec = pltpu.PrefetchScalarGridSpec(
        num_scalar_prefetch=6,
        grid=(n_blocks,),
        in_specs=[
            pl.BlockSpec((span, q_width), lambda i, *_: (0, 0)),
            pl.BlockSpec(fresh_rows.shape, lambda i, *_: (0, 0)),
            block,
            block,
        ],
        out_specs=[pl.BlockSpec((span, out_width), lambda i, *_: (0, 0)), block, block],
        scratch_shapes=[
            pltpu.VMEM((q_heads, span, head_dim), jnp.float32),
            pltpu.VMEM((q_heads, span, head_dim), jnp.float32),
            pltpu.VMEM((q_heads, span, head_dim), jnp.float32),
        ],
    )
    flops = n_blocks * span * q_heads * block_size * head_dim
    return pl.pallas_call(
        functools.partial(attention_kernel, q_heads=q_heads, head_dim=head_dim),
        grid_spec=grid_spec,
        out_shape=(
            jax.ShapeDtypeStruct((span, out_width), jnp.bfloat16),
            jax.ShapeDtypeStruct(keys.shape, keys.dtype),
            jax.ShapeDtypeStruct(values.shape, values.dtype),
        ),
        compiler_params=pltpu.CompilerParams(vmem_limit_bytes=48 * 1024 * 1024),
        cost_estimate=pl.CostEstimate(
            flops=flops,
            transcendentals=n_blocks * span * q_heads * block_size // 4,
            bytes_accessed=span * (q_width + out_width) * 2 + n_blocks * block_size * kv_width * 4,
        ),
    )(*meta, request, queries, fresh_rows, keys, values)


MESH = pl.DeviceIdType.MESH


def multi_exchange_kernel(*refs, specs):
    n_total = sum(s[4] for s in specs)
    srcs, dsts = refs[:n_total], refs[n_total : 2 * n_total]
    send_sem, recv_sem, own_sem = refs[2 * n_total :]
    here = {"kv": lax.axis_index("kv"), "blk": lax.axis_index("blk")}

    def device(axis, index):
        return (index, here["blk"]) if axis == "kv" else (here["kv"], index)

    groups = []
    arr0, sem0 = 0, 0
    for axis, m, stride, gather, n_arr in specs:
        pos = lax.rem(here[axis] // stride, m)
        base = here[axis] - pos * stride
        groups.append((axis, m, stride, gather, n_arr, pos, base, arr0, sem0))
        arr0 += n_arr
        sem0 += m * n_arr

    barrier = pltpu.get_barrier_semaphore()
    for axis, m, stride, gather, n_arr, pos, base, _, _ in groups:
        for k in range(1, m):
            peer = base + lax.rem(pos + k, m) * stride
            pl.semaphore_signal(barrier, inc=1, device_id=device(axis, peer), device_id_type=MESH)
    pl.semaphore_wait(barrier, sum(s[1] - 1 for s in specs))

    def chunk(src, j, m, gather):
        if gather:
            return src
        rows = src.shape[0] // m
        return src.at[pl.ds(pl.multiple_of(j * rows, rows), rows)]

    owns, copies = [], []
    for axis, m, stride, gather, n_arr, pos, base, a0, s0 in groups:
        for a in range(a0, a0 + n_arr):
            own = pltpu.make_async_copy(chunk(srcs[a], pos, m, gather), dsts[a].at[pos], own_sem.at[a])
            own.start()
            owns.append(own)
    for axis, m, stride, gather, n_arr, pos, base, a0, s0 in groups:
        for k in range(1, m):
            peer_pos = lax.rem(pos + k, m)
            for a in range(n_arr):
                copy = pltpu.make_async_remote_copy(
                    src_ref=chunk(srcs[a0 + a], peer_pos, m, gather),
                    dst_ref=dsts[a0 + a].at[pos],
                    send_sem=send_sem.at[s0 + k * n_arr + a],
                    recv_sem=recv_sem.at[s0 + k * n_arr + a],
                    device_id=device(axis, base + peer_pos * stride),
                    device_id_type=MESH,
                )
                copy.start()
                copies.append(copy)
    for own in owns:
        own.wait()
    c = 0
    for axis, m, stride, gather, n_arr, pos, base, a0, s0 in groups:
        for k in range(1, m):
            sender_pos = lax.rem(pos + m - k, m)
            for a in range(n_arr):
                incoming = pltpu.make_async_remote_copy(
                    src_ref=chunk(srcs[a0 + a], pos, m, gather),
                    dst_ref=dsts[a0 + a].at[sender_pos],
                    send_sem=send_sem.at[s0 + k * n_arr + a],
                    recv_sem=recv_sem.at[s0 + k * n_arr + a],
                    device_id=device(axis, base + sender_pos * stride),
                    device_id_type=MESH,
                )
                copies[c].wait_send()
                incoming.wait_recv()
                c += 1


def multi_exchange(groups, collective_id):
    specs, arrays, shapes = [], [], []
    for axis, m, stride, gather, arrs in groups:
        specs.append((axis, m, stride, gather, len(arrs)))
        for x in arrs:
            rows = x.shape[0] if gather else x.shape[0] // m
            arrays.append(x)
            shapes.append(jax.ShapeDtypeStruct((m, rows) + x.shape[1:], x.dtype))
    n_sem = sum(s[1] * s[4] for s in specs)
    return pl.pallas_call(
        functools.partial(multi_exchange_kernel, specs=tuple(specs)),
        out_shape=tuple(shapes),
        in_specs=[pl.BlockSpec(memory_space=pl.ANY)] * len(arrays),
        out_specs=tuple([pl.BlockSpec(memory_space=pl.ANY)] * len(arrays)),
        scratch_shapes=[
            pltpu.SemaphoreType.DMA((n_sem,)),
            pltpu.SemaphoreType.DMA((n_sem,)),
            pltpu.SemaphoreType.DMA((len(arrays),)),
        ],
        compiler_params=pltpu.CompilerParams(collective_id=collective_id, has_side_effects=True),
    )(*arrays)


def on_device(
    hidden_in,
    norm_gain,
    w_query,
    key_weight,
    value_weight,
    b_query,
    key_bias,
    value_bias,
    key_cache,
    value_cache,
    cached_len,
    block_table,
):
    tok_dev = hidden_in.shape[0]
    n_blk = lax.axis_size("blk")
    device = lax.axis_index("blk")
    requests = cached_len.shape[0]
    tokens = tok_dev * n_blk
    span = tokens // requests
    nb_dev, block_size, kv_width = key_cache.shape
    head_dim = HEAD_SIZE
    kv_heads = kv_width // head_dim
    q_heads = w_query.shape[1] // head_dim
    group_size = q_heads // kv_heads
    gain = norm_gain.astype(jnp.float32)
    ring = span // tok_dev
    cols = n_blk // ring
    position = device % ring
    kv_n = lax.axis_size("kv")
    (got_hidden,) = multi_exchange([("kv", kv_n, 1, True, [hidden_in])], 0)
    whole = got_hidden.transpose(1, 0, 2).reshape(tok_dev, kv_n * hidden_in.shape[1])
    wide_in = whole.astype(jnp.float32)
    scale = lax.rsqrt(jnp.mean(wide_in * wide_in, axis=1, keepdims=True) + EPS)
    normed = (wide_in * scale * gain[None, :]).astype(jnp.bfloat16)
    q_lin = jnp.dot(normed, w_query, preferred_element_type=jnp.float32)
    key_linear = jnp.dot(normed, key_weight, preferred_element_type=jnp.float32)
    value_linear = jnp.dot(normed, value_weight, preferred_element_type=jnp.float32)
    my_tokens = device * tok_dev + jnp.arange(tok_dev, dtype=jnp.int32)
    my_pos = lookup(cached_len, my_tokens // span) + my_tokens % span
    fresh_queries = apply_rotary(
        (q_lin + b_query.astype(jnp.float32)[None, :]).reshape(tok_dev, q_heads, head_dim),
        my_pos,
        head_dim,
    )
    fresh_queries = fresh_queries.astype(jnp.bfloat16).reshape(tok_dev, q_heads * head_dim)
    fresh_keys = apply_rotary(
        (key_linear + key_bias.astype(jnp.float32)[None, :]).reshape(tok_dev, kv_heads, head_dim),
        my_pos,
        head_dim,
    )
    fresh_keys = fresh_keys.astype(jnp.bfloat16).reshape(tok_dev, kv_width)
    fresh_values = (value_linear + value_bias.astype(jnp.float32)[None, :]).astype(jnp.bfloat16)
    q_width = q_heads * head_dim
    packed = jnp.concatenate([fresh_queries, fresh_keys, fresh_values], axis=1)
    ring_packed, col_keys, col_values = multi_exchange(
        [("blk", ring, 1, True, [packed]), ("blk", cols, ring, True, [key_cache, value_cache])], 1
    )
    ring_packed = ring_packed.reshape(span, packed.shape[1])
    fresh_rows = jnp.pad(
        ring_packed[:, q_width:].astype(jnp.float32), ((block_size, block_size + 8), (0, 0))
    )
    holders = jnp.arange(cols, dtype=jnp.int32) * ring + position
    col_ids = (holders[:, None] * nb_dev + jnp.arange(nb_dev, dtype=jnp.int32)[None, :]).reshape(-1)
    meta = block_meta(block_table, col_ids, cached_len, block_size, fresh_rows.shape[0])
    request = (device // ring).reshape(1).astype(jnp.int32)
    parts, merged_k, merged_v = attend(
        ring_packed,
        fresh_rows,
        col_keys.reshape(cols * nb_dev, block_size, kv_width),
        col_values.reshape(cols * nb_dev, block_size, kv_width),
        meta,
        request,
        span,
        q_heads,
        head_dim,
    )
    got, back_k, back_v = multi_exchange(
        [("blk", ring, 1, False, [parts]), ("blk", cols, ring, False, [merged_k, merged_v])], 2
    )
    local_ids = device * nb_dev + jnp.arange(nb_dev, dtype=jnp.int32)
    _, owner, _ = block_owners(block_table, local_ids)
    new_k = back_k.reshape(cols, nb_dev, block_size, kv_width)[owner, jnp.arange(nb_dev)]
    new_v = back_v.reshape(cols, nb_dev, block_size, kv_width)[owner, jnp.arange(nb_dev)]
    got = got.astype(jnp.float32)
    got_w = got[..., :q_width].reshape(ring, tok_dev, q_heads, head_dim)
    got_l = got[..., q_width : q_width + group_size]
    got_m = got[..., q_width + group_size : q_width + 2 * group_size]
    best = jnp.max(got_m, axis=0)
    scale_d = jnp.exp(got_m - best[None])
    mine_total = jnp.sum(got_l * scale_d, axis=0)
    mine_weighted = jnp.sum(got_w * scale_d[..., None], axis=0)
    attn_out = (
        (mine_weighted / mine_total[..., None])
        .astype(jnp.bfloat16)
        .reshape(tok_dev, q_heads * head_dim)
    )
    return (attn_out, new_k, new_v)


def solution(mesh):
    in_specs = (
        P("blk", "kv"),
        P(),
        P(None, "kv"),
        P(None, "kv"),
        P(None, "kv"),
        P("kv"),
        P("kv"),
        P("kv"),
        P("blk", None, "kv"),
        P("blk", None, "kv"),
        P(),
        P(),
    )
    out_specs = (P("blk", "kv"), P("blk", None, "kv"), P("blk", None, "kv"))
    return jax.shard_map(
        on_device, mesh=mesh, in_specs=in_specs, out_specs=out_specs, check_vma=False
    )
```

```python
import functools
import math

import jax
import jax.numpy as jnp
from jax import lax
from jax.experimental import pallas as pl
from jax.experimental.pallas import tpu as pltpu
from jax.sharding import PartitionSpec as P

HEAD_SIZE = 128


EPS = 1e-06
THETA = 1000000.0
NEG_FILL = -1e30


def apply_rotary(values, token_positions, head_dim):
    half = head_dim // 2
    rates = THETA ** (-(jnp.arange(half, dtype=jnp.float32) * 2.0) / head_dim)
    angle = token_positions.astype(jnp.float32)[:, None] * rates[None, :]
    cosine = jnp.cos(angle)[:, None, :]
    sine = jnp.sin(angle)[:, None, :]
    first = values[..., :half]
    second_half = values[..., half:]
    return jnp.concatenate(
        [first * cosine - second_half * sine, second_half * cosine + first * sine], axis=-1
    )


def lookup(table_values, slot_index):
    matches = slot_index[:, None] == jnp.arange(table_values.shape[0], dtype=jnp.int32)[None, :]
    return jnp.sum(jnp.where(matches, table_values[None, :], 0), axis=1)


def block_owners(block_table, block_ids):
    matched = block_table[None, :, :] == block_ids[:, None, None]
    row_ids = jnp.arange(block_table.shape[0], dtype=jnp.int32)[None, :, None]
    col_ids = jnp.arange(block_table.shape[1], dtype=jnp.int32)[None, None, :]
    used = jnp.any(matched, axis=(1, 2)).astype(jnp.int32)
    owner = jnp.sum(jnp.where(matched, row_ids, 0), axis=(1, 2)).astype(jnp.int32)
    column = jnp.sum(jnp.where(matched, col_ids, 0), axis=(1, 2)).astype(jnp.int32)
    return used, owner, column


def merged_block(i, used_ref, owner_ref, column_ref, clen_ref, start_ref, fresh_ref, kc_ref, vc_ref, span):
    block_size, kv_width = kc_ref.shape[1], kc_ref.shape[2]
    start = start_ref[i]
    base = pl.multiple_of((start // 8) * 8, 8)
    window = fresh_ref[pl.ds(base, block_size + 8), :].astype(jnp.bfloat16)
    pick = lax.broadcasted_iota(jnp.int32, (block_size, block_size + 8), 1) == (
        lax.broadcasted_iota(jnp.int32, (block_size, block_size + 8), 0) + (start - base)
    )
    window = jnp.dot(pick.astype(jnp.bfloat16), window, preferred_element_type=jnp.float32)
    slot_pos = column_ref[i] * block_size + lax.broadcasted_iota(
        jnp.int32, (block_size, kv_width), 0
    )
    first_new = clen_ref[owner_ref[i]]
    fresh = (used_ref[i] == 1) & (slot_pos >= first_new) & (slot_pos < first_new + span)
    keys = jnp.where(fresh, window[:, :kv_width], kc_ref[i].astype(jnp.float32))
    values = jnp.where(fresh, window[:, kv_width:], vc_ref[i].astype(jnp.float32))
    return keys.astype(kc_ref.dtype), values.astype(vc_ref.dtype)


def attention_kernel(
    used_ref, owner_ref, column_ref, clen_ref, start_ref, req_ref, q_ref, fresh_ref, kc_ref, vc_ref,
    o_ref, nk_ref, nv_ref, m_sc, l_sc, acc_sc, *, q_heads, head_dim
):
    i = pl.program_id(0)
    r = req_ref[0]
    rows = q_ref.shape[0]
    block_size = kc_ref.shape[1]

    @pl.when(i == 0)
    def _init():
        m_sc[...] = jnp.full(m_sc.shape, NEG_FILL, jnp.float32)
        l_sc[...] = jnp.zeros(l_sc.shape, jnp.float32)
        acc_sc[...] = jnp.zeros(acc_sc.shape, jnp.float32)

    active = (used_ref[i] == 1) & (owner_ref[i] == r)

    @pl.when(jnp.logical_not(active))
    def _keep():
        nk_ref[i] = kc_ref[i]
        nv_ref[i] = vc_ref[i]

    @pl.when(active)
    def _work():
        keys, values = merged_block(
            i, used_ref, owner_ref, column_ref, clen_ref, start_ref, fresh_ref, kc_ref, vc_ref, rows
        )
        nk_ref[i] = keys
        nv_ref[i] = values
        query_pos = clen_ref[r] + lax.broadcasted_iota(jnp.int32, (rows, block_size), 0)
        key_pos = column_ref[i] * block_size + lax.broadcasted_iota(
            jnp.int32, (rows, block_size), 1
        )
        allowed = key_pos <= query_pos
        for g in range(q_heads):
            queries = q_ref[:, g * head_dim : (g + 1) * head_dim]
            score = lax.dot_general(
                queries, keys, (((1,), (1,)), ((), ())), preferred_element_type=jnp.float32
            ) / math.sqrt(head_dim)
            score = jnp.where(allowed, score, NEG_FILL)
            top = m_sc[g]
            new_top = jnp.maximum(top, jnp.max(score, axis=1, keepdims=True))
            weights = jnp.where(allowed, jnp.exp(score - new_top), 0.0)
            factor = jnp.exp(top - new_top)
            l_sc[g] = l_sc[g] * factor + jnp.sum(weights, axis=1, keepdims=True)
            acc_sc[g] = acc_sc[g] * factor + jnp.dot(
                weights.astype(jnp.bfloat16), values, preferred_element_type=jnp.float32
            )
            m_sc[g] = new_top

    @pl.when(i == pl.num_programs(0) - 1)
    def _finish():
        lane = lax.broadcasted_iota(jnp.int32, (rows, head_dim), 1)
        stats = jnp.zeros((rows, head_dim), jnp.float32)
        for g in range(q_heads):
            top = m_sc[g]
            valid = top > NEG_FILL / 2
            ref = jnp.where(valid, top.astype(jnp.bfloat16).astype(jnp.float32), NEG_FILL)
            factor = jnp.where(valid, jnp.exp(top - ref), 0.0)
            o_ref[:, g * head_dim : (g + 1) * head_dim] = (acc_sc[g] * factor).astype(o_ref.dtype)
            stats = jnp.where(lane == g, l_sc[g] * factor, stats)
            stats = jnp.where(lane == q_heads + g, ref, stats)
        o_ref[:, q_heads * head_dim :] = stats.astype(o_ref.dtype)


def block_meta(block_table, block_ids, cached_len, block_size, fresh_len):
    used, owner, column = block_owners(block_table, block_ids)
    start = block_size + column * block_size - cached_len[owner]
    start = jnp.clip(start, 0, fresh_len - block_size - 8).astype(jnp.int32)
    return used, owner, column, cached_len, start


def attend(queries, fresh_rows, keys, values, meta, request, span, q_heads, head_dim):
    n_blocks, block_size, kv_width = keys.shape
    q_width = q_heads * head_dim
    out_width = q_width + head_dim
    block = pl.BlockSpec(keys.shape, lambda i, *_: (0, 0, 0))
    grid_spec = pltpu.PrefetchScalarGridSpec(
        num_scalar_prefetch=6,
        grid=(n_blocks,),
        in_specs=[
            pl.BlockSpec((span, q_width), lambda i, *_: (0, 0)),
            pl.BlockSpec(fresh_rows.shape, lambda i, *_: (0, 0)),
            block,
            block,
        ],
        out_specs=[pl.BlockSpec((span, out_width), lambda i, *_: (0, 0)), block, block],
        scratch_shapes=[
            pltpu.VMEM((q_heads, span, head_dim), jnp.float32),
            pltpu.VMEM((q_heads, span, head_dim), jnp.float32),
            pltpu.VMEM((q_heads, span, head_dim), jnp.float32),
        ],
    )
    flops = n_blocks * span * q_heads * block_size * head_dim
    return pl.pallas_call(
        functools.partial(attention_kernel, q_heads=q_heads, head_dim=head_dim),
        grid_spec=grid_spec,
        out_shape=(
            jax.ShapeDtypeStruct((span, out_width), jnp.bfloat16),
            jax.ShapeDtypeStruct(keys.shape, keys.dtype),
            jax.ShapeDtypeStruct(values.shape, values.dtype),
        ),
        compiler_params=pltpu.CompilerParams(vmem_limit_bytes=48 * 1024 * 1024),
        cost_estimate=pl.CostEstimate(
            flops=flops,
            transcendentals=n_blocks * span * q_heads * block_size // 4,
            bytes_accessed=span * (q_width + out_width) * 2 + n_blocks * block_size * kv_width * 4,
        ),
    )(*meta, request, queries, fresh_rows, keys, values)


def combine_kernel(owner_ref, got_ref, bk_ref, bv_ref, out_ref, nk_ref, nv_ref, *, q_heads, head_dim):
    ring = got_ref.shape[0]
    q_width = q_heads * head_dim
    stats = [got_ref[s, :, q_width:].astype(jnp.float32) for s in range(ring)]
    for g in range(q_heads):
        tops = [st[:, q_heads + g : q_heads + g + 1] for st in stats]
        best = tops[0]
        for t in tops[1:]:
            best = jnp.maximum(best, t)
        weighted = jnp.zeros((out_ref.shape[0], head_dim), jnp.float32)
        total = jnp.zeros((out_ref.shape[0], 1), jnp.float32)
        for s in range(ring):
            factor = jnp.exp(tops[s] - best)
            part = got_ref[s, :, g * head_dim : (g + 1) * head_dim].astype(jnp.float32)
            weighted = weighted + part * factor
            total = total + stats[s][:, g : g + 1] * factor
        out_ref[:, g * head_dim : (g + 1) * head_dim] = (weighted / total).astype(out_ref.dtype)
    for b in range(nk_ref.shape[0]):
        nk_ref[b] = bk_ref[owner_ref[b], b]
        nv_ref[b] = bv_ref[owner_ref[b], b]


def combine(owner, got, back_k, back_v, q_heads, head_dim):
    ring, rows, _ = got.shape
    nb_dev = back_k.shape[1]

    def whole(x):
        return pl.BlockSpec(x.shape, lambda i, *_: (0,) * x.ndim)

    grid_spec = pltpu.PrefetchScalarGridSpec(
        num_scalar_prefetch=1,
        grid=(1,),
        in_specs=[whole(got), whole(back_k), whole(back_v)],
        out_specs=[
            pl.BlockSpec((rows, q_heads * head_dim), lambda i, *_: (0, 0)),
            pl.BlockSpec(back_k.shape[1:], lambda i, *_: (0, 0, 0)),
            pl.BlockSpec(back_v.shape[1:], lambda i, *_: (0, 0, 0)),
        ],
    )
    return pl.pallas_call(
        functools.partial(combine_kernel, q_heads=q_heads, head_dim=head_dim),
        grid_spec=grid_spec,
        out_shape=(
            jax.ShapeDtypeStruct((rows, q_heads * head_dim), jnp.bfloat16),
            jax.ShapeDtypeStruct(back_k.shape[1:], back_k.dtype),
            jax.ShapeDtypeStruct(back_v.shape[1:], back_v.dtype),
        ),
        compiler_params=pltpu.CompilerParams(vmem_limit_bytes=32 * 1024 * 1024),
    )(owner, got, back_k, back_v)


MESH = pl.DeviceIdType.MESH


def multi_exchange_kernel(*refs, specs):
    n_total = sum(s[4] for s in specs)
    srcs, dsts = refs[:n_total], refs[n_total : 2 * n_total]
    send_sem, recv_sem, own_sem = refs[2 * n_total :]
    here = {"kv": lax.axis_index("kv"), "blk": lax.axis_index("blk")}

    def device(axis, index):
        return (index, here["blk"]) if axis == "kv" else (here["kv"], index)

    groups = []
    arr0, sem0 = 0, 0
    for axis, m, stride, gather, n_arr in specs:
        pos = lax.rem(here[axis] // stride, m)
        base = here[axis] - pos * stride
        groups.append((axis, m, stride, gather, n_arr, pos, base, arr0, sem0))
        arr0 += n_arr
        sem0 += m * n_arr

    barrier = pltpu.get_barrier_semaphore()
    for axis, m, stride, gather, n_arr, pos, base, _, _ in groups:
        for k in range(1, m):
            peer = base + lax.rem(pos + k, m) * stride
            pl.semaphore_signal(barrier, inc=1, device_id=device(axis, peer), device_id_type=MESH)
    pl.semaphore_wait(barrier, sum(s[1] - 1 for s in specs))

    def chunk(src, j, m, gather):
        if gather:
            return src
        rows = src.shape[0] // m
        return src.at[pl.ds(pl.multiple_of(j * rows, rows), rows)]

    owns, copies = [], []
    for axis, m, stride, gather, n_arr, pos, base, a0, s0 in groups:
        for a in range(a0, a0 + n_arr):
            own = pltpu.make_async_copy(chunk(srcs[a], pos, m, gather), dsts[a].at[pos], own_sem.at[a])
            own.start()
            owns.append(own)
    for axis, m, stride, gather, n_arr, pos, base, a0, s0 in groups:
        for k in range(1, m):
            peer_pos = lax.rem(pos + k, m)
            for a in range(n_arr):
                copy = pltpu.make_async_remote_copy(
                    src_ref=chunk(srcs[a0 + a], peer_pos, m, gather),
                    dst_ref=dsts[a0 + a].at[pos],
                    send_sem=send_sem.at[s0 + k * n_arr + a],
                    recv_sem=recv_sem.at[s0 + k * n_arr + a],
                    device_id=device(axis, base + peer_pos * stride),
                    device_id_type=MESH,
                )
                copy.start()
                copies.append(copy)
    for own in owns:
        own.wait()
    c = 0
    for axis, m, stride, gather, n_arr, pos, base, a0, s0 in groups:
        for k in range(1, m):
            sender_pos = lax.rem(pos + m - k, m)
            for a in range(n_arr):
                incoming = pltpu.make_async_remote_copy(
                    src_ref=chunk(srcs[a0 + a], pos, m, gather),
                    dst_ref=dsts[a0 + a].at[sender_pos],
                    send_sem=send_sem.at[s0 + k * n_arr + a],
                    recv_sem=recv_sem.at[s0 + k * n_arr + a],
                    device_id=device(axis, base + sender_pos * stride),
                    device_id_type=MESH,
                )
                copies[c].wait_send()
                incoming.wait_recv()
                c += 1


def multi_exchange(groups, collective_id):
    specs, arrays, shapes = [], [], []
    for axis, m, stride, gather, arrs in groups:
        specs.append((axis, m, stride, gather, len(arrs)))
        for x in arrs:
            rows = x.shape[0] if gather else x.shape[0] // m
            arrays.append(x)
            shapes.append(jax.ShapeDtypeStruct((m, rows) + x.shape[1:], x.dtype))
    n_sem = sum(s[1] * s[4] for s in specs)
    return pl.pallas_call(
        functools.partial(multi_exchange_kernel, specs=tuple(specs)),
        out_shape=tuple(shapes),
        in_specs=[pl.BlockSpec(memory_space=pl.ANY)] * len(arrays),
        out_specs=tuple([pl.BlockSpec(memory_space=pl.ANY)] * len(arrays)),
        scratch_shapes=[
            pltpu.SemaphoreType.DMA((n_sem,)),
            pltpu.SemaphoreType.DMA((n_sem,)),
            pltpu.SemaphoreType.DMA((len(arrays),)),
        ],
        compiler_params=pltpu.CompilerParams(collective_id=collective_id, has_side_effects=True),
    )(*arrays)


def on_device(
    hidden_in,
    norm_gain,
    w_query,
    key_weight,
    value_weight,
    b_query,
    key_bias,
    value_bias,
    key_cache,
    value_cache,
    cached_len,
    block_table,
):
    tok_dev = hidden_in.shape[0]
    n_blk = lax.axis_size("blk")
    device = lax.axis_index("blk")
    requests = cached_len.shape[0]
    tokens = tok_dev * n_blk
    span = tokens // requests
    nb_dev, block_size, kv_width = key_cache.shape
    head_dim = HEAD_SIZE
    kv_heads = kv_width // head_dim
    q_heads = w_query.shape[1] // head_dim
    group_size = q_heads // kv_heads
    gain = norm_gain.astype(jnp.float32)
    ring = span // tok_dev
    cols = n_blk // ring
    position = device % ring
    kv_n = lax.axis_size("kv")
    (got_hidden,) = multi_exchange([("kv", kv_n, 1, True, [hidden_in])], 0)
    feat = hidden_in.shape[1]
    wide_in = got_hidden.astype(jnp.float32)
    scale = lax.rsqrt(jnp.mean(wide_in * wide_in, axis=(0, 2), keepdims=True) + EPS)
    normed = (wide_in * scale * gain.reshape(kv_n, 1, feat)).astype(jnp.bfloat16)

    def project(weight):
        return lax.dot_general(
            normed,
            weight.reshape(kv_n, feat, weight.shape[1]),
            (((0, 2), (0, 1)), ((), ())),
            preferred_element_type=jnp.float32,
        )

    q_lin = project(w_query)
    key_linear = project(key_weight)
    value_linear = project(value_weight)
    my_tokens = device * tok_dev + jnp.arange(tok_dev, dtype=jnp.int32)
    my_pos = lookup(cached_len, my_tokens // span) + my_tokens % span
    fresh_queries = apply_rotary(
        (q_lin + b_query.astype(jnp.float32)[None, :]).reshape(tok_dev, q_heads, head_dim),
        my_pos,
        head_dim,
    )
    fresh_queries = fresh_queries.astype(jnp.bfloat16).reshape(tok_dev, q_heads * head_dim)
    fresh_keys = apply_rotary(
        (key_linear + key_bias.astype(jnp.float32)[None, :]).reshape(tok_dev, kv_heads, head_dim),
        my_pos,
        head_dim,
    )
    fresh_keys = fresh_keys.astype(jnp.bfloat16).reshape(tok_dev, kv_width)
    fresh_values = (value_linear + value_bias.astype(jnp.float32)[None, :]).astype(jnp.bfloat16)
    q_width = q_heads * head_dim
    packed = jnp.concatenate([fresh_queries, fresh_keys, fresh_values], axis=1)
    ring_packed, col_keys, col_values = multi_exchange(
        [("blk", ring, 1, True, [packed]), ("blk", cols, ring, True, [key_cache, value_cache])], 1
    )
    ring_packed = ring_packed.reshape(span, packed.shape[1])
    fresh_rows = jnp.pad(
        ring_packed[:, q_width:].astype(jnp.float32), ((block_size, block_size + 8), (0, 0))
    )
    holders = jnp.arange(cols, dtype=jnp.int32) * ring + position
    col_ids = (holders[:, None] * nb_dev + jnp.arange(nb_dev, dtype=jnp.int32)[None, :]).reshape(-1)
    meta = block_meta(block_table, col_ids, cached_len, block_size, fresh_rows.shape[0])
    request = (device // ring).reshape(1).astype(jnp.int32)
    parts, merged_k, merged_v = attend(
        ring_packed,
        fresh_rows,
        col_keys.reshape(cols * nb_dev, block_size, kv_width),
        col_values.reshape(cols * nb_dev, block_size, kv_width),
        meta,
        request,
        span,
        q_heads,
        head_dim,
    )
    got, back_k, back_v = multi_exchange(
        [("blk", ring, 1, False, [parts]), ("blk", cols, ring, False, [merged_k, merged_v])], 2
    )
    local_ids = device * nb_dev + jnp.arange(nb_dev, dtype=jnp.int32)
    _, owner, _ = block_owners(block_table, local_ids)
    attn_out, new_k, new_v = combine(
        owner,
        got,
        back_k.reshape(cols, nb_dev, block_size, kv_width),
        back_v.reshape(cols, nb_dev, block_size, kv_width),
        q_heads,
        head_dim,
    )
    return (attn_out, new_k, new_v)


def solution(mesh):
    in_specs = (
        P("blk", "kv"),
        P(),
        P(None, "kv"),
        P(None, "kv"),
        P(None, "kv"),
        P("kv"),
        P("kv"),
        P("kv"),
        P("blk", None, "kv"),
        P("blk", None, "kv"),
        P(),
        P(),
    )
    out_specs = (P("blk", "kv"), P("blk", None, "kv"), P("blk", None, "kv"))
    return jax.shard_map(
        on_device, mesh=mesh, in_specs=in_specs, out_specs=out_specs, check_vma=False
    )
```

```python
import functools
import math

import jax
import jax.numpy as jnp
from jax import lax
from jax.experimental import pallas as pl
from jax.experimental.pallas import tpu as pltpu
from jax.sharding import PartitionSpec as P

HEAD_SIZE = 128


EPS = 1e-06
THETA = 1000000.0
NEG_FILL = -1e30


def apply_rotary(values, token_positions, head_dim):
    half = head_dim // 2
    rates = THETA ** (-(jnp.arange(half, dtype=jnp.float32) * 2.0) / head_dim)
    angle = token_positions.astype(jnp.float32)[:, None] * rates[None, :]
    cosine = jnp.cos(angle)[:, None, :]
    sine = jnp.sin(angle)[:, None, :]
    first = values[..., :half]
    second_half = values[..., half:]
    return jnp.concatenate(
        [first * cosine - second_half * sine, second_half * cosine + first * sine], axis=-1
    )


def lookup(table_values, slot_index):
    matches = slot_index[:, None] == jnp.arange(table_values.shape[0], dtype=jnp.int32)[None, :]
    return jnp.sum(jnp.where(matches, table_values[None, :], 0), axis=1)


def block_owners(block_table, block_ids):
    matched = block_table[None, :, :] == block_ids[:, None, None]
    row_ids = jnp.arange(block_table.shape[0], dtype=jnp.int32)[None, :, None]
    col_ids = jnp.arange(block_table.shape[1], dtype=jnp.int32)[None, None, :]
    used = jnp.any(matched, axis=(1, 2)).astype(jnp.int32)
    owner = jnp.sum(jnp.where(matched, row_ids, 0), axis=(1, 2)).astype(jnp.int32)
    column = jnp.sum(jnp.where(matched, col_ids, 0), axis=(1, 2)).astype(jnp.int32)
    return used, owner, column


def merged_block(i, used_ref, owner_ref, column_ref, clen_ref, start_ref, fresh_ref, kc_ref, vc_ref, span):
    block_size, kv_width = kc_ref.shape[1], kc_ref.shape[2]
    start = start_ref[i]
    base = pl.multiple_of((start // 8) * 8, 8)
    window = fresh_ref[pl.ds(base, block_size + 8), :].astype(jnp.bfloat16)
    pick = lax.broadcasted_iota(jnp.int32, (block_size, block_size + 8), 1) == (
        lax.broadcasted_iota(jnp.int32, (block_size, block_size + 8), 0) + (start - base)
    )
    window = jnp.dot(pick.astype(jnp.bfloat16), window, preferred_element_type=jnp.float32)
    slot_pos = column_ref[i] * block_size + lax.broadcasted_iota(
        jnp.int32, (block_size, kv_width), 0
    )
    first_new = clen_ref[owner_ref[i]]
    fresh = (used_ref[i] == 1) & (slot_pos >= first_new) & (slot_pos < first_new + span)
    keys = jnp.where(fresh, window[:, :kv_width], kc_ref[i].astype(jnp.float32))
    values = jnp.where(fresh, window[:, kv_width:], vc_ref[i].astype(jnp.float32))
    return keys.astype(kc_ref.dtype), values.astype(vc_ref.dtype)


def attention_kernel(
    used_ref, owner_ref, column_ref, clen_ref, start_ref, req_ref, q_ref, fresh_ref, kc_ref, vc_ref,
    o_ref, nk_ref, nv_ref, m_sc, l_sc, acc_sc, *, q_heads, head_dim
):
    r = req_ref[0]
    rows = q_ref.shape[0]
    block_size = kc_ref.shape[1]
    m_sc[...] = jnp.full(m_sc.shape, NEG_FILL, jnp.float32)
    l_sc[...] = jnp.zeros(l_sc.shape, jnp.float32)
    acc_sc[...] = jnp.zeros(acc_sc.shape, jnp.float32)

    def attend_heads(keys, values, allowed):
        for g in range(q_heads):
            queries = q_ref[:, g * head_dim : (g + 1) * head_dim]
            score = lax.dot_general(
                queries, keys, (((1,), (1,)), ((), ())), preferred_element_type=jnp.float32
            ) / math.sqrt(head_dim)
            if allowed is not None:
                score = jnp.where(allowed, score, NEG_FILL)
            top = m_sc[g]
            new_top = jnp.maximum(top, jnp.max(score, axis=1, keepdims=True))
            weights = jnp.exp(score - new_top)
            if allowed is not None:
                weights = jnp.where(allowed, weights, 0.0)
            factor = jnp.exp(top - new_top)
            l_sc[g] = l_sc[g] * factor + jnp.sum(weights, axis=1, keepdims=True)
            acc_sc[g] = acc_sc[g] * factor + jnp.dot(
                weights.astype(jnp.bfloat16), values, preferred_element_type=jnp.float32
            )
            m_sc[g] = new_top

    def visit(i, carry):
        active = (used_ref[i] == 1) & (owner_ref[i] == r)

        @pl.when(jnp.logical_not(active))
        def _keep():
            nk_ref[i] = kc_ref[i]
            nv_ref[i] = vc_ref[i]

        @pl.when(active)
        def _work():
            keys, values = merged_block(
                i, used_ref, owner_ref, column_ref, clen_ref, start_ref, fresh_ref, kc_ref, vc_ref, rows
            )
            nk_ref[i] = keys
            nv_ref[i] = values
            seen = column_ref[i] * block_size + block_size - 1 <= clen_ref[r]

            @pl.when(seen)
            def _all():
                attend_heads(keys, values, None)

            @pl.when(jnp.logical_not(seen))
            def _masked():
                query_pos = clen_ref[r] + lax.broadcasted_iota(jnp.int32, (rows, block_size), 0)
                key_pos = column_ref[i] * block_size + lax.broadcasted_iota(
                    jnp.int32, (rows, block_size), 1
                )
                attend_heads(keys, values, key_pos <= query_pos)

        return carry

    lax.fori_loop(0, kc_ref.shape[0], visit, 0)

    lane = lax.broadcasted_iota(jnp.int32, (rows, head_dim), 1)
    stats = jnp.zeros((rows, head_dim), jnp.float32)
    for g in range(q_heads):
        top = m_sc[g]
        valid = top > NEG_FILL / 2
        ref = jnp.where(valid, top.astype(jnp.bfloat16).astype(jnp.float32), NEG_FILL)
        factor = jnp.where(valid, jnp.exp(top - ref), 0.0)
        o_ref[:, g * head_dim : (g + 1) * head_dim] = (acc_sc[g] * factor).astype(o_ref.dtype)
        stats = jnp.where(lane == g, l_sc[g] * factor, stats)
        stats = jnp.where(lane == q_heads + g, ref, stats)
    o_ref[:, q_heads * head_dim :] = stats.astype(o_ref.dtype)


def block_meta(block_table, block_ids, cached_len, block_size, fresh_len):
    used, owner, column = block_owners(block_table, block_ids)
    start = block_size + column * block_size - cached_len[owner]
    start = jnp.clip(start, 0, fresh_len - block_size - 8).astype(jnp.int32)
    return used, owner, column, cached_len, start


def attend(queries, fresh_rows, keys, values, meta, request, span, q_heads, head_dim):
    n_blocks, block_size, kv_width = keys.shape
    q_width = q_heads * head_dim
    out_width = q_width + head_dim
    block = pl.BlockSpec(keys.shape, lambda i, *_: (0, 0, 0))
    grid_spec = pltpu.PrefetchScalarGridSpec(
        num_scalar_prefetch=6,
        grid=(1,),
        in_specs=[
            pl.BlockSpec((span, q_width), lambda i, *_: (0, 0)),
            pl.BlockSpec(fresh_rows.shape, lambda i, *_: (0, 0)),
            block,
            block,
        ],
        out_specs=[pl.BlockSpec((span, out_width), lambda i, *_: (0, 0)), block, block],
        scratch_shapes=[
            pltpu.VMEM((q_heads, span, head_dim), jnp.float32),
            pltpu.VMEM((q_heads, span, head_dim), jnp.float32),
            pltpu.VMEM((q_heads, span, head_dim), jnp.float32),
        ],
    )
    flops = n_blocks * span * q_heads * block_size * head_dim
    return pl.pallas_call(
        functools.partial(attention_kernel, q_heads=q_heads, head_dim=head_dim),
        grid_spec=grid_spec,
        out_shape=(
            jax.ShapeDtypeStruct((span, out_width), jnp.bfloat16),
            jax.ShapeDtypeStruct(keys.shape, keys.dtype),
            jax.ShapeDtypeStruct(values.shape, values.dtype),
        ),
        compiler_params=pltpu.CompilerParams(vmem_limit_bytes=48 * 1024 * 1024),
        cost_estimate=pl.CostEstimate(
            flops=flops,
            transcendentals=n_blocks * span * q_heads * block_size // 4,
            bytes_accessed=span * (q_width + out_width) * 2 + n_blocks * block_size * kv_width * 4,
        ),
    )(*meta, request, queries, fresh_rows, keys, values)


def combine_kernel(owner_ref, got_ref, bk_ref, bv_ref, out_ref, nk_ref, nv_ref, *, q_heads, head_dim):
    ring = got_ref.shape[0]
    q_width = q_heads * head_dim
    stats = [got_ref[s, :, q_width:].astype(jnp.float32) for s in range(ring)]
    for g in range(q_heads):
        tops = [st[:, q_heads + g : q_heads + g + 1] for st in stats]
        best = tops[0]
        for t in tops[1:]:
            best = jnp.maximum(best, t)
        weighted = jnp.zeros((out_ref.shape[0], head_dim), jnp.float32)
        total = jnp.zeros((out_ref.shape[0], 1), jnp.float32)
        for s in range(ring):
            factor = jnp.exp(tops[s] - best)
            part = got_ref[s, :, g * head_dim : (g + 1) * head_dim].astype(jnp.float32)
            weighted = weighted + part * factor
            total = total + stats[s][:, g : g + 1] * factor
        out_ref[:, g * head_dim : (g + 1) * head_dim] = (weighted / total).astype(out_ref.dtype)
    for b in range(nk_ref.shape[0]):
        nk_ref[b] = bk_ref[owner_ref[b], b]
        nv_ref[b] = bv_ref[owner_ref[b], b]


def combine(owner, got, back_k, back_v, q_heads, head_dim):
    ring, rows, _ = got.shape
    nb_dev = back_k.shape[1]

    def whole(x):
        return pl.BlockSpec(x.shape, lambda i, *_: (0,) * x.ndim)

    grid_spec = pltpu.PrefetchScalarGridSpec(
        num_scalar_prefetch=1,
        grid=(1,),
        in_specs=[whole(got), whole(back_k), whole(back_v)],
        out_specs=[
            pl.BlockSpec((rows, q_heads * head_dim), lambda i, *_: (0, 0)),
            pl.BlockSpec(back_k.shape[1:], lambda i, *_: (0, 0, 0)),
            pl.BlockSpec(back_v.shape[1:], lambda i, *_: (0, 0, 0)),
        ],
    )
    return pl.pallas_call(
        functools.partial(combine_kernel, q_heads=q_heads, head_dim=head_dim),
        grid_spec=grid_spec,
        out_shape=(
            jax.ShapeDtypeStruct((rows, q_heads * head_dim), jnp.bfloat16),
            jax.ShapeDtypeStruct(back_k.shape[1:], back_k.dtype),
            jax.ShapeDtypeStruct(back_v.shape[1:], back_v.dtype),
        ),
        compiler_params=pltpu.CompilerParams(vmem_limit_bytes=32 * 1024 * 1024),
    )(owner, got, back_k, back_v)


MESH = pl.DeviceIdType.MESH


def multi_exchange_kernel(*refs, specs):
    n_total = sum(s[4] for s in specs)
    srcs, dsts = refs[:n_total], refs[n_total : 2 * n_total]
    send_sem, recv_sem, own_sem = refs[2 * n_total :]
    here = {"kv": lax.axis_index("kv"), "blk": lax.axis_index("blk")}

    def device(axis, index):
        return (index, here["blk"]) if axis == "kv" else (here["kv"], index)

    groups = []
    arr0, sem0 = 0, 0
    for axis, m, stride, gather, n_arr in specs:
        pos = lax.rem(here[axis] // stride, m)
        base = here[axis] - pos * stride
        groups.append((axis, m, stride, gather, n_arr, pos, base, arr0, sem0))
        arr0 += n_arr
        sem0 += m * n_arr

    barrier = pltpu.get_barrier_semaphore()
    for axis, m, stride, gather, n_arr, pos, base, _, _ in groups:
        for k in range(1, m):
            peer = base + lax.rem(pos + k, m) * stride
            pl.semaphore_signal(barrier, inc=1, device_id=device(axis, peer), device_id_type=MESH)
    pl.semaphore_wait(barrier, sum(s[1] - 1 for s in specs))

    def chunk(src, j, m, gather):
        if gather:
            return src
        rows = src.shape[0] // m
        return src.at[pl.ds(pl.multiple_of(j * rows, rows), rows)]

    owns, copies = [], []
    for axis, m, stride, gather, n_arr, pos, base, a0, s0 in groups:
        for a in range(a0, a0 + n_arr):
            own = pltpu.make_async_copy(chunk(srcs[a], pos, m, gather), dsts[a].at[pos], own_sem.at[a])
            own.start()
            owns.append(own)
    for axis, m, stride, gather, n_arr, pos, base, a0, s0 in groups:
        for k in range(1, m):
            peer_pos = lax.rem(pos + k, m)
            for a in range(n_arr):
                copy = pltpu.make_async_remote_copy(
                    src_ref=chunk(srcs[a0 + a], peer_pos, m, gather),
                    dst_ref=dsts[a0 + a].at[pos],
                    send_sem=send_sem.at[s0 + k * n_arr + a],
                    recv_sem=recv_sem.at[s0 + k * n_arr + a],
                    device_id=device(axis, base + peer_pos * stride),
                    device_id_type=MESH,
                )
                copy.start()
                copies.append(copy)
    for own in owns:
        own.wait()
    c = 0
    for axis, m, stride, gather, n_arr, pos, base, a0, s0 in groups:
        for k in range(1, m):
            sender_pos = lax.rem(pos + m - k, m)
            for a in range(n_arr):
                incoming = pltpu.make_async_remote_copy(
                    src_ref=chunk(srcs[a0 + a], pos, m, gather),
                    dst_ref=dsts[a0 + a].at[sender_pos],
                    send_sem=send_sem.at[s0 + k * n_arr + a],
                    recv_sem=recv_sem.at[s0 + k * n_arr + a],
                    device_id=device(axis, base + sender_pos * stride),
                    device_id_type=MESH,
                )
                copies[c].wait_send()
                incoming.wait_recv()
                c += 1


def multi_exchange(groups, collective_id):
    specs, arrays, shapes = [], [], []
    for axis, m, stride, gather, arrs in groups:
        specs.append((axis, m, stride, gather, len(arrs)))
        for x in arrs:
            rows = x.shape[0] if gather else x.shape[0] // m
            arrays.append(x)
            shapes.append(jax.ShapeDtypeStruct((m, rows) + x.shape[1:], x.dtype))
    n_sem = sum(s[1] * s[4] for s in specs)
    return pl.pallas_call(
        functools.partial(multi_exchange_kernel, specs=tuple(specs)),
        out_shape=tuple(shapes),
        in_specs=[pl.BlockSpec(memory_space=pl.ANY)] * len(arrays),
        out_specs=tuple([pl.BlockSpec(memory_space=pl.ANY)] * len(arrays)),
        scratch_shapes=[
            pltpu.SemaphoreType.DMA((n_sem,)),
            pltpu.SemaphoreType.DMA((n_sem,)),
            pltpu.SemaphoreType.DMA((len(arrays),)),
        ],
        compiler_params=pltpu.CompilerParams(collective_id=collective_id, has_side_effects=True),
    )(*arrays)


def on_device(
    hidden_in,
    norm_gain,
    w_query,
    key_weight,
    value_weight,
    b_query,
    key_bias,
    value_bias,
    key_cache,
    value_cache,
    cached_len,
    block_table,
):
    tok_dev = hidden_in.shape[0]
    n_blk = lax.axis_size("blk")
    device = lax.axis_index("blk")
    requests = cached_len.shape[0]
    tokens = tok_dev * n_blk
    span = tokens // requests
    nb_dev, block_size, kv_width = key_cache.shape
    head_dim = HEAD_SIZE
    kv_heads = kv_width // head_dim
    q_heads = w_query.shape[1] // head_dim
    group_size = q_heads // kv_heads
    gain = norm_gain.astype(jnp.float32)
    ring = span // tok_dev
    cols = n_blk // ring
    position = device % ring
    kv_n = lax.axis_size("kv")
    (got_hidden,) = multi_exchange([("kv", kv_n, 1, True, [hidden_in])], 0)
    feat = hidden_in.shape[1]
    wide_in = got_hidden.astype(jnp.float32)
    scale = lax.rsqrt(jnp.mean(wide_in * wide_in, axis=(0, 2), keepdims=True) + EPS)
    normed = (wide_in * scale * gain.reshape(kv_n, 1, feat)).astype(jnp.bfloat16)

    def project(weight):
        return lax.dot_general(
            normed,
            weight.reshape(kv_n, feat, weight.shape[1]),
            (((0, 2), (0, 1)), ((), ())),
            preferred_element_type=jnp.float32,
        )

    q_lin = project(w_query)
    key_linear = project(key_weight)
    value_linear = project(value_weight)
    my_tokens = device * tok_dev + jnp.arange(tok_dev, dtype=jnp.int32)
    my_pos = lookup(cached_len, my_tokens // span) + my_tokens % span
    fresh_queries = apply_rotary(
        (q_lin + b_query.astype(jnp.float32)[None, :]).reshape(tok_dev, q_heads, head_dim),
        my_pos,
        head_dim,
    )
    fresh_queries = fresh_queries.astype(jnp.bfloat16).reshape(tok_dev, q_heads * head_dim)
    fresh_keys = apply_rotary(
        (key_linear + key_bias.astype(jnp.float32)[None, :]).reshape(tok_dev, kv_heads, head_dim),
        my_pos,
        head_dim,
    )
    fresh_keys = fresh_keys.astype(jnp.bfloat16).reshape(tok_dev, kv_width)
    fresh_values = (value_linear + value_bias.astype(jnp.float32)[None, :]).astype(jnp.bfloat16)
    q_width = q_heads * head_dim
    packed = jnp.concatenate([fresh_queries, fresh_keys, fresh_values], axis=1)
    ring_packed, col_keys, col_values = multi_exchange(
        [("blk", ring, 1, True, [packed]), ("blk", cols, ring, True, [key_cache, value_cache])], 1
    )
    ring_packed = ring_packed.reshape(span, packed.shape[1])
    fresh_rows = jnp.pad(
        ring_packed[:, q_width:].astype(jnp.float32), ((block_size, block_size + 8), (0, 0))
    )
    holders = jnp.arange(cols, dtype=jnp.int32) * ring + position
    col_ids = (holders[:, None] * nb_dev + jnp.arange(nb_dev, dtype=jnp.int32)[None, :]).reshape(-1)
    meta = block_meta(block_table, col_ids, cached_len, block_size, fresh_rows.shape[0])
    request = (device // ring).reshape(1).astype(jnp.int32)
    parts, merged_k, merged_v = attend(
        ring_packed,
        fresh_rows,
        col_keys.reshape(cols * nb_dev, block_size, kv_width),
        col_values.reshape(cols * nb_dev, block_size, kv_width),
        meta,
        request,
        span,
        q_heads,
        head_dim,
    )
    got, back_k, back_v = multi_exchange(
        [("blk", ring, 1, False, [parts]), ("blk", cols, ring, False, [merged_k, merged_v])], 2
    )
    local_ids = device * nb_dev + jnp.arange(nb_dev, dtype=jnp.int32)
    _, owner, _ = block_owners(block_table, local_ids)
    attn_out, new_k, new_v = combine(
        owner,
        got,
        back_k.reshape(cols, nb_dev, block_size, kv_width),
        back_v.reshape(cols, nb_dev, block_size, kv_width),
        q_heads,
        head_dim,
    )
    return (attn_out, new_k, new_v)


def solution(mesh):
    in_specs = (
        P("blk", "kv"),
        P(),
        P(None, "kv"),
        P(None, "kv"),
        P(None, "kv"),
        P("kv"),
        P("kv"),
        P("kv"),
        P("blk", None, "kv"),
        P("blk", None, "kv"),
        P(),
        P(),
    )
    out_specs = (P("blk", "kv"), P("blk", None, "kv"), P("blk", None, "kv"))
    return jax.shard_map(
        on_device, mesh=mesh, in_specs=in_specs, out_specs=out_specs, check_vma=False
    )
```

```python
import functools
import math

import jax
import jax.numpy as jnp
from jax import lax
from jax.experimental import pallas as pl
from jax.experimental.pallas import tpu as pltpu
from jax.sharding import PartitionSpec as P

HEAD_SIZE = 128


EPS = 1e-06
THETA = 1000000.0
NEG_FILL = -1e30


def apply_rotary(values, token_positions, head_dim):
    half = head_dim // 2
    rates = THETA ** (-(jnp.arange(half, dtype=jnp.float32) * 2.0) / head_dim)
    angle = token_positions.astype(jnp.float32)[:, None] * rates[None, :]
    cosine = jnp.cos(angle)[:, None, :]
    sine = jnp.sin(angle)[:, None, :]
    first = values[..., :half]
    second_half = values[..., half:]
    return jnp.concatenate(
        [first * cosine - second_half * sine, second_half * cosine + first * sine], axis=-1
    )


def lookup(table_values, slot_index):
    matches = slot_index[:, None] == jnp.arange(table_values.shape[0], dtype=jnp.int32)[None, :]
    return jnp.sum(jnp.where(matches, table_values[None, :], 0), axis=1)


def block_owners(block_table, block_ids):
    matched = block_table[None, :, :] == block_ids[:, None, None]
    row_ids = jnp.arange(block_table.shape[0], dtype=jnp.int32)[None, :, None]
    col_ids = jnp.arange(block_table.shape[1], dtype=jnp.int32)[None, None, :]
    used = jnp.any(matched, axis=(1, 2)).astype(jnp.int32)
    owner = jnp.sum(jnp.where(matched, row_ids, 0), axis=(1, 2)).astype(jnp.int32)
    column = jnp.sum(jnp.where(matched, col_ids, 0), axis=(1, 2)).astype(jnp.int32)
    return used, owner, column


def merged_block(i, used_ref, owner_ref, column_ref, clen_ref, start_ref, fresh_ref, kc_ref, vc_ref, span):
    block_size, kv_width = kc_ref.shape[1], kc_ref.shape[2]
    start = start_ref[i]
    base = pl.multiple_of((start // 8) * 8, 8)
    window = fresh_ref[pl.ds(base, block_size + 8), :].astype(jnp.bfloat16)
    pick = lax.broadcasted_iota(jnp.int32, (block_size, block_size + 8), 1) == (
        lax.broadcasted_iota(jnp.int32, (block_size, block_size + 8), 0) + (start - base)
    )
    window = jnp.dot(pick.astype(jnp.bfloat16), window, preferred_element_type=jnp.float32)
    slot_pos = column_ref[i] * block_size + lax.broadcasted_iota(
        jnp.int32, (block_size, kv_width), 0
    )
    first_new = clen_ref[owner_ref[i]]
    fresh = (used_ref[i] == 1) & (slot_pos >= first_new) & (slot_pos < first_new + span)
    keys = jnp.where(fresh, window[:, :kv_width], kc_ref[i].astype(jnp.float32))
    values = jnp.where(fresh, window[:, kv_width:], vc_ref[i].astype(jnp.float32))
    return keys.astype(kc_ref.dtype), values.astype(vc_ref.dtype)


def attention_kernel(
    used_ref, owner_ref, column_ref, clen_ref, start_ref, req_ref, q_ref, fresh_ref, kc_ref, vc_ref,
    o_ref, nk_ref, nv_ref, m_sc, l_sc, acc_sc, *, q_heads, head_dim
):
    r = req_ref[0]
    rows = q_ref.shape[0]
    block_size = kc_ref.shape[1]
    m_sc[...] = jnp.full(m_sc.shape, NEG_FILL, jnp.float32)
    l_sc[...] = jnp.zeros(l_sc.shape, jnp.float32)
    acc_sc[...] = jnp.zeros(acc_sc.shape, jnp.float32)

    def attend_heads(keys, values, allowed):
        for g in range(q_heads):
            queries = q_ref[:, g * head_dim : (g + 1) * head_dim]
            score = lax.dot_general(
                queries, keys, (((1,), (1,)), ((), ())), preferred_element_type=jnp.float32
            ) / math.sqrt(head_dim)
            if allowed is not None:
                score = jnp.where(allowed, score, NEG_FILL)
            top = m_sc[g]
            new_top = jnp.maximum(top, jnp.max(score, axis=1, keepdims=True))
            weights = jnp.exp(score - new_top)
            if allowed is not None:
                weights = jnp.where(allowed, weights, 0.0)
            factor = jnp.exp(top - new_top)
            l_sc[g] = l_sc[g] * factor + jnp.sum(weights, axis=1, keepdims=True)
            acc_sc[g] = acc_sc[g] * factor + jnp.dot(
                weights.astype(jnp.bfloat16), values, preferred_element_type=jnp.float32
            )
            m_sc[g] = new_top

    def visit(i, carry):
        active = (used_ref[i] == 1) & (owner_ref[i] == r)

        @pl.when(jnp.logical_not(active))
        def _keep():
            nk_ref[i] = kc_ref[i]
            nv_ref[i] = vc_ref[i]

        @pl.when(active)
        def _work():
            keys, values = merged_block(
                i, used_ref, owner_ref, column_ref, clen_ref, start_ref, fresh_ref, kc_ref, vc_ref, rows
            )
            nk_ref[i] = keys
            nv_ref[i] = values
            seen = column_ref[i] * block_size + block_size - 1 <= clen_ref[r]

            @pl.when(seen)
            def _all():
                attend_heads(keys, values, None)

            @pl.when(jnp.logical_not(seen))
            def _masked():
                query_pos = clen_ref[r] + lax.broadcasted_iota(jnp.int32, (rows, block_size), 0)
                key_pos = column_ref[i] * block_size + lax.broadcasted_iota(
                    jnp.int32, (rows, block_size), 1
                )
                attend_heads(keys, values, key_pos <= query_pos)

        return carry

    lax.fori_loop(0, kc_ref.shape[0], visit, 0)

    lane = lax.broadcasted_iota(jnp.int32, (rows, head_dim), 1)
    stats = jnp.zeros((rows, head_dim), jnp.float32)
    for g in range(q_heads):
        top = m_sc[g]
        valid = top > NEG_FILL / 2
        ref = jnp.where(valid, top.astype(jnp.bfloat16).astype(jnp.float32), NEG_FILL)
        factor = jnp.where(valid, jnp.exp(top - ref), 0.0)
        o_ref[:, g * head_dim : (g + 1) * head_dim] = (acc_sc[g] * factor).astype(o_ref.dtype)
        stats = jnp.where(lane == g, l_sc[g] * factor, stats)
        stats = jnp.where(lane == q_heads + g, ref, stats)
    o_ref[:, q_heads * head_dim :] = stats.astype(o_ref.dtype)


def block_meta(block_table, block_ids, cached_len, block_size, fresh_len):
    used, owner, column = block_owners(block_table, block_ids)
    start = block_size + column * block_size - cached_len[owner]
    start = jnp.clip(start, 0, fresh_len - block_size - 8).astype(jnp.int32)
    return used, owner, column, cached_len, start


def attend(queries, fresh_rows, keys, values, meta, request, span, q_heads, head_dim):
    n_blocks, block_size, kv_width = keys.shape
    q_width = q_heads * head_dim
    out_width = q_width + head_dim
    block = pl.BlockSpec(keys.shape, lambda i, *_: (0, 0, 0))
    grid_spec = pltpu.PrefetchScalarGridSpec(
        num_scalar_prefetch=6,
        grid=(1,),
        in_specs=[
            pl.BlockSpec((span, q_width), lambda i, *_: (0, 0)),
            pl.BlockSpec(fresh_rows.shape, lambda i, *_: (0, 0)),
            block,
            block,
        ],
        out_specs=[pl.BlockSpec((span, out_width), lambda i, *_: (0, 0)), block, block],
        scratch_shapes=[
            pltpu.VMEM((q_heads, span, head_dim), jnp.float32),
            pltpu.VMEM((q_heads, span, head_dim), jnp.float32),
            pltpu.VMEM((q_heads, span, head_dim), jnp.float32),
        ],
    )
    flops = n_blocks * span * q_heads * block_size * head_dim
    return pl.pallas_call(
        functools.partial(attention_kernel, q_heads=q_heads, head_dim=head_dim),
        grid_spec=grid_spec,
        out_shape=(
            jax.ShapeDtypeStruct((span, out_width), jnp.bfloat16),
            jax.ShapeDtypeStruct(keys.shape, keys.dtype),
            jax.ShapeDtypeStruct(values.shape, values.dtype),
        ),
        compiler_params=pltpu.CompilerParams(vmem_limit_bytes=48 * 1024 * 1024),
        cost_estimate=pl.CostEstimate(
            flops=flops,
            transcendentals=n_blocks * span * q_heads * block_size // 4,
            bytes_accessed=span * (q_width + out_width) * 2 + n_blocks * block_size * kv_width * 4,
        ),
    )(*meta, request, queries, fresh_rows, keys, values)


def combine_kernel(owner_ref, got_ref, bk_ref, bv_ref, out_ref, nk_ref, nv_ref, *, q_heads, head_dim):
    ring = got_ref.shape[0]
    q_width = q_heads * head_dim
    stats = [got_ref[s, :, q_width:].astype(jnp.float32) for s in range(ring)]
    for g in range(q_heads):
        tops = [st[:, q_heads + g : q_heads + g + 1] for st in stats]
        best = tops[0]
        for t in tops[1:]:
            best = jnp.maximum(best, t)
        weighted = jnp.zeros((out_ref.shape[0], head_dim), jnp.float32)
        total = jnp.zeros((out_ref.shape[0], 1), jnp.float32)
        for s in range(ring):
            factor = jnp.exp(tops[s] - best)
            part = got_ref[s, :, g * head_dim : (g + 1) * head_dim].astype(jnp.float32)
            weighted = weighted + part * factor
            total = total + stats[s][:, g : g + 1] * factor
        out_ref[:, g * head_dim : (g + 1) * head_dim] = (weighted / total).astype(out_ref.dtype)
    for b in range(nk_ref.shape[0]):
        nk_ref[b] = bk_ref[owner_ref[b], b]
        nv_ref[b] = bv_ref[owner_ref[b], b]


def combine(owner, got, back_k, back_v, q_heads, head_dim):
    ring, rows, _ = got.shape
    nb_dev = back_k.shape[1]

    def whole(x):
        return pl.BlockSpec(x.shape, lambda i, *_: (0,) * x.ndim)

    grid_spec = pltpu.PrefetchScalarGridSpec(
        num_scalar_prefetch=1,
        grid=(1,),
        in_specs=[whole(got), whole(back_k), whole(back_v)],
        out_specs=[
            pl.BlockSpec((rows, q_heads * head_dim), lambda i, *_: (0, 0)),
            pl.BlockSpec(back_k.shape[1:], lambda i, *_: (0, 0, 0)),
            pl.BlockSpec(back_v.shape[1:], lambda i, *_: (0, 0, 0)),
        ],
    )
    return pl.pallas_call(
        functools.partial(combine_kernel, q_heads=q_heads, head_dim=head_dim),
        grid_spec=grid_spec,
        out_shape=(
            jax.ShapeDtypeStruct((rows, q_heads * head_dim), jnp.bfloat16),
            jax.ShapeDtypeStruct(back_k.shape[1:], back_k.dtype),
            jax.ShapeDtypeStruct(back_v.shape[1:], back_v.dtype),
        ),
        compiler_params=pltpu.CompilerParams(vmem_limit_bytes=32 * 1024 * 1024),
    )(owner, got, back_k, back_v)


MESH = pl.DeviceIdType.MESH


def forward_gather(src, dst, send_sem, recv_sem, own_sem, right, left, pos, m):
    streams = [(right, m // 2, 0, -1), (left, (m - 1) // 2, m // 2, 1)]
    own = pltpu.make_async_copy(src, dst.at[pos], own_sem)
    own.start()

    def hop(target, source, origin, sem):
        return pltpu.make_async_remote_copy(
            src_ref=source, dst_ref=dst.at[origin], send_sem=send_sem.at[sem],
            recv_sem=recv_sem.at[sem], device_id=target, device_id_type=MESH,
        )

    sent = []
    for target, n, s0, side in streams:
        if n > 0:
            first = hop(target, src, pos, s0)
            first.start()
            sent.append(first)
    own.wait()
    for k in range(1, m // 2):
        for target, n, s0, side in streams:
            if k < n:
                origin = lax.rem(pos + m + side * k, m)
                hop(target, src, origin, s0 + k - 1).wait_recv()
                nxt = hop(target, dst.at[origin], origin, s0 + k)
                nxt.start()
                sent.append(nxt)
    for target, n, s0, side in streams:
        if n > 0:
            origin = lax.rem(pos + m + side * n, m)
            hop(target, src, origin, s0 + n - 1).wait_recv()
    for copy in sent:
        copy.wait_send()


def multi_exchange_kernel(*refs, specs):
    n_total = sum(s[4] for s in specs)
    srcs, dsts = refs[:n_total], refs[n_total : 2 * n_total]
    send_sem, recv_sem, own_sem = refs[2 * n_total :]
    here = {"kv": lax.axis_index("kv"), "blk": lax.axis_index("blk")}

    def device(axis, index):
        return (index, here["blk"]) if axis == "kv" else (here["kv"], index)

    groups, forwards = [], []
    arr0, sem0 = 0, 0
    n_greet = 0
    barrier = pltpu.get_barrier_semaphore()
    for axis, m, stride, gather, n_arr, forward in specs:
        pos = lax.rem(here[axis] // stride, m)
        base = here[axis] - pos * stride
        if forward:
            right = device(axis, base + lax.rem(pos + 1, m) * stride)
            left = device(axis, base + lax.rem(pos + m - 1, m) * stride)
            forwards.append((right, left, pos, m, arr0, sem0))
            for peer in [right, left][: min(2, m - 1)]:
                pl.semaphore_signal(barrier, inc=1, device_id=peer, device_id_type=MESH)
            n_greet += min(2, m - 1)
        else:
            groups.append((axis, m, stride, gather, n_arr, pos, base, arr0, sem0))
            for k in range(1, m):
                peer = base + lax.rem(pos + k, m) * stride
                pl.semaphore_signal(barrier, inc=1, device_id=device(axis, peer), device_id_type=MESH)
            n_greet += m - 1
        arr0 += n_arr
        sem0 += m * n_arr
    pl.semaphore_wait(barrier, n_greet)

    def chunk(src, j, m, gather):
        if gather:
            return src
        rows = src.shape[0] // m
        return src.at[pl.ds(pl.multiple_of(j * rows, rows), rows)]

    owns, copies = [], []
    for axis, m, stride, gather, n_arr, pos, base, a0, s0 in groups:
        for a in range(a0, a0 + n_arr):
            own = pltpu.make_async_copy(chunk(srcs[a], pos, m, gather), dsts[a].at[pos], own_sem.at[a])
            own.start()
            owns.append(own)
    for axis, m, stride, gather, n_arr, pos, base, a0, s0 in groups:
        for k in range(1, m):
            peer_pos = lax.rem(pos + k, m)
            for a in range(n_arr):
                copy = pltpu.make_async_remote_copy(
                    src_ref=chunk(srcs[a0 + a], peer_pos, m, gather),
                    dst_ref=dsts[a0 + a].at[pos],
                    send_sem=send_sem.at[s0 + k * n_arr + a],
                    recv_sem=recv_sem.at[s0 + k * n_arr + a],
                    device_id=device(axis, base + peer_pos * stride),
                    device_id_type=MESH,
                )
                copy.start()
                copies.append(copy)
    for right, left, pos, m, a0, s0 in forwards:
        forward_gather(
            srcs[a0], dsts[a0], send_sem.at[pl.ds(s0, m)], recv_sem.at[pl.ds(s0, m)],
            own_sem.at[a0], right, left, pos, m,
        )
    for own in owns:
        own.wait()
    c = 0
    for axis, m, stride, gather, n_arr, pos, base, a0, s0 in groups:
        for k in range(1, m):
            sender_pos = lax.rem(pos + m - k, m)
            for a in range(n_arr):
                incoming = pltpu.make_async_remote_copy(
                    src_ref=chunk(srcs[a0 + a], pos, m, gather),
                    dst_ref=dsts[a0 + a].at[sender_pos],
                    send_sem=send_sem.at[s0 + k * n_arr + a],
                    recv_sem=recv_sem.at[s0 + k * n_arr + a],
                    device_id=device(axis, base + sender_pos * stride),
                    device_id_type=MESH,
                )
                copies[c].wait_send()
                incoming.wait_recv()
                c += 1


def multi_exchange(groups, collective_id):
    specs, arrays, shapes = [], [], []
    for group in groups:
        axis, m, stride, gather, arrs = group[:5]
        forward = len(group) > 5 and group[5]
        specs.append((axis, m, stride, gather, len(arrs), forward))
        for x in arrs:
            rows = x.shape[0] if gather else x.shape[0] // m
            arrays.append(x)
            shapes.append(jax.ShapeDtypeStruct((m, rows) + x.shape[1:], x.dtype))
    n_sem = sum(s[1] * s[4] for s in specs)
    return pl.pallas_call(
        functools.partial(multi_exchange_kernel, specs=tuple(specs)),
        out_shape=tuple(shapes),
        in_specs=[pl.BlockSpec(memory_space=pl.ANY)] * len(arrays),
        out_specs=tuple([pl.BlockSpec(memory_space=pl.ANY)] * len(arrays)),
        scratch_shapes=[
            pltpu.SemaphoreType.DMA((n_sem,)),
            pltpu.SemaphoreType.DMA((n_sem,)),
            pltpu.SemaphoreType.DMA((len(arrays),)),
        ],
        compiler_params=pltpu.CompilerParams(collective_id=collective_id, has_side_effects=True),
    )(*arrays)


def on_device(
    hidden_in,
    norm_gain,
    w_query,
    key_weight,
    value_weight,
    b_query,
    key_bias,
    value_bias,
    key_cache,
    value_cache,
    cached_len,
    block_table,
):
    tok_dev = hidden_in.shape[0]
    n_blk = lax.axis_size("blk")
    device = lax.axis_index("blk")
    requests = cached_len.shape[0]
    tokens = tok_dev * n_blk
    span = tokens // requests
    nb_dev, block_size, kv_width = key_cache.shape
    head_dim = HEAD_SIZE
    kv_heads = kv_width // head_dim
    q_heads = w_query.shape[1] // head_dim
    group_size = q_heads // kv_heads
    gain = norm_gain.astype(jnp.float32)
    ring = span // tok_dev
    cols = n_blk // ring
    position = device % ring
    kv_n = lax.axis_size("kv")
    (got_hidden,) = multi_exchange([("kv", kv_n, 1, True, [hidden_in])], 0)
    feat = hidden_in.shape[1]
    wide_in = got_hidden.astype(jnp.float32)
    scale = lax.rsqrt(jnp.mean(wide_in * wide_in, axis=(0, 2), keepdims=True) + EPS)
    normed = (wide_in * scale * gain.reshape(kv_n, 1, feat)).astype(jnp.bfloat16)

    def project(weight):
        return lax.dot_general(
            normed,
            weight.reshape(kv_n, feat, weight.shape[1]),
            (((0, 2), (0, 1)), ((), ())),
            preferred_element_type=jnp.float32,
        )

    q_lin = project(w_query)
    key_linear = project(key_weight)
    value_linear = project(value_weight)
    my_tokens = device * tok_dev + jnp.arange(tok_dev, dtype=jnp.int32)
    my_pos = lookup(cached_len, my_tokens // span) + my_tokens % span
    fresh_queries = apply_rotary(
        (q_lin + b_query.astype(jnp.float32)[None, :]).reshape(tok_dev, q_heads, head_dim),
        my_pos,
        head_dim,
    )
    fresh_queries = fresh_queries.astype(jnp.bfloat16).reshape(tok_dev, q_heads * head_dim)
    fresh_keys = apply_rotary(
        (key_linear + key_bias.astype(jnp.float32)[None, :]).reshape(tok_dev, kv_heads, head_dim),
        my_pos,
        head_dim,
    )
    fresh_keys = fresh_keys.astype(jnp.bfloat16).reshape(tok_dev, kv_width)
    fresh_values = (value_linear + value_bias.astype(jnp.float32)[None, :]).astype(jnp.bfloat16)
    q_width = q_heads * head_dim
    packed = jnp.concatenate([fresh_queries, fresh_keys, fresh_values], axis=1)
    ring_packed, col_keys, col_values = multi_exchange(
        [("blk", ring, 1, True, [packed], True), ("blk", cols, ring, True, [key_cache, value_cache])], 1
    )
    ring_packed = ring_packed.reshape(span, packed.shape[1])
    fresh_rows = jnp.pad(
        ring_packed[:, q_width:].astype(jnp.float32), ((block_size, block_size + 8), (0, 0))
    )
    holders = jnp.arange(cols, dtype=jnp.int32) * ring + position
    col_ids = (holders[:, None] * nb_dev + jnp.arange(nb_dev, dtype=jnp.int32)[None, :]).reshape(-1)
    meta = block_meta(block_table, col_ids, cached_len, block_size, fresh_rows.shape[0])
    request = (device // ring).reshape(1).astype(jnp.int32)
    parts, merged_k, merged_v = attend(
        ring_packed,
        fresh_rows,
        col_keys.reshape(cols * nb_dev, block_size, kv_width),
        col_values.reshape(cols * nb_dev, block_size, kv_width),
        meta,
        request,
        span,
        q_heads,
        head_dim,
    )
    got, back_k, back_v = multi_exchange(
        [("blk", ring, 1, False, [parts]), ("blk", cols, ring, False, [merged_k, merged_v])], 2
    )
    local_ids = device * nb_dev + jnp.arange(nb_dev, dtype=jnp.int32)
    _, owner, _ = block_owners(block_table, local_ids)
    attn_out, new_k, new_v = combine(
        owner,
        got,
        back_k.reshape(cols, nb_dev, block_size, kv_width),
        back_v.reshape(cols, nb_dev, block_size, kv_width),
        q_heads,
        head_dim,
    )
    return (attn_out, new_k, new_v)


def solution(mesh):
    in_specs = (
        P("blk", "kv"),
        P(),
        P(None, "kv"),
        P(None, "kv"),
        P(None, "kv"),
        P("kv"),
        P("kv"),
        P("kv"),
        P("blk", None, "kv"),
        P("blk", None, "kv"),
        P(),
        P(),
    )
    out_specs = (P("blk", "kv"), P("blk", None, "kv"), P("blk", None, "kv"))
    return jax.shard_map(
        on_device, mesh=mesh, in_specs=in_specs, out_specs=out_specs, check_vma=False
    )
```

```python
import functools
import math

import jax
import jax.numpy as jnp
from jax import lax
from jax.experimental import pallas as pl
from jax.experimental.pallas import tpu as pltpu
from jax.sharding import PartitionSpec as P

HEAD_SIZE = 128


EPS = 1e-06
THETA = 1000000.0
NEG_FILL = -1e30


def apply_rotary(values, token_positions, head_dim):
    half = head_dim // 2
    rates = THETA ** (-(jnp.arange(half, dtype=jnp.float32) * 2.0) / head_dim)
    angle = token_positions.astype(jnp.float32)[:, None] * rates[None, :]
    cosine = jnp.cos(angle)[:, None, :]
    sine = jnp.sin(angle)[:, None, :]
    first = values[..., :half]
    second_half = values[..., half:]
    return jnp.concatenate(
        [first * cosine - second_half * sine, second_half * cosine + first * sine], axis=-1
    )


def lookup(table_values, slot_index):
    matches = slot_index[:, None] == jnp.arange(table_values.shape[0], dtype=jnp.int32)[None, :]
    return jnp.sum(jnp.where(matches, table_values[None, :], 0), axis=1)


def block_owners(block_table, block_ids):
    matched = block_table[None, :, :] == block_ids[:, None, None]
    row_ids = jnp.arange(block_table.shape[0], dtype=jnp.int32)[None, :, None]
    col_ids = jnp.arange(block_table.shape[1], dtype=jnp.int32)[None, None, :]
    used = jnp.any(matched, axis=(1, 2)).astype(jnp.int32)
    owner = jnp.sum(jnp.where(matched, row_ids, 0), axis=(1, 2)).astype(jnp.int32)
    column = jnp.sum(jnp.where(matched, col_ids, 0), axis=(1, 2)).astype(jnp.int32)
    return used, owner, column


def merged_block(i, used_ref, owner_ref, column_ref, clen_ref, start_ref, fresh_ref, kc_ref, vc_ref, span):
    block_size, kv_width = kc_ref.shape[1], kc_ref.shape[2]
    start = start_ref[i]
    base = pl.multiple_of((start // 8) * 8, 8)
    window = fresh_ref[pl.ds(base, block_size + 8), :].astype(jnp.bfloat16)
    pick = lax.broadcasted_iota(jnp.int32, (block_size, block_size + 8), 1) == (
        lax.broadcasted_iota(jnp.int32, (block_size, block_size + 8), 0) + (start - base)
    )
    window = jnp.dot(pick.astype(jnp.bfloat16), window, preferred_element_type=jnp.float32)
    slot_pos = column_ref[i] * block_size + lax.broadcasted_iota(
        jnp.int32, (block_size, kv_width), 0
    )
    first_new = clen_ref[owner_ref[i]]
    fresh = (used_ref[i] == 1) & (slot_pos >= first_new) & (slot_pos < first_new + span)
    keys = jnp.where(fresh, window[:, :kv_width], kc_ref[i].astype(jnp.float32))
    values = jnp.where(fresh, window[:, kv_width:], vc_ref[i].astype(jnp.float32))
    return keys.astype(kc_ref.dtype), values.astype(vc_ref.dtype)


def attention_kernel(
    used_ref, owner_ref, column_ref, clen_ref, start_ref, req_ref, q_ref, fresh_ref, kc_ref, vc_ref,
    o_ref, nk_ref, nv_ref, m_sc, l_sc, acc_sc, *, q_heads, head_dim
):
    r = req_ref[0]
    rows = q_ref.shape[0]
    block_size = kc_ref.shape[1]
    m_sc[...] = jnp.full(m_sc.shape, NEG_FILL, jnp.float32)
    l_sc[...] = jnp.zeros(l_sc.shape, jnp.float32)
    acc_sc[...] = jnp.zeros(acc_sc.shape, jnp.float32)

    def attend_heads(keys, values, allowed):
        for g in range(q_heads):
            queries = q_ref[:, g * head_dim : (g + 1) * head_dim]
            score = lax.dot_general(
                queries, keys, (((1,), (1,)), ((), ())), preferred_element_type=jnp.float32
            ) / math.sqrt(head_dim)
            if allowed is not None:
                score = jnp.where(allowed, score, NEG_FILL)
            top = m_sc[g]
            new_top = jnp.maximum(top, jnp.max(score, axis=1, keepdims=True))
            weights = jnp.exp(score - new_top)
            if allowed is not None:
                weights = jnp.where(allowed, weights, 0.0)
            factor = jnp.exp(top - new_top)
            l_sc[g] = l_sc[g] * factor + jnp.sum(weights, axis=1, keepdims=True)
            acc_sc[g] = acc_sc[g] * factor + jnp.dot(
                weights.astype(jnp.bfloat16), values, preferred_element_type=jnp.float32
            )
            m_sc[g] = new_top

    def visit(i, carry):
        active = (used_ref[i] == 1) & (owner_ref[i] == r)

        @pl.when(active)
        def _work():
            has_new = column_ref[i] * block_size + block_size - 1 >= clen_ref[r]

            @pl.when(has_new)
            def _merge():
                keys, values = merged_block(
                    i, used_ref, owner_ref, column_ref, clen_ref, start_ref, fresh_ref, kc_ref,
                    vc_ref, rows,
                )
                nk_ref[i] = keys
                nv_ref[i] = values

            @pl.when(jnp.logical_not(has_new))
            def _cached():
                nk_ref[i] = kc_ref[i]
                nv_ref[i] = vc_ref[i]

            keys = nk_ref[i]
            values = nv_ref[i]
            seen = column_ref[i] * block_size + block_size - 1 <= clen_ref[r]

            @pl.when(seen)
            def _all():
                attend_heads(keys, values, None)

            @pl.when(jnp.logical_not(seen))
            def _masked():
                query_pos = clen_ref[r] + lax.broadcasted_iota(jnp.int32, (rows, block_size), 0)
                key_pos = column_ref[i] * block_size + lax.broadcasted_iota(
                    jnp.int32, (rows, block_size), 1
                )
                attend_heads(keys, values, key_pos <= query_pos)

        return carry

    lax.fori_loop(0, kc_ref.shape[0], visit, 0)

    lane = lax.broadcasted_iota(jnp.int32, (rows, head_dim), 1)
    stats = jnp.zeros((rows, head_dim), jnp.float32)
    for g in range(q_heads):
        top = m_sc[g]
        valid = top > NEG_FILL / 2
        ref = jnp.where(valid, top.astype(jnp.bfloat16).astype(jnp.float32), NEG_FILL)
        factor = jnp.where(valid, jnp.exp(top - ref), 0.0)
        o_ref[:, g * head_dim : (g + 1) * head_dim] = (acc_sc[g] * factor).astype(o_ref.dtype)
        stats = jnp.where(lane == g, l_sc[g] * factor, stats)
        stats = jnp.where(lane == q_heads + g, ref, stats)
    o_ref[:, q_heads * head_dim :] = stats.astype(o_ref.dtype)


def block_meta(block_table, block_ids, cached_len, block_size, fresh_len):
    used, owner, column = block_owners(block_table, block_ids)
    start = block_size + column * block_size - cached_len[owner]
    start = jnp.clip(start, 0, fresh_len - block_size - 8).astype(jnp.int32)
    return used, owner, column, cached_len, start


def attend(queries, fresh_rows, keys, values, meta, request, span, q_heads, head_dim):
    n_blocks, block_size, kv_width = keys.shape
    q_width = q_heads * head_dim
    out_width = q_width + head_dim
    block = pl.BlockSpec(keys.shape, lambda i, *_: (0, 0, 0))
    grid_spec = pltpu.PrefetchScalarGridSpec(
        num_scalar_prefetch=6,
        grid=(1,),
        in_specs=[
            pl.BlockSpec((span, q_width), lambda i, *_: (0, 0)),
            pl.BlockSpec(fresh_rows.shape, lambda i, *_: (0, 0)),
            block,
            block,
        ],
        out_specs=[pl.BlockSpec((span, out_width), lambda i, *_: (0, 0)), block, block],
        scratch_shapes=[
            pltpu.VMEM((q_heads, span, head_dim), jnp.float32),
            pltpu.VMEM((q_heads, span, head_dim), jnp.float32),
            pltpu.VMEM((q_heads, span, head_dim), jnp.float32),
        ],
    )
    flops = n_blocks * span * q_heads * block_size * head_dim
    return pl.pallas_call(
        functools.partial(attention_kernel, q_heads=q_heads, head_dim=head_dim),
        grid_spec=grid_spec,
        out_shape=(
            jax.ShapeDtypeStruct((span, out_width), jnp.bfloat16),
            jax.ShapeDtypeStruct(keys.shape, keys.dtype),
            jax.ShapeDtypeStruct(values.shape, values.dtype),
        ),
        compiler_params=pltpu.CompilerParams(vmem_limit_bytes=48 * 1024 * 1024),
        cost_estimate=pl.CostEstimate(
            flops=flops,
            transcendentals=n_blocks * span * q_heads * block_size // 4,
            bytes_accessed=span * (q_width + out_width) * 2 + n_blocks * block_size * kv_width * 4,
        ),
    )(*meta, request, queries, fresh_rows, keys, values)


def combine_kernel(used_ref, owner_ref, got_ref, bk_ref, bv_ref, kc_ref, vc_ref, out_ref, nk_ref, nv_ref, *, q_heads, head_dim):
    ring = got_ref.shape[0]
    q_width = q_heads * head_dim
    stats = [got_ref[s, :, q_width:].astype(jnp.float32) for s in range(ring)]
    for g in range(q_heads):
        tops = [st[:, q_heads + g : q_heads + g + 1] for st in stats]
        best = tops[0]
        for t in tops[1:]:
            best = jnp.maximum(best, t)
        weighted = jnp.zeros((out_ref.shape[0], head_dim), jnp.float32)
        total = jnp.zeros((out_ref.shape[0], 1), jnp.float32)
        for s in range(ring):
            factor = jnp.exp(tops[s] - best)
            part = got_ref[s, :, g * head_dim : (g + 1) * head_dim].astype(jnp.float32)
            weighted = weighted + part * factor
            total = total + stats[s][:, g : g + 1] * factor
        out_ref[:, g * head_dim : (g + 1) * head_dim] = (weighted / total).astype(out_ref.dtype)
    for b in range(nk_ref.shape[0]):
        nk_ref[b] = jnp.where(used_ref[b] == 1, bk_ref[owner_ref[b], b], kc_ref[b])
        nv_ref[b] = jnp.where(used_ref[b] == 1, bv_ref[owner_ref[b], b], vc_ref[b])


def combine(used, owner, got, back_k, back_v, key_cache, value_cache, q_heads, head_dim):
    ring, rows, _ = got.shape
    nb_dev = back_k.shape[1]

    def whole(x):
        return pl.BlockSpec(x.shape, lambda i, *_: (0,) * x.ndim)

    grid_spec = pltpu.PrefetchScalarGridSpec(
        num_scalar_prefetch=2,
        grid=(1,),
        in_specs=[whole(got), whole(back_k), whole(back_v), whole(key_cache), whole(value_cache)],
        out_specs=[
            pl.BlockSpec((rows, q_heads * head_dim), lambda i, *_: (0, 0)),
            pl.BlockSpec(back_k.shape[1:], lambda i, *_: (0, 0, 0)),
            pl.BlockSpec(back_v.shape[1:], lambda i, *_: (0, 0, 0)),
        ],
    )
    return pl.pallas_call(
        functools.partial(combine_kernel, q_heads=q_heads, head_dim=head_dim),
        grid_spec=grid_spec,
        out_shape=(
            jax.ShapeDtypeStruct((rows, q_heads * head_dim), jnp.bfloat16),
            jax.ShapeDtypeStruct(back_k.shape[1:], back_k.dtype),
            jax.ShapeDtypeStruct(back_v.shape[1:], back_v.dtype),
        ),
        compiler_params=pltpu.CompilerParams(vmem_limit_bytes=32 * 1024 * 1024),
    )(used, owner, got, back_k, back_v, key_cache, value_cache)


MESH = pl.DeviceIdType.MESH


def multi_exchange_kernel(*refs, specs):
    n_total = sum(s[4] for s in specs)
    srcs, dsts = refs[:n_total], refs[n_total : 2 * n_total]
    send_sem, recv_sem, own_sem = refs[2 * n_total :]
    here = {"kv": lax.axis_index("kv"), "blk": lax.axis_index("blk")}

    def device(axis, index):
        return (index, here["blk"]) if axis == "kv" else (here["kv"], index)

    groups = []
    arr0, sem0 = 0, 0
    for axis, m, stride, gather, n_arr in specs:
        pos = lax.rem(here[axis] // stride, m)
        base = here[axis] - pos * stride
        groups.append((axis, m, stride, gather, n_arr, pos, base, arr0, sem0))
        arr0 += n_arr
        sem0 += m * n_arr

    barrier = pltpu.get_barrier_semaphore()
    for axis, m, stride, gather, n_arr, pos, base, _, _ in groups:
        for k in range(1, m):
            peer = base + lax.rem(pos + k, m) * stride
            pl.semaphore_signal(barrier, inc=1, device_id=device(axis, peer), device_id_type=MESH)
    pl.semaphore_wait(barrier, sum(s[1] - 1 for s in specs))

    def chunk(src, j, m, gather):
        if gather:
            return src
        rows = src.shape[0] // m
        return src.at[pl.ds(pl.multiple_of(j * rows, rows), rows)]

    owns, copies = [], []
    for axis, m, stride, gather, n_arr, pos, base, a0, s0 in groups:
        for a in range(a0, a0 + n_arr):
            own = pltpu.make_async_copy(chunk(srcs[a], pos, m, gather), dsts[a].at[pos], own_sem.at[a])
            own.start()
            owns.append(own)
    for axis, m, stride, gather, n_arr, pos, base, a0, s0 in groups:
        for k in range(1, m):
            peer_pos = lax.rem(pos + k, m)
            for a in range(n_arr):
                copy = pltpu.make_async_remote_copy(
                    src_ref=chunk(srcs[a0 + a], peer_pos, m, gather),
                    dst_ref=dsts[a0 + a].at[pos],
                    send_sem=send_sem.at[s0 + k * n_arr + a],
                    recv_sem=recv_sem.at[s0 + k * n_arr + a],
                    device_id=device(axis, base + peer_pos * stride),
                    device_id_type=MESH,
                )
                copy.start()
                copies.append(copy)
    for own in owns:
        own.wait()
    c = 0
    for axis, m, stride, gather, n_arr, pos, base, a0, s0 in groups:
        for k in range(1, m):
            sender_pos = lax.rem(pos + m - k, m)
            for a in range(n_arr):
                incoming = pltpu.make_async_remote_copy(
                    src_ref=chunk(srcs[a0 + a], pos, m, gather),
                    dst_ref=dsts[a0 + a].at[sender_pos],
                    send_sem=send_sem.at[s0 + k * n_arr + a],
                    recv_sem=recv_sem.at[s0 + k * n_arr + a],
                    device_id=device(axis, base + sender_pos * stride),
                    device_id_type=MESH,
                )
                copies[c].wait_send()
                incoming.wait_recv()
                c += 1


def multi_exchange(groups, collective_id):
    specs, arrays, shapes = [], [], []
    for axis, m, stride, gather, arrs in groups:
        specs.append((axis, m, stride, gather, len(arrs)))
        for x in arrs:
            rows = x.shape[0] if gather else x.shape[0] // m
            arrays.append(x)
            shapes.append(jax.ShapeDtypeStruct((m, rows) + x.shape[1:], x.dtype))
    n_sem = sum(s[1] * s[4] for s in specs)
    return pl.pallas_call(
        functools.partial(multi_exchange_kernel, specs=tuple(specs)),
        out_shape=tuple(shapes),
        in_specs=[pl.BlockSpec(memory_space=pl.ANY)] * len(arrays),
        out_specs=tuple([pl.BlockSpec(memory_space=pl.ANY)] * len(arrays)),
        scratch_shapes=[
            pltpu.SemaphoreType.DMA((n_sem,)),
            pltpu.SemaphoreType.DMA((n_sem,)),
            pltpu.SemaphoreType.DMA((len(arrays),)),
        ],
        compiler_params=pltpu.CompilerParams(collective_id=collective_id, has_side_effects=True),
    )(*arrays)


def on_device(
    hidden_in,
    norm_gain,
    w_query,
    key_weight,
    value_weight,
    b_query,
    key_bias,
    value_bias,
    key_cache,
    value_cache,
    cached_len,
    block_table,
):
    tok_dev = hidden_in.shape[0]
    n_blk = lax.axis_size("blk")
    device = lax.axis_index("blk")
    requests = cached_len.shape[0]
    tokens = tok_dev * n_blk
    span = tokens // requests
    nb_dev, block_size, kv_width = key_cache.shape
    head_dim = HEAD_SIZE
    kv_heads = kv_width // head_dim
    q_heads = w_query.shape[1] // head_dim
    group_size = q_heads // kv_heads
    gain = norm_gain.astype(jnp.float32)
    ring = span // tok_dev
    cols = n_blk // ring
    position = device % ring
    kv_n = lax.axis_size("kv")
    (got_hidden,) = multi_exchange([("kv", kv_n, 1, True, [hidden_in])], 0)
    feat = hidden_in.shape[1]
    wide_in = got_hidden.astype(jnp.float32)
    scale = lax.rsqrt(jnp.mean(wide_in * wide_in, axis=(0, 2), keepdims=True) + EPS)
    normed = (wide_in * scale * gain.reshape(kv_n, 1, feat)).astype(jnp.bfloat16)

    def project(weight):
        return lax.dot_general(
            normed,
            weight.reshape(kv_n, feat, weight.shape[1]),
            (((0, 2), (0, 1)), ((), ())),
            preferred_element_type=jnp.float32,
        )

    q_lin = project(w_query)
    key_linear = project(key_weight)
    value_linear = project(value_weight)
    my_tokens = device * tok_dev + jnp.arange(tok_dev, dtype=jnp.int32)
    my_pos = lookup(cached_len, my_tokens // span) + my_tokens % span
    fresh_queries = apply_rotary(
        (q_lin + b_query.astype(jnp.float32)[None, :]).reshape(tok_dev, q_heads, head_dim),
        my_pos,
        head_dim,
    )
    fresh_queries = fresh_queries.astype(jnp.bfloat16).reshape(tok_dev, q_heads * head_dim)
    fresh_keys = apply_rotary(
        (key_linear + key_bias.astype(jnp.float32)[None, :]).reshape(tok_dev, kv_heads, head_dim),
        my_pos,
        head_dim,
    )
    fresh_keys = fresh_keys.astype(jnp.bfloat16).reshape(tok_dev, kv_width)
    fresh_values = (value_linear + value_bias.astype(jnp.float32)[None, :]).astype(jnp.bfloat16)
    q_width = q_heads * head_dim
    packed = jnp.concatenate([fresh_queries, fresh_keys, fresh_values], axis=1)
    ring_packed, col_keys, col_values = multi_exchange(
        [("blk", ring, 1, True, [packed]), ("blk", cols, ring, True, [key_cache, value_cache])], 1
    )
    ring_packed = ring_packed.reshape(span, packed.shape[1])
    fresh_rows = jnp.pad(
        ring_packed[:, q_width:].astype(jnp.float32), ((block_size, block_size + 8), (0, 0))
    )
    holders = jnp.arange(cols, dtype=jnp.int32) * ring + position
    col_ids = (holders[:, None] * nb_dev + jnp.arange(nb_dev, dtype=jnp.int32)[None, :]).reshape(-1)
    meta = block_meta(block_table, col_ids, cached_len, block_size, fresh_rows.shape[0])
    request = (device // ring).reshape(1).astype(jnp.int32)
    parts, merged_k, merged_v = attend(
        ring_packed,
        fresh_rows,
        col_keys.reshape(cols * nb_dev, block_size, kv_width),
        col_values.reshape(cols * nb_dev, block_size, kv_width),
        meta,
        request,
        span,
        q_heads,
        head_dim,
    )
    got, back_k, back_v = multi_exchange(
        [("blk", ring, 1, False, [parts]), ("blk", cols, ring, False, [merged_k, merged_v])], 2
    )
    mine = (device // ring) * nb_dev
    used = lax.dynamic_slice_in_dim(meta[0], mine, nb_dev)
    owner = lax.dynamic_slice_in_dim(meta[1], mine, nb_dev)
    attn_out, new_k, new_v = combine(
        used,
        owner,
        got,
        back_k.reshape(cols, nb_dev, block_size, kv_width),
        back_v.reshape(cols, nb_dev, block_size, kv_width),
        key_cache,
        value_cache,
        q_heads,
        head_dim,
    )
    return (attn_out, new_k, new_v)


def solution(mesh):
    in_specs = (
        P("blk", "kv"),
        P(),
        P(None, "kv"),
        P(None, "kv"),
        P(None, "kv"),
        P("kv"),
        P("kv"),
        P("kv"),
        P("blk", None, "kv"),
        P("blk", None, "kv"),
        P(),
        P(),
    )
    out_specs = (P("blk", "kv"), P("blk", None, "kv"), P("blk", None, "kv"))
    return jax.shard_map(
        on_device, mesh=mesh, in_specs=in_specs, out_specs=out_specs, check_vma=False
    )
```

```python
import functools
import math

import jax
import jax.numpy as jnp
from jax import lax
from jax.experimental import pallas as pl
from jax.experimental.pallas import tpu as pltpu
from jax.sharding import PartitionSpec as P

HEAD_SIZE = 128


EPS = 1e-06
THETA = 1000000.0
NEG_FILL = -1e30


def apply_rotary(values, token_positions, head_dim):
    half = head_dim // 2
    rates = THETA ** (-(jnp.arange(half, dtype=jnp.float32) * 2.0) / head_dim)
    angle = token_positions.astype(jnp.float32)[:, None] * rates[None, :]
    cosine = jnp.cos(angle)[:, None, :]
    sine = jnp.sin(angle)[:, None, :]
    first = values[..., :half]
    second_half = values[..., half:]
    return jnp.concatenate(
        [first * cosine - second_half * sine, second_half * cosine + first * sine], axis=-1
    )


def lookup(table_values, slot_index):
    matches = slot_index[:, None] == jnp.arange(table_values.shape[0], dtype=jnp.int32)[None, :]
    return jnp.sum(jnp.where(matches, table_values[None, :], 0), axis=1)


def block_owners(block_table, block_ids):
    matched = block_table[None, :, :] == block_ids[:, None, None]
    row_ids = jnp.arange(block_table.shape[0], dtype=jnp.int32)[None, :, None]
    col_ids = jnp.arange(block_table.shape[1], dtype=jnp.int32)[None, None, :]
    used = jnp.any(matched, axis=(1, 2)).astype(jnp.int32)
    owner = jnp.sum(jnp.where(matched, row_ids, 0), axis=(1, 2)).astype(jnp.int32)
    column = jnp.sum(jnp.where(matched, col_ids, 0), axis=(1, 2)).astype(jnp.int32)
    return used, owner, column


def merged_block(i, used_ref, owner_ref, column_ref, clen_ref, start_ref, fresh_ref, kc_ref, vc_ref, span):
    block_size, kv_width = kc_ref.shape[1], kc_ref.shape[2]
    start = start_ref[i]
    base = pl.multiple_of((start // 8) * 8, 8)
    window = fresh_ref[pl.ds(base, block_size + 8), :].astype(jnp.bfloat16)
    pick = lax.broadcasted_iota(jnp.int32, (block_size, block_size + 8), 1) == (
        lax.broadcasted_iota(jnp.int32, (block_size, block_size + 8), 0) + (start - base)
    )
    window = jnp.dot(pick.astype(jnp.bfloat16), window, preferred_element_type=jnp.float32)
    slot_pos = column_ref[i] * block_size + lax.broadcasted_iota(
        jnp.int32, (block_size, kv_width), 0
    )
    first_new = clen_ref[owner_ref[i]]
    fresh = (used_ref[i] == 1) & (slot_pos >= first_new) & (slot_pos < first_new + span)
    keys = jnp.where(fresh, window[:, :kv_width], kc_ref[i].astype(jnp.float32))
    values = jnp.where(fresh, window[:, kv_width:], vc_ref[i].astype(jnp.float32))
    return keys.astype(kc_ref.dtype), values.astype(vc_ref.dtype)


def attention_kernel(
    used_ref, owner_ref, column_ref, clen_ref, start_ref, req_ref, q_ref, fresh_ref, kc_ref, vc_ref,
    o_hbm, nk_hbm, nv_hbm, o_ref, nk_ref, nv_ref, m_sc, l_sc, acc_sc, out_sem, *, q_heads, head_dim
):
    r = req_ref[0]
    rows = q_ref.shape[0]
    block_size = kc_ref.shape[1]
    m_sc[...] = jnp.full(m_sc.shape, NEG_FILL, jnp.float32)
    l_sc[...] = jnp.zeros(l_sc.shape, jnp.float32)
    acc_sc[...] = jnp.zeros(acc_sc.shape, jnp.float32)

    def attend_heads(keys, values, allowed):
        for g in range(q_heads):
            queries = q_ref[:, g * head_dim : (g + 1) * head_dim]
            score = lax.dot_general(
                queries, keys, (((1,), (1,)), ((), ())), preferred_element_type=jnp.float32
            ) / math.sqrt(head_dim)
            if allowed is not None:
                score = jnp.where(allowed, score, NEG_FILL)
            top = m_sc[g]
            new_top = jnp.maximum(top, jnp.max(score, axis=1, keepdims=True))
            weights = jnp.exp(score - new_top)
            if allowed is not None:
                weights = jnp.where(allowed, weights, 0.0)
            factor = jnp.exp(top - new_top)
            l_sc[g] = l_sc[g] * factor + jnp.sum(weights, axis=1, keepdims=True)
            acc_sc[g] = acc_sc[g] * factor + jnp.dot(
                weights.astype(jnp.bfloat16), values, preferred_element_type=jnp.float32
            )
            m_sc[g] = new_top

    def visit(i, carry):
        active = (used_ref[i] == 1) & (owner_ref[i] == r)

        @pl.when(active)
        def _work():
            has_new = column_ref[i] * block_size + block_size - 1 >= clen_ref[r]

            @pl.when(has_new)
            def _merge():
                keys, values = merged_block(
                    i, used_ref, owner_ref, column_ref, clen_ref, start_ref, fresh_ref, kc_ref,
                    vc_ref, rows,
                )
                nk_ref[i] = keys
                nv_ref[i] = values

            @pl.when(jnp.logical_not(has_new))
            def _cached():
                nk_ref[i] = kc_ref[i]
                nv_ref[i] = vc_ref[i]

            keys = nk_ref[i]
            values = nv_ref[i]
            seen = column_ref[i] * block_size + block_size - 1 <= clen_ref[r]

            @pl.when(seen)
            def _all():
                attend_heads(keys, values, None)

            @pl.when(jnp.logical_not(seen))
            def _masked():
                query_pos = clen_ref[r] + lax.broadcasted_iota(jnp.int32, (rows, block_size), 0)
                key_pos = column_ref[i] * block_size + lax.broadcasted_iota(
                    jnp.int32, (rows, block_size), 1
                )
                attend_heads(keys, values, key_pos <= query_pos)

        return carry

    lax.fori_loop(0, kc_ref.shape[0], visit, 0)

    lane = lax.broadcasted_iota(jnp.int32, (rows, head_dim), 1)
    stats = jnp.zeros((rows, head_dim), jnp.float32)
    for g in range(q_heads):
        top = m_sc[g]
        valid = top > NEG_FILL / 2
        ref = jnp.where(valid, top.astype(jnp.bfloat16).astype(jnp.float32), NEG_FILL)
        factor = jnp.where(valid, jnp.exp(top - ref), 0.0)
        o_ref[:, g * head_dim : (g + 1) * head_dim] = (acc_sc[g] * factor).astype(o_ref.dtype)
        stats = jnp.where(lane == g, l_sc[g] * factor, stats)
        stats = jnp.where(lane == q_heads + g, ref, stats)
    o_ref[:, q_heads * head_dim :] = stats.astype(o_ref.dtype)
    outs = [
        pltpu.make_async_copy(o_ref, o_hbm, out_sem.at[0]),
        pltpu.make_async_copy(nk_ref, nk_hbm, out_sem.at[1]),
        pltpu.make_async_copy(nv_ref, nv_hbm, out_sem.at[2]),
    ]
    for copy in outs:
        copy.start()
    for copy in outs:
        copy.wait()


def block_meta(block_table, block_ids, cached_len, block_size, fresh_len):
    used, owner, column = block_owners(block_table, block_ids)
    start = block_size + column * block_size - cached_len[owner]
    start = jnp.clip(start, 0, fresh_len - block_size - 8).astype(jnp.int32)
    return used, owner, column, cached_len, start


def attend(queries, fresh_rows, keys, values, meta, request, span, q_heads, head_dim):
    n_blocks, block_size, kv_width = keys.shape
    q_width = q_heads * head_dim
    out_width = q_width + head_dim
    block = pl.BlockSpec(keys.shape, lambda i, *_: (0, 0, 0))
    grid_spec = pltpu.PrefetchScalarGridSpec(
        num_scalar_prefetch=6,
        grid=(1,),
        in_specs=[
            pl.BlockSpec((span, q_width), lambda i, *_: (0, 0)),
            pl.BlockSpec(fresh_rows.shape, lambda i, *_: (0, 0)),
            block,
            block,
        ],
        out_specs=[pl.BlockSpec(memory_space=pl.ANY)] * 3,
        scratch_shapes=[
            pltpu.VMEM((span, out_width), jnp.bfloat16),
            pltpu.VMEM(keys.shape, keys.dtype),
            pltpu.VMEM(values.shape, values.dtype),
            pltpu.VMEM((q_heads, span, head_dim), jnp.float32),
            pltpu.VMEM((q_heads, span, head_dim), jnp.float32),
            pltpu.VMEM((q_heads, span, head_dim), jnp.float32),
            pltpu.SemaphoreType.DMA((3,)),
        ],
    )
    flops = n_blocks * span * q_heads * block_size * head_dim
    return pl.pallas_call(
        functools.partial(attention_kernel, q_heads=q_heads, head_dim=head_dim),
        grid_spec=grid_spec,
        out_shape=(
            jax.ShapeDtypeStruct((span, out_width), jnp.bfloat16),
            jax.ShapeDtypeStruct(keys.shape, keys.dtype),
            jax.ShapeDtypeStruct(values.shape, values.dtype),
        ),
        compiler_params=pltpu.CompilerParams(vmem_limit_bytes=48 * 1024 * 1024),
        cost_estimate=pl.CostEstimate(
            flops=flops,
            transcendentals=n_blocks * span * q_heads * block_size // 4,
            bytes_accessed=span * (q_width + out_width) * 2 + n_blocks * block_size * kv_width * 4,
        ),
    )(*meta, request, queries, fresh_rows, keys, values)


def combine_kernel(
    used_ref, owner_ref, got_ref, bk_hbm, bv_hbm, kc_ref, vc_ref, out_ref, nk_ref, nv_ref, bk_ref, bv_ref,
    sem, *, q_heads, head_dim
):
    fetches = []
    for b in range(nk_ref.shape[0]):
        for a, (src, dst) in enumerate(((bk_hbm, bk_ref), (bv_hbm, bv_ref))):
            fetch = pltpu.make_async_copy(src.at[owner_ref[b], b], dst.at[b], sem.at[a, b])
            fetch.start()
            fetches.append(fetch)
    ring = got_ref.shape[0]
    q_width = q_heads * head_dim
    stats = [got_ref[s, :, q_width:].astype(jnp.float32) for s in range(ring)]
    for g in range(q_heads):
        tops = [st[:, q_heads + g : q_heads + g + 1] for st in stats]
        best = tops[0]
        for t in tops[1:]:
            best = jnp.maximum(best, t)
        weighted = jnp.zeros((out_ref.shape[0], head_dim), jnp.float32)
        total = jnp.zeros((out_ref.shape[0], 1), jnp.float32)
        for s in range(ring):
            factor = jnp.exp(tops[s] - best)
            part = got_ref[s, :, g * head_dim : (g + 1) * head_dim].astype(jnp.float32)
            weighted = weighted + part * factor
            total = total + stats[s][:, g : g + 1] * factor
        out_ref[:, g * head_dim : (g + 1) * head_dim] = (weighted / total).astype(out_ref.dtype)
    for fetch in fetches:
        fetch.wait()
    for b in range(nk_ref.shape[0]):
        nk_ref[b] = jnp.where(used_ref[b] == 1, bk_ref[b], kc_ref[b])
        nv_ref[b] = jnp.where(used_ref[b] == 1, bv_ref[b], vc_ref[b])


def combine(used, owner, got, back_k, back_v, key_cache, value_cache, q_heads, head_dim):
    ring, rows, _ = got.shape
    nb_dev = back_k.shape[1]

    def whole(x):
        return pl.BlockSpec(x.shape, lambda i, *_: (0,) * x.ndim)

    grid_spec = pltpu.PrefetchScalarGridSpec(
        num_scalar_prefetch=2,
        grid=(1,),
        in_specs=[
            whole(got),
            pl.BlockSpec(memory_space=pl.ANY),
            pl.BlockSpec(memory_space=pl.ANY),
            whole(key_cache),
            whole(value_cache),
        ],
        out_specs=[
            pl.BlockSpec((rows, q_heads * head_dim), lambda i, *_: (0, 0)),
            pl.BlockSpec(back_k.shape[1:], lambda i, *_: (0, 0, 0)),
            pl.BlockSpec(back_v.shape[1:], lambda i, *_: (0, 0, 0)),
        ],
        scratch_shapes=[
            pltpu.VMEM(back_k.shape[1:], back_k.dtype),
            pltpu.VMEM(back_v.shape[1:], back_v.dtype),
            pltpu.SemaphoreType.DMA((2, nb_dev)),
        ],
    )
    return pl.pallas_call(
        functools.partial(combine_kernel, q_heads=q_heads, head_dim=head_dim),
        grid_spec=grid_spec,
        out_shape=(
            jax.ShapeDtypeStruct((rows, q_heads * head_dim), jnp.bfloat16),
            jax.ShapeDtypeStruct(back_k.shape[1:], back_k.dtype),
            jax.ShapeDtypeStruct(back_v.shape[1:], back_v.dtype),
        ),
        compiler_params=pltpu.CompilerParams(vmem_limit_bytes=32 * 1024 * 1024),
    )(used, owner, got, back_k, back_v, key_cache, value_cache)


MESH = pl.DeviceIdType.MESH


def multi_exchange_kernel(*refs, specs):
    n_total = sum(s[4] for s in specs)
    srcs, dsts = refs[:n_total], refs[n_total : 2 * n_total]
    send_sem, recv_sem, own_sem = refs[2 * n_total :]
    here = {"kv": lax.axis_index("kv"), "blk": lax.axis_index("blk")}

    def device(axis, index):
        return (index, here["blk"]) if axis == "kv" else (here["kv"], index)

    groups = []
    arr0, sem0 = 0, 0
    for axis, m, stride, gather, n_arr in specs:
        pos = lax.rem(here[axis] // stride, m)
        base = here[axis] - pos * stride
        groups.append((axis, m, stride, gather, n_arr, pos, base, arr0, sem0))
        arr0 += n_arr
        sem0 += m * n_arr

    barrier = pltpu.get_barrier_semaphore()
    for axis, m, stride, gather, n_arr, pos, base, _, _ in groups:
        for k in range(1, m):
            peer = base + lax.rem(pos + k, m) * stride
            pl.semaphore_signal(barrier, inc=1, device_id=device(axis, peer), device_id_type=MESH)
    pl.semaphore_wait(barrier, sum(s[1] - 1 for s in specs))

    def chunk(src, j, m, gather):
        if gather:
            return src
        rows = src.shape[0] // m
        return src.at[pl.ds(pl.multiple_of(j * rows, rows), rows)]

    owns, copies = [], []
    for axis, m, stride, gather, n_arr, pos, base, a0, s0 in groups:
        for a in range(a0, a0 + n_arr):
            own = pltpu.make_async_copy(chunk(srcs[a], pos, m, gather), dsts[a].at[pos], own_sem.at[a])
            own.start()
            owns.append(own)
    for axis, m, stride, gather, n_arr, pos, base, a0, s0 in groups:
        for k in range(1, m):
            peer_pos = lax.rem(pos + k, m)
            for a in range(n_arr):
                copy = pltpu.make_async_remote_copy(
                    src_ref=chunk(srcs[a0 + a], peer_pos, m, gather),
                    dst_ref=dsts[a0 + a].at[pos],
                    send_sem=send_sem.at[s0 + k * n_arr + a],
                    recv_sem=recv_sem.at[s0 + k * n_arr + a],
                    device_id=device(axis, base + peer_pos * stride),
                    device_id_type=MESH,
                )
                copy.start()
                copies.append(copy)
    for own in owns:
        own.wait()
    c = 0
    for axis, m, stride, gather, n_arr, pos, base, a0, s0 in groups:
        for k in range(1, m):
            sender_pos = lax.rem(pos + m - k, m)
            for a in range(n_arr):
                incoming = pltpu.make_async_remote_copy(
                    src_ref=chunk(srcs[a0 + a], pos, m, gather),
                    dst_ref=dsts[a0 + a].at[sender_pos],
                    send_sem=send_sem.at[s0 + k * n_arr + a],
                    recv_sem=recv_sem.at[s0 + k * n_arr + a],
                    device_id=device(axis, base + sender_pos * stride),
                    device_id_type=MESH,
                )
                copies[c].wait_send()
                incoming.wait_recv()
                c += 1


def multi_exchange(groups, collective_id):
    specs, arrays, shapes = [], [], []
    for axis, m, stride, gather, arrs in groups:
        specs.append((axis, m, stride, gather, len(arrs)))
        for x in arrs:
            rows = x.shape[0] if gather else x.shape[0] // m
            arrays.append(x)
            shapes.append(jax.ShapeDtypeStruct((m, rows) + x.shape[1:], x.dtype))
    n_sem = sum(s[1] * s[4] for s in specs)
    return pl.pallas_call(
        functools.partial(multi_exchange_kernel, specs=tuple(specs)),
        out_shape=tuple(shapes),
        in_specs=[pl.BlockSpec(memory_space=pl.ANY)] * len(arrays),
        out_specs=tuple([pl.BlockSpec(memory_space=pl.ANY)] * len(arrays)),
        scratch_shapes=[
            pltpu.SemaphoreType.DMA((n_sem,)),
            pltpu.SemaphoreType.DMA((n_sem,)),
            pltpu.SemaphoreType.DMA((len(arrays),)),
        ],
        compiler_params=pltpu.CompilerParams(collective_id=collective_id, has_side_effects=True),
    )(*arrays)


def on_device(
    hidden_in,
    norm_gain,
    w_query,
    key_weight,
    value_weight,
    b_query,
    key_bias,
    value_bias,
    key_cache,
    value_cache,
    cached_len,
    block_table,
):
    tok_dev = hidden_in.shape[0]
    n_blk = lax.axis_size("blk")
    device = lax.axis_index("blk")
    requests = cached_len.shape[0]
    tokens = tok_dev * n_blk
    span = tokens // requests
    nb_dev, block_size, kv_width = key_cache.shape
    head_dim = HEAD_SIZE
    kv_heads = kv_width // head_dim
    q_heads = w_query.shape[1] // head_dim
    group_size = q_heads // kv_heads
    gain = norm_gain.astype(jnp.float32)
    ring = span // tok_dev
    cols = n_blk // ring
    position = device % ring
    kv_n = lax.axis_size("kv")
    (got_hidden,) = multi_exchange([("kv", kv_n, 1, True, [hidden_in])], 0)
    feat = hidden_in.shape[1]
    wide_in = got_hidden.astype(jnp.float32)
    scale = lax.rsqrt(jnp.mean(wide_in * wide_in, axis=(0, 2), keepdims=True) + EPS)
    normed = (wide_in * scale * gain.reshape(kv_n, 1, feat)).astype(jnp.bfloat16)

    def project(weight):
        return lax.dot_general(
            normed,
            weight.reshape(kv_n, feat, weight.shape[1]),
            (((0, 2), (0, 1)), ((), ())),
            preferred_element_type=jnp.float32,
        )

    q_lin = project(w_query)
    key_linear = project(key_weight)
    value_linear = project(value_weight)
    my_tokens = device * tok_dev + jnp.arange(tok_dev, dtype=jnp.int32)
    my_pos = lookup(cached_len, my_tokens // span) + my_tokens % span
    fresh_queries = apply_rotary(
        (q_lin + b_query.astype(jnp.float32)[None, :]).reshape(tok_dev, q_heads, head_dim),
        my_pos,
        head_dim,
    )
    fresh_queries = fresh_queries.astype(jnp.bfloat16).reshape(tok_dev, q_heads * head_dim)
    fresh_keys = apply_rotary(
        (key_linear + key_bias.astype(jnp.float32)[None, :]).reshape(tok_dev, kv_heads, head_dim),
        my_pos,
        head_dim,
    )
    fresh_keys = fresh_keys.astype(jnp.bfloat16).reshape(tok_dev, kv_width)
    fresh_values = (value_linear + value_bias.astype(jnp.float32)[None, :]).astype(jnp.bfloat16)
    q_width = q_heads * head_dim
    packed = jnp.concatenate([fresh_queries, fresh_keys, fresh_values], axis=1)
    ring_packed, col_keys, col_values = multi_exchange(
        [("blk", ring, 1, True, [packed]), ("blk", cols, ring, True, [key_cache, value_cache])], 1
    )
    ring_packed = ring_packed.reshape(span, packed.shape[1])
    fresh_rows = jnp.pad(
        ring_packed[:, q_width:].astype(jnp.float32), ((block_size, block_size + 8), (0, 0))
    )
    holders = jnp.arange(cols, dtype=jnp.int32) * ring + position
    col_ids = (holders[:, None] * nb_dev + jnp.arange(nb_dev, dtype=jnp.int32)[None, :]).reshape(-1)
    meta = block_meta(block_table, col_ids, cached_len, block_size, fresh_rows.shape[0])
    request = (device // ring).reshape(1).astype(jnp.int32)
    parts, merged_k, merged_v = attend(
        ring_packed,
        fresh_rows,
        col_keys.reshape(cols * nb_dev, block_size, kv_width),
        col_values.reshape(cols * nb_dev, block_size, kv_width),
        meta,
        request,
        span,
        q_heads,
        head_dim,
    )
    got, back_k, back_v = multi_exchange(
        [("blk", ring, 1, False, [parts]), ("blk", cols, ring, False, [merged_k, merged_v])], 2
    )
    mine = (device // ring) * nb_dev
    used = lax.dynamic_slice_in_dim(meta[0], mine, nb_dev)
    owner = lax.dynamic_slice_in_dim(meta[1], mine, nb_dev)
    attn_out, new_k, new_v = combine(
        used,
        owner,
        got,
        back_k.reshape(cols, nb_dev, block_size, kv_width),
        back_v.reshape(cols, nb_dev, block_size, kv_width),
        key_cache,
        value_cache,
        q_heads,
        head_dim,
    )
    return (attn_out, new_k, new_v)


def solution(mesh):
    in_specs = (
        P("blk", "kv"),
        P(),
        P(None, "kv"),
        P(None, "kv"),
        P(None, "kv"),
        P("kv"),
        P("kv"),
        P("kv"),
        P("blk", None, "kv"),
        P("blk", None, "kv"),
        P(),
        P(),
    )
    out_specs = (P("blk", "kv"), P("blk", None, "kv"), P("blk", None, "kv"))
    return jax.shard_map(
        on_device, mesh=mesh, in_specs=in_specs, out_specs=out_specs, check_vma=False
    )
```

```python
import functools
import math

import jax
import jax.numpy as jnp
from jax import lax
from jax.experimental import pallas as pl
from jax.experimental.pallas import tpu as pltpu
from jax.sharding import PartitionSpec as P

HEAD_SIZE = 128


EPS = 1e-06
THETA = 1000000.0
NEG_FILL = -1e30


def apply_rotary(values, token_positions, head_dim):
    half = head_dim // 2
    rates = THETA ** (-(jnp.arange(half, dtype=jnp.float32) * 2.0) / head_dim)
    angle = token_positions.astype(jnp.float32)[:, None] * rates[None, :]
    cosine = jnp.cos(angle)[:, None, :]
    sine = jnp.sin(angle)[:, None, :]
    first = values[..., :half]
    second_half = values[..., half:]
    return jnp.concatenate(
        [first * cosine - second_half * sine, second_half * cosine + first * sine], axis=-1
    )


def lookup(table_values, slot_index):
    matches = slot_index[:, None] == jnp.arange(table_values.shape[0], dtype=jnp.int32)[None, :]
    return jnp.sum(jnp.where(matches, table_values[None, :], 0), axis=1)


def block_owners(block_table, block_ids):
    matched = block_table[None, :, :] == block_ids[:, None, None]
    row_ids = jnp.arange(block_table.shape[0], dtype=jnp.int32)[None, :, None]
    col_ids = jnp.arange(block_table.shape[1], dtype=jnp.int32)[None, None, :]
    used = jnp.any(matched, axis=(1, 2)).astype(jnp.int32)
    owner = jnp.sum(jnp.where(matched, row_ids, 0), axis=(1, 2)).astype(jnp.int32)
    column = jnp.sum(jnp.where(matched, col_ids, 0), axis=(1, 2)).astype(jnp.int32)
    return used, owner, column


def merged_block(i, used_ref, owner_ref, column_ref, clen_ref, start_ref, fresh_ref, kc_ref, vc_ref, span):
    block_size, kv_width = kc_ref.shape[1], kc_ref.shape[2]
    start = start_ref[i]
    base = pl.multiple_of((start // 8) * 8, 8)
    window = fresh_ref[pl.ds(base, block_size + 8), :].astype(jnp.bfloat16)
    pick = lax.broadcasted_iota(jnp.int32, (block_size, block_size + 8), 1) == (
        lax.broadcasted_iota(jnp.int32, (block_size, block_size + 8), 0) + (start - base)
    )
    window = jnp.dot(pick.astype(jnp.bfloat16), window, preferred_element_type=jnp.float32)
    slot_pos = column_ref[i] * block_size + lax.broadcasted_iota(
        jnp.int32, (block_size, kv_width), 0
    )
    first_new = clen_ref[owner_ref[i]]
    fresh = (used_ref[i] == 1) & (slot_pos >= first_new) & (slot_pos < first_new + span)
    keys = jnp.where(fresh, window[:, :kv_width], kc_ref[i].astype(jnp.float32))
    values = jnp.where(fresh, window[:, kv_width:], vc_ref[i].astype(jnp.float32))
    return keys.astype(kc_ref.dtype), values.astype(vc_ref.dtype)


def attention_kernel(
    used_ref, owner_ref, column_ref, clen_ref, start_ref, req_ref, q_ref, fresh_ref, kc_ref, vc_ref,
    o_hbm, nk_hbm, nv_hbm, o_ref, nk_ref, nv_ref, m_sc, l_sc, acc_sc, out_sem, *, q_heads, head_dim
):
    r = req_ref[0]
    rows = q_ref.shape[0]
    block_size = kc_ref.shape[1]
    m_sc[...] = jnp.full(m_sc.shape, NEG_FILL, jnp.float32)
    l_sc[...] = jnp.zeros(l_sc.shape, jnp.float32)
    acc_sc[...] = jnp.zeros(acc_sc.shape, jnp.float32)

    def attend_heads(keys, values, allowed):
        for g in range(q_heads):
            queries = q_ref[:, g * head_dim : (g + 1) * head_dim]
            score = lax.dot_general(
                queries, keys, (((1,), (1,)), ((), ())), preferred_element_type=jnp.float32
            ) / math.sqrt(head_dim)
            if allowed is not None:
                score = jnp.where(allowed, score, NEG_FILL)
            top = m_sc[g]
            new_top = jnp.maximum(top, jnp.max(score, axis=1, keepdims=True))
            weights = jnp.exp(score - new_top)
            if allowed is not None:
                weights = jnp.where(allowed, weights, 0.0)
            factor = jnp.exp(top - new_top)
            l_sc[g] = l_sc[g] * factor + jnp.sum(weights, axis=1, keepdims=True)
            acc_sc[g] = acc_sc[g] * factor + jnp.dot(
                weights.astype(jnp.bfloat16), values, preferred_element_type=jnp.float32
            )
            m_sc[g] = new_top

    def visit(i, carry):
        active = (used_ref[i] == 1) & (owner_ref[i] == r)

        @pl.when(active)
        def _work():
            has_new = column_ref[i] * block_size + block_size - 1 >= clen_ref[r]

            @pl.when(has_new)
            def _merge():
                keys, values = merged_block(
                    i, used_ref, owner_ref, column_ref, clen_ref, start_ref, fresh_ref, kc_ref,
                    vc_ref, rows,
                )
                nk_ref[i] = keys
                nv_ref[i] = values

            @pl.when(jnp.logical_not(has_new))
            def _cached():
                nk_ref[i] = kc_ref[i]
                nv_ref[i] = vc_ref[i]

            keys = nk_ref[i]
            values = nv_ref[i]
            seen = column_ref[i] * block_size + block_size - 1 <= clen_ref[r]

            @pl.when(seen)
            def _all():
                attend_heads(keys, values, None)

            @pl.when(jnp.logical_not(seen))
            def _masked():
                query_pos = clen_ref[r] + lax.broadcasted_iota(jnp.int32, (rows, block_size), 0)
                key_pos = column_ref[i] * block_size + lax.broadcasted_iota(
                    jnp.int32, (rows, block_size), 1
                )
                attend_heads(keys, values, key_pos <= query_pos)

        return carry

    lax.fori_loop(0, kc_ref.shape[0], visit, 0)

    lane = lax.broadcasted_iota(jnp.int32, (rows, head_dim), 1)
    stats = jnp.zeros((rows, head_dim), jnp.float32)
    for g in range(q_heads):
        top = m_sc[g]
        valid = top > NEG_FILL / 2
        ref = jnp.where(valid, top.astype(jnp.bfloat16).astype(jnp.float32), NEG_FILL)
        factor = jnp.where(valid, jnp.exp(top - ref), 0.0)
        o_ref[:, g * head_dim : (g + 1) * head_dim] = (acc_sc[g] * factor).astype(o_ref.dtype)
        stats = jnp.where(lane == g, l_sc[g] * factor, stats)
        stats = jnp.where(lane == q_heads + g, ref, stats)
    o_ref[:, q_heads * head_dim :] = stats.astype(o_ref.dtype)
    outs = [
        pltpu.make_async_copy(o_ref, o_hbm, out_sem.at[0]),
        pltpu.make_async_copy(nk_ref, nk_hbm, out_sem.at[1]),
        pltpu.make_async_copy(nv_ref, nv_hbm, out_sem.at[2]),
    ]
    for copy in outs:
        copy.start()
    for copy in outs:
        copy.wait()


def block_meta(block_table, block_ids, cached_len, block_size, fresh_len):
    used, owner, column = block_owners(block_table, block_ids)
    start = block_size + column * block_size - cached_len[owner]
    start = jnp.clip(start, 0, fresh_len - block_size - 8).astype(jnp.int32)
    return used, owner, column, cached_len, start


def attend(queries, fresh_rows, keys, values, meta, request, span, q_heads, head_dim):
    n_blocks, block_size, kv_width = keys.shape
    q_width = q_heads * head_dim
    out_width = q_width + head_dim
    block = pl.BlockSpec(keys.shape, lambda i, *_: (0, 0, 0))
    grid_spec = pltpu.PrefetchScalarGridSpec(
        num_scalar_prefetch=6,
        grid=(1,),
        in_specs=[
            pl.BlockSpec((span, q_width), lambda i, *_: (0, 0)),
            pl.BlockSpec(fresh_rows.shape, lambda i, *_: (0, 0)),
            block,
            block,
        ],
        out_specs=[pl.BlockSpec(memory_space=pl.ANY)] * 3,
        scratch_shapes=[
            pltpu.VMEM((span, out_width), jnp.bfloat16),
            pltpu.VMEM(keys.shape, keys.dtype),
            pltpu.VMEM(values.shape, values.dtype),
            pltpu.VMEM((q_heads, span, head_dim), jnp.float32),
            pltpu.VMEM((q_heads, span, head_dim), jnp.float32),
            pltpu.VMEM((q_heads, span, head_dim), jnp.float32),
            pltpu.SemaphoreType.DMA((3,)),
        ],
    )
    flops = n_blocks * span * q_heads * block_size * head_dim
    return pl.pallas_call(
        functools.partial(attention_kernel, q_heads=q_heads, head_dim=head_dim),
        grid_spec=grid_spec,
        out_shape=(
            jax.ShapeDtypeStruct((span, out_width), jnp.bfloat16),
            jax.ShapeDtypeStruct(keys.shape, keys.dtype),
            jax.ShapeDtypeStruct(values.shape, values.dtype),
        ),
        compiler_params=pltpu.CompilerParams(vmem_limit_bytes=48 * 1024 * 1024),
        cost_estimate=pl.CostEstimate(
            flops=flops,
            transcendentals=n_blocks * span * q_heads * block_size // 4,
            bytes_accessed=span * (q_width + out_width) * 2 + n_blocks * block_size * kv_width * 4,
        ),
    )(*meta, request, queries, fresh_rows, keys, values)


def combine_kernel(
    used_ref, owner_ref, got_ref, bk_hbm, bv_hbm, kc_ref, vc_ref, out_ref, nk_ref, nv_ref, bk_ref, bv_ref,
    sem, *, q_heads, head_dim
):
    fetches = []
    for b in range(nk_ref.shape[0]):
        for a, (src, dst) in enumerate(((bk_hbm, bk_ref), (bv_hbm, bv_ref))):
            fetch = pltpu.make_async_copy(src.at[owner_ref[b], b], dst.at[b], sem.at[a, b])
            fetch.start()
            fetches.append(fetch)
    ring = got_ref.shape[0]
    q_width = q_heads * head_dim
    stats = [got_ref[s, :, q_width:].astype(jnp.float32) for s in range(ring)]
    for g in range(q_heads):
        tops = [st[:, q_heads + g : q_heads + g + 1] for st in stats]
        best = tops[0]
        for t in tops[1:]:
            best = jnp.maximum(best, t)
        weighted = jnp.zeros((out_ref.shape[0], head_dim), jnp.float32)
        total = jnp.zeros((out_ref.shape[0], 1), jnp.float32)
        for s in range(ring):
            factor = jnp.exp(tops[s] - best)
            part = got_ref[s, :, g * head_dim : (g + 1) * head_dim].astype(jnp.float32)
            weighted = weighted + part * factor
            total = total + stats[s][:, g : g + 1] * factor
        out_ref[:, g * head_dim : (g + 1) * head_dim] = (weighted / total).astype(out_ref.dtype)
    for fetch in fetches:
        fetch.wait()
    for b in range(nk_ref.shape[0]):
        nk_ref[b] = jnp.where(used_ref[b] == 1, bk_ref[b], kc_ref[b])
        nv_ref[b] = jnp.where(used_ref[b] == 1, bv_ref[b], vc_ref[b])


def combine(used, owner, got, back_k, back_v, key_cache, value_cache, q_heads, head_dim):
    ring, rows, _ = got.shape
    nb_dev = back_k.shape[1]

    def whole(x):
        return pl.BlockSpec(x.shape, lambda i, *_: (0,) * x.ndim)

    grid_spec = pltpu.PrefetchScalarGridSpec(
        num_scalar_prefetch=2,
        grid=(1,),
        in_specs=[
            whole(got),
            pl.BlockSpec(memory_space=pl.ANY),
            pl.BlockSpec(memory_space=pl.ANY),
            whole(key_cache),
            whole(value_cache),
        ],
        out_specs=[
            pl.BlockSpec((rows, q_heads * head_dim), lambda i, *_: (0, 0)),
            pl.BlockSpec(back_k.shape[1:], lambda i, *_: (0, 0, 0)),
            pl.BlockSpec(back_v.shape[1:], lambda i, *_: (0, 0, 0)),
        ],
        scratch_shapes=[
            pltpu.VMEM(back_k.shape[1:], back_k.dtype),
            pltpu.VMEM(back_v.shape[1:], back_v.dtype),
            pltpu.SemaphoreType.DMA((2, nb_dev)),
        ],
    )
    return pl.pallas_call(
        functools.partial(combine_kernel, q_heads=q_heads, head_dim=head_dim),
        grid_spec=grid_spec,
        out_shape=(
            jax.ShapeDtypeStruct((rows, q_heads * head_dim), jnp.bfloat16),
            jax.ShapeDtypeStruct(back_k.shape[1:], back_k.dtype),
            jax.ShapeDtypeStruct(back_v.shape[1:], back_v.dtype),
        ),
        compiler_params=pltpu.CompilerParams(vmem_limit_bytes=32 * 1024 * 1024),
    )(used, owner, got, back_k, back_v, key_cache, value_cache)


MESH = pl.DeviceIdType.MESH


def multi_exchange_kernel(*refs, specs):
    n_total = sum(s[4] for s in specs)
    srcs, dsts = refs[:n_total], refs[n_total : 2 * n_total]
    send_sem, recv_sem, own_sem = refs[2 * n_total :]
    here = {"kv": lax.axis_index("kv"), "blk": lax.axis_index("blk")}

    def device(axis, index):
        return (index, here["blk"]) if axis == "kv" else (here["kv"], index)

    groups = []
    arr0, sem0 = 0, 0
    for axis, m, stride, gather, n_arr in specs:
        pos = lax.rem(here[axis] // stride, m)
        base = here[axis] - pos * stride
        groups.append((axis, m, stride, gather, n_arr, pos, base, arr0, sem0))
        arr0 += n_arr
        sem0 += m * n_arr

    barrier = pltpu.get_barrier_semaphore()
    for axis, m, stride, gather, n_arr, pos, base, _, _ in groups:
        for k in range(1, m):
            peer = base + lax.rem(pos + k, m) * stride
            pl.semaphore_signal(barrier, inc=1, device_id=device(axis, peer), device_id_type=MESH)
    pl.semaphore_wait(barrier, sum(s[1] - 1 for s in specs))

    def chunk(src, j, m, gather):
        if gather:
            return src
        rows = src.shape[0] // m
        return src.at[pl.ds(pl.multiple_of(j * rows, rows), rows)]

    owns, copies = [], []
    for axis, m, stride, gather, n_arr, pos, base, a0, s0 in groups:
        for a in range(a0, a0 + n_arr):
            own = pltpu.make_async_copy(chunk(srcs[a], pos, m, gather), dsts[a].at[pos], own_sem.at[a])
            own.start()
            owns.append(own)
    for axis, m, stride, gather, n_arr, pos, base, a0, s0 in groups:
        for k in range(1, m):
            peer_pos = lax.rem(pos + k, m)
            for a in range(n_arr):
                copy = pltpu.make_async_remote_copy(
                    src_ref=chunk(srcs[a0 + a], peer_pos, m, gather),
                    dst_ref=dsts[a0 + a].at[pos],
                    send_sem=send_sem.at[s0 + k * n_arr + a],
                    recv_sem=recv_sem.at[s0 + k * n_arr + a],
                    device_id=device(axis, base + peer_pos * stride),
                    device_id_type=MESH,
                )
                copy.start()
                copies.append(copy)
    for own in owns:
        own.wait()
    c = 0
    for axis, m, stride, gather, n_arr, pos, base, a0, s0 in groups:
        for k in range(1, m):
            sender_pos = lax.rem(pos + m - k, m)
            for a in range(n_arr):
                incoming = pltpu.make_async_remote_copy(
                    src_ref=chunk(srcs[a0 + a], pos, m, gather),
                    dst_ref=dsts[a0 + a].at[sender_pos],
                    send_sem=send_sem.at[s0 + k * n_arr + a],
                    recv_sem=recv_sem.at[s0 + k * n_arr + a],
                    device_id=device(axis, base + sender_pos * stride),
                    device_id_type=MESH,
                )
                copies[c].wait_send()
                incoming.wait_recv()
                c += 1


def multi_exchange(groups, collective_id):
    specs, arrays, shapes = [], [], []
    for axis, m, stride, gather, arrs in groups:
        specs.append((axis, m, stride, gather, len(arrs)))
        for x in arrs:
            rows = x.shape[0] if gather else x.shape[0] // m
            arrays.append(x)
            shapes.append(jax.ShapeDtypeStruct((m, rows) + x.shape[1:], x.dtype))
    n_sem = sum(s[1] * s[4] for s in specs)
    return pl.pallas_call(
        functools.partial(multi_exchange_kernel, specs=tuple(specs)),
        out_shape=tuple(shapes),
        in_specs=[pl.BlockSpec(memory_space=pl.ANY)] * len(arrays),
        out_specs=tuple([pl.BlockSpec(memory_space=pl.ANY)] * len(arrays)),
        scratch_shapes=[
            pltpu.SemaphoreType.DMA((n_sem,)),
            pltpu.SemaphoreType.DMA((n_sem,)),
            pltpu.SemaphoreType.DMA((len(arrays),)),
        ],
        compiler_params=pltpu.CompilerParams(collective_id=collective_id, has_side_effects=True),
    )(*arrays)


def on_device(
    hidden_in,
    norm_gain,
    w_query,
    key_weight,
    value_weight,
    b_query,
    key_bias,
    value_bias,
    key_cache,
    value_cache,
    cached_len,
    block_table,
):
    tok_dev = hidden_in.shape[0]
    n_blk = lax.axis_size("blk")
    device = lax.axis_index("blk")
    requests = cached_len.shape[0]
    tokens = tok_dev * n_blk
    span = tokens // requests
    nb_dev, block_size, kv_width = key_cache.shape
    head_dim = HEAD_SIZE
    kv_heads = kv_width // head_dim
    q_heads = w_query.shape[1] // head_dim
    group_size = q_heads // kv_heads
    gain = norm_gain.astype(jnp.float32)
    ring = span // tok_dev
    cols = n_blk // ring
    position = device % ring
    kv_n = lax.axis_size("kv")
    (got_hidden,) = multi_exchange([("kv", kv_n, 1, True, [hidden_in])], 0)
    feat = hidden_in.shape[1]
    wide_in = got_hidden.astype(jnp.float32)
    scale = lax.rsqrt(jnp.mean(wide_in * wide_in, axis=(0, 2), keepdims=True) + EPS)
    normed = (wide_in * scale * gain.reshape(kv_n, 1, feat)).astype(jnp.bfloat16)

    def project(weight):
        return lax.dot_general(
            normed,
            weight.reshape(kv_n, feat, weight.shape[1]),
            (((0, 2), (0, 1)), ((), ())),
            preferred_element_type=jnp.float32,
        )

    q_lin = project(w_query)
    key_linear = project(key_weight)
    value_linear = project(value_weight)
    my_tokens = device * tok_dev + jnp.arange(tok_dev, dtype=jnp.int32)
    my_pos = lookup(cached_len, my_tokens // span) + my_tokens % span
    fresh_queries = apply_rotary(
        (q_lin + b_query.astype(jnp.float32)[None, :]).reshape(tok_dev, q_heads, head_dim),
        my_pos,
        head_dim,
    )
    fresh_queries = fresh_queries.astype(jnp.bfloat16).reshape(tok_dev, q_heads * head_dim)
    fresh_keys = apply_rotary(
        (key_linear + key_bias.astype(jnp.float32)[None, :]).reshape(tok_dev, kv_heads, head_dim),
        my_pos,
        head_dim,
    )
    fresh_keys = fresh_keys.astype(jnp.bfloat16).reshape(tok_dev, kv_width)
    fresh_values = (value_linear + value_bias.astype(jnp.float32)[None, :]).astype(jnp.bfloat16)
    q_width = q_heads * head_dim
    packed = jnp.concatenate([fresh_queries, fresh_keys, fresh_values], axis=1)
    col_keys, col_values, ring_packed = multi_exchange(
        [("blk", cols, ring, True, [key_cache, value_cache]), ("blk", ring, 1, True, [packed])], 1
    )
    ring_packed = ring_packed.reshape(span, packed.shape[1])
    fresh_rows = jnp.pad(
        ring_packed[:, q_width:].astype(jnp.float32), ((block_size, block_size + 8), (0, 0))
    )
    holders = jnp.arange(cols, dtype=jnp.int32) * ring + position
    col_ids = (holders[:, None] * nb_dev + jnp.arange(nb_dev, dtype=jnp.int32)[None, :]).reshape(-1)
    meta = block_meta(block_table, col_ids, cached_len, block_size, fresh_rows.shape[0])
    request = (device // ring).reshape(1).astype(jnp.int32)
    parts, merged_k, merged_v = attend(
        ring_packed,
        fresh_rows,
        col_keys.reshape(cols * nb_dev, block_size, kv_width),
        col_values.reshape(cols * nb_dev, block_size, kv_width),
        meta,
        request,
        span,
        q_heads,
        head_dim,
    )
    back_k, back_v, got = multi_exchange(
        [("blk", cols, ring, False, [merged_k, merged_v]), ("blk", ring, 1, False, [parts])], 2
    )
    mine = (device // ring) * nb_dev
    used = lax.dynamic_slice_in_dim(meta[0], mine, nb_dev)
    owner = lax.dynamic_slice_in_dim(meta[1], mine, nb_dev)
    attn_out, new_k, new_v = combine(
        used,
        owner,
        got,
        back_k.reshape(cols, nb_dev, block_size, kv_width),
        back_v.reshape(cols, nb_dev, block_size, kv_width),
        key_cache,
        value_cache,
        q_heads,
        head_dim,
    )
    return (attn_out, new_k, new_v)


def solution(mesh):
    in_specs = (
        P("blk", "kv"),
        P(),
        P(None, "kv"),
        P(None, "kv"),
        P(None, "kv"),
        P("kv"),
        P("kv"),
        P("kv"),
        P("blk", None, "kv"),
        P("blk", None, "kv"),
        P(),
        P(),
    )
    out_specs = (P("blk", "kv"), P("blk", None, "kv"), P("blk", None, "kv"))
    return jax.shard_map(
        on_device, mesh=mesh, in_specs=in_specs, out_specs=out_specs, check_vma=False
    )
```

```python
import functools
import math

import jax
import jax.numpy as jnp
from jax import lax
from jax.experimental import pallas as pl
from jax.experimental.pallas import tpu as pltpu
from jax.sharding import PartitionSpec as P

HEAD_SIZE = 128


EPS = 1e-06
THETA = 1000000.0
NEG_FILL = -1e30


def apply_rotary(values, token_positions, head_dim):
    half = head_dim // 2
    rates = THETA ** (-(jnp.arange(half, dtype=jnp.float32) * 2.0) / head_dim)
    angle = token_positions.astype(jnp.float32)[:, None] * rates[None, :]
    cosine = jnp.cos(angle)[:, None, :]
    sine = jnp.sin(angle)[:, None, :]
    first = values[..., :half]
    second_half = values[..., half:]
    return jnp.concatenate(
        [first * cosine - second_half * sine, second_half * cosine + first * sine], axis=-1
    )


def lookup(table_values, slot_index):
    matches = slot_index[:, None] == jnp.arange(table_values.shape[0], dtype=jnp.int32)[None, :]
    return jnp.sum(jnp.where(matches, table_values[None, :], 0), axis=1)


def block_owners(block_table, block_ids):
    matched = block_table[None, :, :] == block_ids[:, None, None]
    row_ids = jnp.arange(block_table.shape[0], dtype=jnp.int32)[None, :, None]
    col_ids = jnp.arange(block_table.shape[1], dtype=jnp.int32)[None, None, :]
    used = jnp.any(matched, axis=(1, 2)).astype(jnp.int32)
    owner = jnp.sum(jnp.where(matched, row_ids, 0), axis=(1, 2)).astype(jnp.int32)
    column = jnp.sum(jnp.where(matched, col_ids, 0), axis=(1, 2)).astype(jnp.int32)
    return used, owner, column


def merged_block(i, used_ref, owner_ref, column_ref, clen_ref, start_ref, fresh_ref, kc_ref, vc_ref, span):
    block_size, kv_width = kc_ref.shape[1], kc_ref.shape[2]
    start = start_ref[i]
    base = pl.multiple_of((start // 8) * 8, 8)
    window = fresh_ref[pl.ds(base, block_size + 8), :].astype(jnp.bfloat16)
    pick = lax.broadcasted_iota(jnp.int32, (block_size, block_size + 8), 1) == (
        lax.broadcasted_iota(jnp.int32, (block_size, block_size + 8), 0) + (start - base)
    )
    window = jnp.dot(pick.astype(jnp.bfloat16), window, preferred_element_type=jnp.float32)
    slot_pos = column_ref[i] * block_size + lax.broadcasted_iota(
        jnp.int32, (block_size, kv_width), 0
    )
    first_new = clen_ref[owner_ref[i]]
    fresh = (used_ref[i] == 1) & (slot_pos >= first_new) & (slot_pos < first_new + span)
    keys = jnp.where(fresh, window[:, :kv_width], kc_ref[i].astype(jnp.float32))
    values = jnp.where(fresh, window[:, kv_width:], vc_ref[i].astype(jnp.float32))
    return keys.astype(kc_ref.dtype), values.astype(vc_ref.dtype)


def attention_kernel(
    used_ref, owner_ref, column_ref, clen_ref, start_ref, req_ref, q_ref, fresh_ref, kc_ref, vc_ref,
    o_hbm, nk_hbm, nv_hbm, o_ref, nk_ref, nv_ref, m_sc, l_sc, acc_sc, out_sem, *, q_heads, head_dim
):
    r = req_ref[0]
    rows = q_ref.shape[0]
    block_size = kc_ref.shape[1]
    m_sc[...] = jnp.full(m_sc.shape, NEG_FILL, jnp.float32)
    l_sc[...] = jnp.zeros(l_sc.shape, jnp.float32)
    acc_sc[...] = jnp.zeros(acc_sc.shape, jnp.float32)

    def attend_heads(keys, values, allowed):
        for g in range(q_heads):
            queries = q_ref[:, g * head_dim : (g + 1) * head_dim]
            score = lax.dot_general(
                queries, keys, (((1,), (1,)), ((), ())), preferred_element_type=jnp.float32
            ) / math.sqrt(head_dim)
            if allowed is not None:
                score = jnp.where(allowed, score, NEG_FILL)
            top = m_sc[g]
            new_top = jnp.maximum(top, jnp.max(score, axis=1, keepdims=True))
            weights = jnp.exp(score - new_top)
            if allowed is not None:
                weights = jnp.where(allowed, weights, 0.0)
            factor = jnp.exp(top - new_top)
            l_sc[g] = l_sc[g] * factor + jnp.sum(weights, axis=1, keepdims=True)
            acc_sc[g] = acc_sc[g] * factor + jnp.dot(
                weights.astype(jnp.bfloat16), values, preferred_element_type=jnp.float32
            )
            m_sc[g] = new_top

    def visit(i, carry):
        active = (used_ref[i] == 1) & (owner_ref[i] == r)

        @pl.when(active)
        def _work():
            has_new = column_ref[i] * block_size + block_size - 1 >= clen_ref[r]

            @pl.when(has_new)
            def _merge():
                keys, values = merged_block(
                    i, used_ref, owner_ref, column_ref, clen_ref, start_ref, fresh_ref, kc_ref,
                    vc_ref, rows,
                )
                nk_ref[i] = keys
                nv_ref[i] = values

            @pl.when(jnp.logical_not(has_new))
            def _cached():
                nk_ref[i] = kc_ref[i]
                nv_ref[i] = vc_ref[i]

            keys = nk_ref[i]
            values = nv_ref[i]
            seen = column_ref[i] * block_size + block_size - 1 <= clen_ref[r]

            @pl.when(seen)
            def _all():
                attend_heads(keys, values, None)

            @pl.when(jnp.logical_not(seen))
            def _masked():
                query_pos = clen_ref[r] + lax.broadcasted_iota(jnp.int32, (rows, block_size), 0)
                key_pos = column_ref[i] * block_size + lax.broadcasted_iota(
                    jnp.int32, (rows, block_size), 1
                )
                attend_heads(keys, values, key_pos <= query_pos)

        return carry

    lax.fori_loop(0, kc_ref.shape[0], visit, 0)

    lane = lax.broadcasted_iota(jnp.int32, (rows, head_dim), 1)
    stats = jnp.zeros((rows, head_dim), jnp.float32)
    for g in range(q_heads):
        top = m_sc[g]
        valid = top > NEG_FILL / 2
        ref = jnp.where(valid, top.astype(jnp.bfloat16).astype(jnp.float32), NEG_FILL)
        factor = jnp.where(valid, jnp.exp(top - ref), 0.0)
        o_ref[:, g * head_dim : (g + 1) * head_dim] = (acc_sc[g] * factor).astype(o_ref.dtype)
        stats = jnp.where(lane == g, l_sc[g] * factor, stats)
        stats = jnp.where(lane == q_heads + g, ref, stats)
    o_ref[:, q_heads * head_dim :] = stats.astype(o_ref.dtype)
    outs = [
        pltpu.make_async_copy(o_ref, o_hbm, out_sem.at[0]),
        pltpu.make_async_copy(nk_ref, nk_hbm, out_sem.at[1]),
        pltpu.make_async_copy(nv_ref, nv_hbm, out_sem.at[2]),
    ]
    for copy in outs:
        copy.start()
    for copy in outs:
        copy.wait()


def block_meta(block_table, block_ids, cached_len, block_size, fresh_len):
    used, owner, column = block_owners(block_table, block_ids)
    start = block_size + column * block_size - cached_len[owner]
    start = jnp.clip(start, 0, fresh_len - block_size - 8).astype(jnp.int32)
    return used, owner, column, cached_len, start


def attend(queries, fresh_rows, keys, values, meta, request, span, q_heads, head_dim):
    n_blocks, block_size, kv_width = keys.shape
    q_width = q_heads * head_dim
    out_width = q_width + head_dim
    block = pl.BlockSpec(keys.shape, lambda i, *_: (0, 0, 0))
    grid_spec = pltpu.PrefetchScalarGridSpec(
        num_scalar_prefetch=6,
        grid=(1,),
        in_specs=[
            pl.BlockSpec((span, q_width), lambda i, *_: (0, 0)),
            pl.BlockSpec(fresh_rows.shape, lambda i, *_: (0, 0)),
            block,
            block,
        ],
        out_specs=[pl.BlockSpec(memory_space=pl.ANY)] * 3,
        scratch_shapes=[
            pltpu.VMEM((span, out_width), jnp.bfloat16),
            pltpu.VMEM(keys.shape, keys.dtype),
            pltpu.VMEM(values.shape, values.dtype),
            pltpu.VMEM((q_heads, span, head_dim), jnp.float32),
            pltpu.VMEM((q_heads, span, head_dim), jnp.float32),
            pltpu.VMEM((q_heads, span, head_dim), jnp.float32),
            pltpu.SemaphoreType.DMA((3,)),
        ],
    )
    flops = n_blocks * span * q_heads * block_size * head_dim
    return pl.pallas_call(
        functools.partial(attention_kernel, q_heads=q_heads, head_dim=head_dim),
        grid_spec=grid_spec,
        out_shape=(
            jax.ShapeDtypeStruct((span, out_width), jnp.bfloat16),
            jax.ShapeDtypeStruct(keys.shape, keys.dtype),
            jax.ShapeDtypeStruct(values.shape, values.dtype),
        ),
        compiler_params=pltpu.CompilerParams(vmem_limit_bytes=48 * 1024 * 1024),
        cost_estimate=pl.CostEstimate(
            flops=flops,
            transcendentals=n_blocks * span * q_heads * block_size // 4,
            bytes_accessed=span * (q_width + out_width) * 2 + n_blocks * block_size * kv_width * 4,
        ),
    )(*meta, request, queries, fresh_rows, keys, values)


def combine_kernel(
    used_ref, owner_ref, got_ref, bk_hbm, bv_hbm, kc_ref, vc_ref, out_ref, nk_ref, nv_ref, bk_ref, bv_ref,
    sem, *, q_heads, head_dim
):
    fetches = []
    for b in range(nk_ref.shape[0]):
        for a, (src, dst) in enumerate(((bk_hbm, bk_ref), (bv_hbm, bv_ref))):
            fetch = pltpu.make_async_copy(src.at[owner_ref[b], b], dst.at[b], sem.at[a, b])
            fetch.start()
            fetches.append(fetch)
    ring = got_ref.shape[0]
    q_width = q_heads * head_dim
    stats = [got_ref[s, :, q_width:].astype(jnp.float32) for s in range(ring)]
    for g in range(q_heads):
        tops = [st[:, q_heads + g : q_heads + g + 1] for st in stats]
        best = tops[0]
        for t in tops[1:]:
            best = jnp.maximum(best, t)
        weighted = jnp.zeros((out_ref.shape[0], head_dim), jnp.float32)
        total = jnp.zeros((out_ref.shape[0], 1), jnp.float32)
        for s in range(ring):
            factor = jnp.exp(tops[s] - best)
            part = got_ref[s, :, g * head_dim : (g + 1) * head_dim].astype(jnp.float32)
            weighted = weighted + part * factor
            total = total + stats[s][:, g : g + 1] * factor
        out_ref[:, g * head_dim : (g + 1) * head_dim] = (weighted / total).astype(out_ref.dtype)
    for fetch in fetches:
        fetch.wait()
    for b in range(nk_ref.shape[0]):
        nk_ref[b] = jnp.where(used_ref[b] == 1, bk_ref[b], kc_ref[b])
        nv_ref[b] = jnp.where(used_ref[b] == 1, bv_ref[b], vc_ref[b])


def combine(used, owner, got, back_k, back_v, key_cache, value_cache, q_heads, head_dim):
    ring, rows, _ = got.shape
    nb_dev = back_k.shape[1]

    def whole(x):
        return pl.BlockSpec(x.shape, lambda i, *_: (0,) * x.ndim)

    grid_spec = pltpu.PrefetchScalarGridSpec(
        num_scalar_prefetch=2,
        grid=(1,),
        in_specs=[
            whole(got),
            pl.BlockSpec(memory_space=pl.ANY),
            pl.BlockSpec(memory_space=pl.ANY),
            whole(key_cache),
            whole(value_cache),
        ],
        out_specs=[
            pl.BlockSpec((rows, q_heads * head_dim), lambda i, *_: (0, 0)),
            pl.BlockSpec(back_k.shape[1:], lambda i, *_: (0, 0, 0)),
            pl.BlockSpec(back_v.shape[1:], lambda i, *_: (0, 0, 0)),
        ],
        scratch_shapes=[
            pltpu.VMEM(back_k.shape[1:], back_k.dtype),
            pltpu.VMEM(back_v.shape[1:], back_v.dtype),
            pltpu.SemaphoreType.DMA((2, nb_dev)),
        ],
    )
    return pl.pallas_call(
        functools.partial(combine_kernel, q_heads=q_heads, head_dim=head_dim),
        grid_spec=grid_spec,
        out_shape=(
            jax.ShapeDtypeStruct((rows, q_heads * head_dim), jnp.bfloat16),
            jax.ShapeDtypeStruct(back_k.shape[1:], back_k.dtype),
            jax.ShapeDtypeStruct(back_v.shape[1:], back_v.dtype),
        ),
        compiler_params=pltpu.CompilerParams(vmem_limit_bytes=32 * 1024 * 1024),
    )(used, owner, got, back_k, back_v, key_cache, value_cache)


MESH = pl.DeviceIdType.MESH


def multi_exchange_kernel(*refs, specs):
    n_total = sum(s[4] for s in specs)
    srcs, dsts = refs[:n_total], refs[n_total : 2 * n_total]
    send_sem, recv_sem, own_sem = refs[2 * n_total :]
    here = {"kv": lax.axis_index("kv"), "blk": lax.axis_index("blk")}

    def device(axis, index):
        return (index, here["blk"]) if axis == "kv" else (here["kv"], index)

    groups = []
    arr0, sem0 = 0, 0
    for axis, m, stride, gather, n_arr in specs:
        pos = lax.rem(here[axis] // stride, m)
        base = here[axis] - pos * stride
        groups.append((axis, m, stride, gather, n_arr, pos, base, arr0, sem0))
        arr0 += n_arr
        sem0 += m * n_arr

    barrier = pltpu.get_barrier_semaphore()
    for axis, m, stride, gather, n_arr, pos, base, _, _ in groups:
        for k in range(1, m):
            peer = base + lax.rem(pos + k, m) * stride
            pl.semaphore_signal(barrier, inc=1, device_id=device(axis, peer), device_id_type=MESH)
    pl.semaphore_wait(barrier, sum(s[1] - 1 for s in specs))

    def chunk(src, j, m, gather):
        if gather:
            return src
        rows = src.shape[0] // m
        return src.at[pl.ds(pl.multiple_of(j * rows, rows), rows)]

    owns, copies = [], []
    for axis, m, stride, gather, n_arr, pos, base, a0, s0 in groups:
        for a in range(a0, a0 + n_arr):
            own = pltpu.make_async_copy(chunk(srcs[a], pos, m, gather), dsts[a].at[pos], own_sem.at[a])
            own.start()
            owns.append(own)
    started = {}
    for k in range(1, max(g[1] for g in groups)):
        for gi, (axis, m, stride, gather, n_arr, pos, base, a0, s0) in enumerate(groups):
            if k >= m:
                continue
            peer_pos = lax.rem(pos + k, m)
            for a in range(n_arr):
                copy = pltpu.make_async_remote_copy(
                    src_ref=chunk(srcs[a0 + a], peer_pos, m, gather),
                    dst_ref=dsts[a0 + a].at[pos],
                    send_sem=send_sem.at[s0 + k * n_arr + a],
                    recv_sem=recv_sem.at[s0 + k * n_arr + a],
                    device_id=device(axis, base + peer_pos * stride),
                    device_id_type=MESH,
                )
                copy.start()
                started[(gi, k, a)] = copy
    for gi, (axis, m, stride, gather, n_arr, pos, base, a0, s0) in enumerate(groups):
        for k in range(1, m):
            for a in range(n_arr):
                copies.append(started[(gi, k, a)])
    for own in owns:
        own.wait()
    c = 0
    for axis, m, stride, gather, n_arr, pos, base, a0, s0 in groups:
        for k in range(1, m):
            sender_pos = lax.rem(pos + m - k, m)
            for a in range(n_arr):
                incoming = pltpu.make_async_remote_copy(
                    src_ref=chunk(srcs[a0 + a], pos, m, gather),
                    dst_ref=dsts[a0 + a].at[sender_pos],
                    send_sem=send_sem.at[s0 + k * n_arr + a],
                    recv_sem=recv_sem.at[s0 + k * n_arr + a],
                    device_id=device(axis, base + sender_pos * stride),
                    device_id_type=MESH,
                )
                copies[c].wait_send()
                incoming.wait_recv()
                c += 1


def multi_exchange(groups, collective_id):
    specs, arrays, shapes = [], [], []
    for axis, m, stride, gather, arrs in groups:
        specs.append((axis, m, stride, gather, len(arrs)))
        for x in arrs:
            rows = x.shape[0] if gather else x.shape[0] // m
            arrays.append(x)
            shapes.append(jax.ShapeDtypeStruct((m, rows) + x.shape[1:], x.dtype))
    n_sem = sum(s[1] * s[4] for s in specs)
    return pl.pallas_call(
        functools.partial(multi_exchange_kernel, specs=tuple(specs)),
        out_shape=tuple(shapes),
        in_specs=[pl.BlockSpec(memory_space=pl.ANY)] * len(arrays),
        out_specs=tuple([pl.BlockSpec(memory_space=pl.ANY)] * len(arrays)),
        scratch_shapes=[
            pltpu.SemaphoreType.DMA((n_sem,)),
            pltpu.SemaphoreType.DMA((n_sem,)),
            pltpu.SemaphoreType.DMA((len(arrays),)),
        ],
        compiler_params=pltpu.CompilerParams(collective_id=collective_id, has_side_effects=True),
    )(*arrays)


def on_device(
    hidden_in,
    norm_gain,
    w_query,
    key_weight,
    value_weight,
    b_query,
    key_bias,
    value_bias,
    key_cache,
    value_cache,
    cached_len,
    block_table,
):
    tok_dev = hidden_in.shape[0]
    n_blk = lax.axis_size("blk")
    device = lax.axis_index("blk")
    requests = cached_len.shape[0]
    tokens = tok_dev * n_blk
    span = tokens // requests
    nb_dev, block_size, kv_width = key_cache.shape
    head_dim = HEAD_SIZE
    kv_heads = kv_width // head_dim
    q_heads = w_query.shape[1] // head_dim
    group_size = q_heads // kv_heads
    gain = norm_gain.astype(jnp.float32)
    ring = span // tok_dev
    cols = n_blk // ring
    position = device % ring
    kv_n = lax.axis_size("kv")
    (got_hidden,) = multi_exchange([("kv", kv_n, 1, True, [hidden_in])], 0)
    feat = hidden_in.shape[1]
    wide_in = got_hidden.astype(jnp.float32)
    scale = lax.rsqrt(jnp.mean(wide_in * wide_in, axis=(0, 2), keepdims=True) + EPS)
    normed = (wide_in * scale * gain.reshape(kv_n, 1, feat)).astype(jnp.bfloat16)

    def project(weight):
        return lax.dot_general(
            normed,
            weight.reshape(kv_n, feat, weight.shape[1]),
            (((0, 2), (0, 1)), ((), ())),
            preferred_element_type=jnp.float32,
        )

    q_lin = project(w_query)
    key_linear = project(key_weight)
    value_linear = project(value_weight)
    my_tokens = device * tok_dev + jnp.arange(tok_dev, dtype=jnp.int32)
    my_pos = lookup(cached_len, my_tokens // span) + my_tokens % span
    fresh_queries = apply_rotary(
        (q_lin + b_query.astype(jnp.float32)[None, :]).reshape(tok_dev, q_heads, head_dim),
        my_pos,
        head_dim,
    )
    fresh_queries = fresh_queries.astype(jnp.bfloat16).reshape(tok_dev, q_heads * head_dim)
    fresh_keys = apply_rotary(
        (key_linear + key_bias.astype(jnp.float32)[None, :]).reshape(tok_dev, kv_heads, head_dim),
        my_pos,
        head_dim,
    )
    fresh_keys = fresh_keys.astype(jnp.bfloat16).reshape(tok_dev, kv_width)
    fresh_values = (value_linear + value_bias.astype(jnp.float32)[None, :]).astype(jnp.bfloat16)
    q_width = q_heads * head_dim
    packed = jnp.concatenate([fresh_queries, fresh_keys, fresh_values], axis=1)
    ring_packed, col_keys, col_values = multi_exchange(
        [("blk", ring, 1, True, [packed]), ("blk", cols, ring, True, [key_cache, value_cache])], 1
    )
    ring_packed = ring_packed.reshape(span, packed.shape[1])
    fresh_rows = jnp.pad(
        ring_packed[:, q_width:].astype(jnp.float32), ((block_size, block_size + 8), (0, 0))
    )
    holders = jnp.arange(cols, dtype=jnp.int32) * ring + position
    col_ids = (holders[:, None] * nb_dev + jnp.arange(nb_dev, dtype=jnp.int32)[None, :]).reshape(-1)
    meta = block_meta(block_table, col_ids, cached_len, block_size, fresh_rows.shape[0])
    request = (device // ring).reshape(1).astype(jnp.int32)
    parts, merged_k, merged_v = attend(
        ring_packed,
        fresh_rows,
        col_keys.reshape(cols * nb_dev, block_size, kv_width),
        col_values.reshape(cols * nb_dev, block_size, kv_width),
        meta,
        request,
        span,
        q_heads,
        head_dim,
    )
    got, back_k, back_v = multi_exchange(
        [("blk", ring, 1, False, [parts]), ("blk", cols, ring, False, [merged_k, merged_v])], 2
    )
    mine = (device // ring) * nb_dev
    used = lax.dynamic_slice_in_dim(meta[0], mine, nb_dev)
    owner = lax.dynamic_slice_in_dim(meta[1], mine, nb_dev)
    attn_out, new_k, new_v = combine(
        used,
        owner,
        got,
        back_k.reshape(cols, nb_dev, block_size, kv_width),
        back_v.reshape(cols, nb_dev, block_size, kv_width),
        key_cache,
        value_cache,
        q_heads,
        head_dim,
    )
    return (attn_out, new_k, new_v)


def solution(mesh):
    in_specs = (
        P("blk", "kv"),
        P(),
        P(None, "kv"),
        P(None, "kv"),
        P(None, "kv"),
        P("kv"),
        P("kv"),
        P("kv"),
        P("blk", None, "kv"),
        P("blk", None, "kv"),
        P(),
        P(),
    )
    out_specs = (P("blk", "kv"), P("blk", None, "kv"), P("blk", None, "kv"))
    return jax.shard_map(
        on_device, mesh=mesh, in_specs=in_specs, out_specs=out_specs, check_vma=False
    )
```
